32 devices in a mesh: grp: 4 (over y, x), seq: 8 (over z, core).
Axes of the slice: x: 2, y: 2, z: 4, core: 2. Of those that a mesh axis runs over, the one named last changes fastest.
Arguments:
- audio: bfloat16 [4, 2048, 1280], P('grp', 'seq'), may hold values from -6 to 6, as said below
- block_ids: int32 [4, 2048], P('grp', 'seq'), may hold values from 0 to 39, never falling along the last dimension, each value on 1 to 100 neighbouring positions
- norm_gain: float32 [1280], replicated, may hold values from 0.1 to 1.9
- qkv_weight: bfloat16 [1280, 3840], P(None, 'grp'), may hold values from -8 to 8
- out_weight: bfloat16 [1280, 1280], P(None, 'grp'), may hold values from -0.15625 to 0.15625
- adapter_weight: bfloat16 [2560, 2048], P(None, 'grp'), may hold values from -0.125 to 0.125
- moe_gain: float32 [2048], replicated, may hold values from 0.1 to 1.9
- gate_weight: bfloat16 [8, 2048, 768], P('seq'), may hold values from -0.125 to 0.125
- up_weight: bfloat16 [8, 2048, 768], P('seq'), may hold values from -0.125 to 0.125
- down_weight: bfloat16 [8, 768, 2048], P('seq'), may hold values from -0.21875 to 0.21875
- routes: int32 [4, 1024, 4], P('grp', 'seq'), may hold values from 0 to 7, all different within a row; in each aligned block of 128 rows (0 to 127, 128 to 255, ..., all dimensions but the last counted through in order) at most 96 rows name the same one
- route_weights: float32 [4, 1024, 4], P('grp', 'seq'), may hold values from 0.05 to 1
Outputs:
- thinker_out: bfloat16 [4, 1024, 2048], P('grp', 'seq')
The draws below stay inside these ranges and needn't reach their ends.
Inputs may be any that keep to these rules, and one draw needn't show every extreme that they name: `audio`: in the hidden draw, frames come in nearly equal adjacent pairs. `block_ids`: block numbers never fall along a slab's frames; each block holds 1 to 100 frames, and some block exactly 100. `routes`: each token names 4 different experts; among the tokens of one device no expert is named by more than 96 of them, and in every draw some expert is named by exactly 96.
All inputs are finite; a program needn't handle non-finite values.
Results may differ from the reference program's by a relative error of at most 0.011.
Values may be sent and summed in bfloat16 or wider, within the bound.
A program may use at most 128 MiB of HBM per device.

```python
import math
import jax
import jax.numpy as jnp
import numpy as np
from jax import lax

D = 1280
HEADS = 20
HEAD = 64
DM = 2048
FF = 768
TOK_DEV = 256
WIN = 100
TOPK = 4
EXPERTS = 8
CAP = 96
SLABS = 4
FRAMES = 2048
TOKENS = 1024
N_SEQ = 8


def draw_audio(key, part):
    base = jax.random.normal(key, (SLABS, FRAMES, D), jnp.float32)
    return jnp.clip(base, -6.0, 6.0).astype(jnp.bfloat16)


def draw_qkv_weight(key, part):
    weight = jax.random.normal(key, (D, 3 * D), jnp.float32) * D ** (-0.5)
    return jnp.clip(weight, -8.0, 8.0).astype(jnp.bfloat16)


def block_levels(stream_key, shape, cuts, low, top_value):
    def one(dim, parts):
        steps = jax.random.uniform(jax.random.fold_in(jax.random.fold_in(stream_key, 6), dim), (parts,), jnp.float32, low / len(cuts), top_value / len(cuts))
        return jnp.repeat(jnp.exp(steps), shape[dim] // parts).reshape((-1,) + (1,) * (len(shape) - dim - 1))

    loudness = one(*cuts[0])
    for cut in cuts[1:]:
        loudness = loudness * one(*cut)
    return loudness


def split_up(count, total, reach, lean):
    portions = [(1 << 20) // math.isqrt(grade ** lean) + 1 for grade in range(2, count + 1)]
    surplus, given = total - reach - (count - 1), [1] * (count - 1)
    while surplus > 0:
        movable = [i for i in range(count - 1) if given[i] < reach]
        pool, budget = sum([portions[i] for i in movable]), surplus
        for i in movable:
            extra = min(reach - given[i], max(1, budget * portions[i] // pool), surplus)
            given[i] = given[i] + extra
            surplus = surplus - extra
    return np.array([reach] + given)


def ragged_sizes(stream_key, amount, total, reach, lean):
    if amount == 2:
        one = jax.random.randint(stream_key, (), max(1, total - reach), min(reach, total - 1) + 1)
        return jnp.stack([one, total - one])
    lengths = jnp.asarray(split_up(amount, total, reach, lean), jnp.int32)
    twos = (amount - 1) // 2
    source_of, sink = lengths[1:1 + 2 * twos:2], lengths[2:2 + 2 * twos:2]
    room = jnp.minimum(source_of - 1, reach - sink)
    passed = jax.random.randint(jax.random.fold_in(stream_key, 1), (twos,), 0, 1 << 20) % (room + 1)
    lengths = lengths.at[1:1 + 2 * twos:2].set(source_of - passed).at[2:2 + 2 * twos:2].set(sink + passed)
    return lengths[jax.random.permutation(jax.random.fold_in(stream_key, 2), amount)]


def deal_out(key, own, number, rows, amount, top, limit, skew):
    ranking = jax.random.permutation(key, amount)
    heavy_load, common = load_shares(amount, rows * top, limit, skew, True), load_shares(amount, rows * top, limit, skew, False)
    places = jnp.arange(amount)

    def named(lengths, rotation):
        used = int((lengths > 0).sum())
        fixed = max(1, used // 4)
        moved = fixed + (places - fixed + rotation * (used - fixed)) % max(1, amount - fixed)
        return jnp.zeros((amount,), jnp.int32).at[ranking[jnp.where(places < fixed, places, moved)]].set(jnp.asarray(lengths, jnp.int32))

    lengths = jnp.where(number % 4 == 0, named(heavy_load, number // 4), named(common, number - number // 4 - 1))
    mixed = jax.random.permutation(jax.random.fold_in(own, 3), amount)
    source_of, taker = mixed[0:amount // 2 * 2:2], mixed[1:amount // 2 * 2:2]
    room = jnp.minimum(lengths[source_of] - 1, limit - lengths[taker]) // 2
    room = jnp.where((source_of == ranking[0]) | (taker == ranking[0]) | (lengths[taker] == 0), 0, jnp.maximum(room, 0))
    moved = jax.random.randint(jax.random.fold_in(own, 4), (amount // 2,), 0, 1 << 20) % (room + 1)
    lengths = lengths.at[source_of].add(-moved).at[taker].add(moved)
    members = jnp.searchsorted(jnp.cumsum(lengths), jnp.arange(rows * top), side="right").astype(jnp.int32)
    grid = members.reshape(top, rows).T
    grid = grid[jax.random.permutation(jax.random.fold_in(own, 1), rows)]
    rotation = jax.random.randint(jax.random.fold_in(own, 2), (rows, 1), 0, top)
    return jnp.take_along_axis(grid, (jnp.arange(top)[None, :] + rotation) % top, axis=1)


def load_shares(amount, total, limit, lean, full):
    portions = [(1 << 20) // math.isqrt(rank ** lean) + 1 for rank in range(1, amount + 1)]
    largest = limit if full else min(limit, max(-(-total // amount), total * portions[0] // sum(portions)))
    least = 1 if total - largest >= amount - 1 else 0
    holding, surplus = [largest] + [least] * (amount - 1), total - largest - least * (amount - 1)
    while surplus > 0:
        movable = [i for i in range(1, amount) if holding[i] < largest] or [i for i in range(1, amount) if holding[i] < limit]
        pool, remaining = sum([portions[i] for i in movable]), surplus
        for i in movable:
            more = min(limit - holding[i], max(1, remaining * portions[i] // pool), surplus)
            holding[i] = holding[i] + more
            surplus = surplus - more
    return np.array(holding)


def bell_draw(own_key, extent, width, bound, cuts=(), kind=jnp.bfloat16):
    level = block_levels(own_key, extent, cuts, -0.22, 0.18) if cuts else 1.0
    drawn = jax.random.normal(own_key, extent, jnp.float32) * width * level
    return jnp.minimum(jnp.maximum(drawn, -bound), bound).astype(kind)


def setup_inputs(seed: int = 0) -> dict:
    seeds = jax.random.split(jax.random.key(seed), 13)
    audio = draw_audio(jax.random.fold_in(seeds[12], 71), 0)
    block_ids = jax.vmap(lambda own: jnp.searchsorted(jnp.cumsum(ragged_sizes(own, 2 * FRAMES // WIN, FRAMES, WIN, 1)), jnp.arange(FRAMES), side="right"))(jax.random.split(seeds[1], SLABS)).reshape((SLABS, FRAMES)).astype(jnp.int32)
    norm_gain = jnp.clip(1.0 + 0.18 * jax.random.normal(seeds[2], (D,), jnp.float32), 0.1, 1.9)
    qkv_weight = draw_qkv_weight(jax.random.fold_in(seeds[12], 71), 0)
    out_weight = bell_draw(seeds[4], (D, D), D ** -0.5, 0.15625, ((1, 4),))
    adapter_weight = bell_draw(seeds[5], (2 * D, DM), (2 * D) ** -0.5, 0.125, ((1, 4),))
    moe_gain = jnp.clip(1.0 + 0.18 * jax.random.normal(seeds[6], (DM,), jnp.float32), 0.1, 1.9)
    gate_weight = bell_draw(seeds[7], (EXPERTS, DM, FF), DM ** -0.5, 0.125, ((0, 8),))
    up_weight = bell_draw(seeds[8], (EXPERTS, DM, FF), DM ** -0.5, 0.125, ((0, 8),))
    down_weight = bell_draw(seeds[9], (EXPERTS, FF, DM), FF ** -0.5, 0.21875, ((0, 8),))
    routes_keys = jax.random.split(jax.random.fold_in(seeds[10], 1), SLABS * TOKENS // (TOK_DEV // 2))
    routes_turns = jax.random.permutation(jax.random.fold_in(seeds[10], 3), SLABS * TOKENS // (TOK_DEV // 2))
    routes = jax.vmap(lambda own, number: deal_out(jax.random.fold_in(seeds[10], 2), own, number, TOK_DEV // 2, EXPERTS, TOPK, CAP, 2))(routes_keys, routes_turns).reshape((SLABS, TOKENS, TOPK))
    route_weights = jnp.clip(jnp.exp(math.log(1.0) - 2.9957323 * jax.random.uniform(seeds[11], (SLABS, TOKENS, TOPK), jnp.float32) ** block_levels(seeds[11], (SLABS, TOKENS, TOPK), ((0, 4), (1, 8)), -0.2, 0.2)), 0.05, 1.0)
    return dict(audio=audio, block_ids=block_ids, norm_gain=norm_gain, qkv_weight=qkv_weight, out_weight=out_weight, adapter_weight=adapter_weight, moe_gain=moe_gain, gate_weight=gate_weight, up_weight=up_weight, down_weight=down_weight, routes=routes, route_weights=route_weights)


LN_EPSILON = 1e-05
RMS_EPSILON = 1e-06
MASKED = -1e+30

def layer_norm(signal, gain):
    widened = signal.astype(jnp.float32)
    average = lax.optimization_barrier(jnp.mean(widened, axis=-1, keepdims=True))
    centred = widened - average
    variance = lax.optimization_barrier(jnp.mean(centred * centred, axis=-1, keepdims=True))
    return centred * lax.rsqrt(variance + LN_EPSILON) * gain

def rms_norm(signal, gain):
    widened = signal.astype(jnp.float32)
    squares = lax.optimization_barrier(jnp.mean(widened * widened, axis=-1, keepdims=True))
    return widened * lax.rsqrt(squares + RMS_EPSILON) * gain

def slab_attention(slab_qkv, slab_ids):
    margin = WIN - 1
    query_all = slab_qkv[:, :D]
    padded = jnp.pad(slab_qkv[:, D:], ((margin, margin), (0, 0)))
    padded_ids = jnp.pad(slab_ids, (margin, margin), constant_values=-1)

    def one_block(block_number):
        first_row = (block_number * TOK_DEV).astype(jnp.int32)
        query_rows = lax.dynamic_slice_in_dim(query_all, first_row, TOK_DEV, 0).reshape(TOK_DEV, HEADS, HEAD)
        query_ids = lax.dynamic_slice_in_dim(slab_ids, first_row, TOK_DEV, 0)
        window = lax.dynamic_slice_in_dim(padded, first_row, TOK_DEV + 2 * margin, 0)
        window_ids = lax.dynamic_slice_in_dim(padded_ids, first_row, TOK_DEV + 2 * margin, 0)
        key_rows = window[:, :D].reshape(-1, HEADS, HEAD).astype(jnp.float32)
        value_rows = window[:, D:].reshape(-1, HEADS, HEAD).astype(jnp.float32)
        scores = jnp.einsum('qhd,khd->hqk', query_rows.astype(jnp.float32), key_rows) * HEAD ** (-0.5)
        allowed = query_ids[:, None] == window_ids[None, :]
        scores = jnp.where(allowed[None], scores, MASKED)
        highest = lax.optimization_barrier(jnp.max(scores, axis=-1, keepdims=True))
        exponent = jnp.exp(scores - highest)
        probability = (exponent / lax.optimization_barrier(jnp.sum(exponent, axis=-1, keepdims=True))).astype(jnp.bfloat16)
        attended = jnp.einsum('hqk,khd->qhd', probability.astype(jnp.float32), value_rows)
        return attended.astype(jnp.bfloat16).reshape(TOK_DEV, D)
    blocks = lax.map(one_block, jnp.arange(N_SEQ, dtype=jnp.int32))
    return blocks.reshape(FRAMES, D)

def reference(audio, block_ids, norm_gain, qkv_weight, out_weight, adapter_weight, moe_gain, gate_weight, up_weight, down_weight, routes, route_weights):
    flat_audio = audio.reshape(SLABS * FRAMES, D)
    normed = layer_norm(flat_audio, norm_gain).astype(jnp.bfloat16)
    qkv_all = jnp.dot(normed, qkv_weight, preferred_element_type=jnp.float32).astype(jnp.bfloat16)
    qkv_all = qkv_all.reshape(SLABS, FRAMES, 3 * D)
    attended = lax.map(lambda pair: slab_attention(pair[0], pair[1]), (qkv_all, block_ids))
    attended = attended.reshape(SLABS * FRAMES, D)
    projected = jnp.dot(attended, out_weight, preferred_element_type=jnp.float32)
    encoded = (flat_audio.astype(jnp.float32) + projected).astype(jnp.bfloat16)
    pooled = encoded.reshape(SLABS * TOKENS, 2 * D)
    thinker_in = jnp.dot(pooled, adapter_weight, preferred_element_type=jnp.float32).astype(jnp.bfloat16)
    expert_in = rms_norm(thinker_in, moe_gain).astype(jnp.bfloat16)
    block_count = SLABS * N_SEQ
    per_block = TOKENS // N_SEQ
    flat_routes = routes.reshape(block_count, per_block * TOPK).astype(jnp.int32)
    expert_ids = jnp.arange(EXPERTS, dtype=jnp.int32)
    membership = (flat_routes[:, :, None] == expert_ids[None, None, :]).astype(jnp.int32)
    positions = lax.optimization_barrier(jnp.sum((jnp.cumsum(membership, axis=1) - 1) * membership, axis=2))
    slot_index = flat_routes * CAP + positions
    block_index = jnp.arange(block_count, dtype=jnp.int32)[:, None]
    token_index = block_index * per_block + jnp.arange(per_block * TOPK, dtype=jnp.int32)[None, :] // TOPK
    shares = route_weights / lax.optimization_barrier(jnp.sum(route_weights, axis=-1, keepdims=True))
    shares = shares.reshape(block_count, per_block * TOPK)
    token_table = jnp.zeros((block_count, EXPERTS * CAP), jnp.int32).at[block_index, slot_index].set(token_index)
    share_table = jnp.zeros((block_count, EXPERTS * CAP), jnp.float32).at[block_index, slot_index].set(shares)
    token_table = token_table.reshape(block_count, EXPERTS, CAP).transpose(1, 0, 2).reshape(EXPERTS, block_count * CAP)
    share_table = share_table.reshape(block_count, EXPERTS, CAP).transpose(1, 0, 2).reshape(EXPERTS, block_count * CAP)

    def one_expert(running, inputs):
        token_rows, row_shares, gate_matrix, up_matrix, down_matrix = inputs
        routed_rows = expert_in[token_rows]
        gate_act = jnp.dot(routed_rows, gate_matrix, preferred_element_type=jnp.float32)
        up_act = jnp.dot(routed_rows, up_matrix, preferred_element_type=jnp.float32)
        hidden = (jax.nn.silu(gate_act) * up_act).astype(jnp.bfloat16)
        produced = jnp.dot(hidden, down_matrix, preferred_element_type=jnp.float32).astype(jnp.bfloat16)
        running = running.at[token_rows].add(row_shares[:, None] * produced.astype(jnp.float32))
        return (running, None)
    start_value = thinker_in.astype(jnp.float32)
    running, unused = lax.scan(one_expert, start_value, (token_table, share_table, gate_weight, up_weight, down_weight))
    return running.astype(jnp.bfloat16).reshape(SLABS, TOKENS, DM)
```

```python
import functools

import jax
import jax.numpy as jnp
from jax import lax
from jax.experimental import pallas as pl
from jax.experimental.pallas import tpu as pltpu
from jax.sharding import PartitionSpec as P

HEAD = 64
EDGE = 128
LN_EPSILON = 1e-05
RMS_EPSILON = 1e-06
MASKED = -1e30
VMEM_LIMIT = 66_000_000
MESH = pl.DeviceIdType.MESH
BF16 = jnp.bfloat16
F32 = jnp.float32
NT = (((1,), (1,)), ((), ()))


def greet(g, s, groups, seqs, across):
    barrier = pltpu.get_barrier_semaphore()
    if across:
        for k in range(1, groups):
            pl.semaphore_signal(
                barrier, inc=1, device_id={"grp": lax.rem(g + k, groups), "seq": s}, device_id_type=MESH
            )
    for k in range(1, seqs):
        pl.semaphore_signal(
            barrier, inc=1, device_id={"grp": g, "seq": lax.rem(s + k, seqs)}, device_id_type=MESH
        )
    pl.semaphore_wait(barrier, seqs - 1 + (groups - 1 if across else 0))


class Gather:
    def __init__(self, g, s, groups, seqs, shard, whole, rows, by_lanes, deep, own_sem, send_sem, recv_sem):
        self.g, self.s, self.groups = g, s, groups
        self.shard, self.whole, self.by_lanes = shard, whole, by_lanes
        self.own_sem, self.send_sem, self.recv_sem = own_sem, send_sem, recv_sem
        self.first, self.rows = rows
        self.routed = groups == 4
        self.deep = deep and self.routed and seqs % 4 == 0
        core, plane = lax.rem(s, 2), lax.rem(s // 2, 2)
        self.other = s + 1 - 2 * core
        self.paired = s + 2 - 4 * plane
        if self.deep:
            self.size = self.rows // 4
            self.start = self.first + (plane * 2 + core) * self.size
            self.paired_start = self.first + ((1 - plane) * 2 + core) * self.size
        else:
            self.size = self.rows // 2
            self.start = self.first + core * self.size
        self.cut = self.size // 2
        self.copies = {}

    def part(self, group, first, count):
        if self.by_lanes:
            columns = self.shard.shape[1]
            start = pl.multiple_of(group * columns, 128)
            return self.whole.at[pl.ds(pl.multiple_of(first, 16), count), pl.ds(start, columns)]
        return self.whole.at[pl.ds(pl.multiple_of(group * self.shard.shape[0] + first, 16), count)]

    def source(self, first, count):
        return self.shard.at[pl.ds(pl.multiple_of(first, 16), count)]

    def send(self, event, source, target, grp, seq):
        copy = pltpu.make_async_remote_copy(
            src_ref=source,
            dst_ref=target,
            send_sem=self.send_sem.at[event],
            recv_sem=self.recv_sem.at[event],
            device_id={"grp": grp, "seq": seq},
            device_id_type=MESH,
        )
        copy.start()
        self.copies[event] = copy

    def pass_on(self, event, part, grp, seq):
        self.send(event, part, part, grp, seq)

    def got(self, *events):
        for event in events:
            self.copies[event].wait_recv()

    def xor(self, k):
        if k == 1:
            return self.g + 1 - 2 * lax.rem(self.g, 2)
        if k == 2:
            return lax.rem(self.g + 2, 4)
        return 3 - self.g

    def begin(self):
        if self.routed:
            for event, k in ((0, 1), (1, 2)):
                self.send(
                    event,
                    self.source(self.start, self.size),
                    self.part(self.g, self.start, self.size),
                    self.xor(k),
                    self.s,
                )
        else:
            for k in range(1, self.groups):
                self.send(
                    k - 1,
                    self.source(self.first, self.rows),
                    self.part(self.g, self.first, self.rows),
                    lax.rem(self.g + k, self.groups),
                    self.s,
                )
        self.own = pltpu.make_async_copy(
            self.source(self.first, self.rows), self.part(self.g, self.first, self.rows), self.own_sem
        )
        self.own.start()

    def forward(self):
        if not self.routed:
            return
        x, y = self.xor(1), self.xor(2)
        self.got(0, 1)
        self.pass_on(2, self.part(y, self.start, self.cut), x, self.s)
        self.pass_on(3, self.part(x, self.start + self.cut, self.size - self.cut), y, self.s)
        for event, k in ((0, x), (1, y)):
            near = self.part(k, self.start, self.size)
            if self.deep:
                self.pass_on(7 + event, near, self.g, self.paired)
            self.pass_on(4 + event, near, self.g, self.other)

    def share(self):
        if not self.routed:
            return
        self.got(2, 3)
        far = self.part(self.xor(3), self.start, self.size)
        if self.deep:
            self.pass_on(9, far, self.g, self.paired)
        self.pass_on(6, far, self.g, self.other)

    def relay(self):
        if not self.deep:
            return
        for event, k in ((0, 1), (1, 2), (2, 3)):
            self.got(7 + event)
            self.pass_on(10 + event, self.part(self.xor(k), self.paired_start, self.size), self.g, self.other)

    def end(self):
        self.own.wait()
        if self.deep:
            self.got(4, 5, 6, 10, 11, 12)
        elif self.routed:
            self.got(4, 5, 6)
        else:
            self.got(*range(self.groups - 1))

    def drain(self):
        for copy in self.copies.values():
            copy.wait_send()


def encoder_kernel(
    groups,
    seqs,
    audio_block,
    ids,
    gain,
    moe_gain,
    routes,
    route_weights,
    qkv_shard,
    out_shard,
    adapter_shard,
    thinker,
    expert_in,
    tables,
    qkv_w,
    out_w,
    adapter_w,
    normed,
    query,
    pairs,
    ids_ext,
    table,
    attended,
    even,
    odd,
    own_sem,
    weight_send,
    weight_recv,
    edge_send,
    edge_recv,
    tab_send,
    tab_recv,
):
    g, s = lax.axis_index("grp"), lax.axis_index("seq")
    audio = audio_block.at[0]
    frames, width = audio.shape
    heads_pairs = width // 128
    blocks = frames // EDGE
    experts = lax.broadcasted_iota(jnp.int32, (128, table.shape[0]), 0)
    given = route_weights[...]
    shares = given / jnp.sum(given, axis=0, keepdims=True)
    chosen = routes[...]
    table[...] = sum(
        jnp.where(experts == chosen[k : k + 1], shares[k : k + 1], 0.0) for k in range(chosen.shape[0])
    ).T
    for b in range(blocks):
        ids_ext[b + 1] = jnp.broadcast_to(ids[0:1, b * EDGE : (b + 1) * EDGE], (8, EDGE))
    greet(g, s, groups, seqs, True)

    def gather(i, shard, whole, rows, by_lanes, deep):
        return Gather(
            g, s, groups, seqs, shard, whole, rows, by_lanes, deep, own_sem.at[i], weight_send.at[i], weight_recv.at[i]
        )

    def split(rows, at):
        return (0, at), (at, rows - at)

    qkv_rows, ad_rows = qkv_shard.shape[0], adapter_shard.shape[0]
    qkv_deep, qkv_plain = split(qkv_rows, (qkv_rows // 2 + 63) // 64 * 64)
    ad_deep, ad_plain = split(ad_rows, ad_rows // 2)
    qkv_a = gather(0, qkv_shard, qkv_w, qkv_deep, False, True)
    qkv_b = gather(1, qkv_shard, qkv_w, qkv_plain, False, False)
    out = gather(2, out_shard, out_w, (0, out_shard.shape[0]), False, False)
    ad_a = gather(3, adapter_shard, adapter_w, ad_deep, True, True)
    ad_b = gather(4, adapter_shard, adapter_w, ad_plain, True, False)
    qkv_a.begin()
    qkv_b.begin()

    table_copies = []
    for k in range(1, seqs):
        copy = pltpu.make_async_remote_copy(
            src_ref=table,
            dst_ref=tables.at[s],
            send_sem=tab_send.at[k - 1],
            recv_sem=tab_recv.at[k - 1],
            device_id={"grp": g, "seq": lax.rem(s + k, seqs)},
            device_id_type=MESH,
        )
        copy.start()
        table_copies.append(copy)
    tables[s] = table[...]

    def edge(event, source, target, step):
        return pltpu.make_async_remote_copy(
            src_ref=source,
            dst_ref=target,
            send_sem=edge_send.at[event],
            recv_sem=edge_recv.at[event],
            device_id={"grp": g, "seq": lax.rem(s + step + seqs, seqs)},
            device_id_type=MESH,
        )

    ids_right = edge(0, ids_ext.at[blocks], ids_ext.at[0], 1)
    ids_left = edge(1, ids_ext.at[1], ids_ext.at[blocks + 1], -1)
    pairs_right = edge(2, pairs.at[pl.ds(frames, EDGE)], pairs.at[pl.ds(0, EDGE)], 1)
    pairs_left = edge(3, pairs.at[pl.ds(EDGE, EDGE)], pairs.at[pl.ds(frames + EDGE, EDGE)], -1)
    has_left, has_right = s > 0, s < seqs - 1

    @pl.when(has_right)
    def _():
        ids_right.start()

    @pl.when(has_left)
    def _():
        ids_left.start()

    @pl.when(s == 0)
    def _():
        ids_ext[0] = jnp.full(ids_ext.shape[1:], -1, jnp.int32)
        pairs[0:EDGE] = jnp.zeros((EDGE, pairs.shape[1]), BF16)

    @pl.when(s == seqs - 1)
    def _():
        ids_ext[blocks + 1] = jnp.full(ids_ext.shape[1:], -1, jnp.int32)
        pairs[frames + EDGE :] = jnp.zeros((EDGE, pairs.shape[1]), BF16)

    def norm_rows(i, _):
        rows = pl.ds(pl.multiple_of(i * 64, 64), 64)
        signal = audio[rows].astype(F32)
        centred = signal - jnp.mean(signal, axis=-1, keepdims=True)
        variance = jnp.mean(centred * centred, axis=-1, keepdims=True)
        normed[rows] = (centred * lax.rsqrt(variance + LN_EPSILON) * gain[...]).astype(BF16)
        return 0

    lax.fori_loop(0, frames // 64, norm_rows, 0)

    qkv_a.forward()
    qkv_b.forward()
    out.begin()
    ad_a.begin()
    qkv_a.share()
    qkv_b.share()
    qkv_a.relay()
    qkv_a.end()
    qkv_b.end()

    tile = 256

    def project_pairs(i, _):
        source = pl.ds(pl.multiple_of(width + i * tile, tile), tile)
        columns = pl.ds(pl.multiple_of(i * tile, tile), tile)
        pairs[EDGE : EDGE + frames, columns] = lax.dot_general(
            normed[...], qkv_w[source], NT, preferred_element_type=F32
        ).astype(BF16)
        return 0

    lax.fori_loop(0, 2 * width // tile, project_pairs, 0)

    @pl.when(has_right)
    def _():
        pairs_right.start()

    @pl.when(has_left)
    def _():
        pairs_left.start()

    out.forward()
    ad_b.begin()

    def project_query(i, _):
        columns = pl.ds(pl.multiple_of(i * tile, tile), tile)
        query[:, columns] = lax.dot_general(
            normed[...], qkv_w[columns], NT, preferred_element_type=F32
        ).astype(BF16)
        return 0

    lax.fori_loop(0, width // tile, project_query, 0)
    out.share()
    ad_a.forward()

    @pl.when(has_left)
    def _():
        ids_right.wait_recv()
        pairs_right.wait_recv()

    @pl.when(has_right)
    def _():
        ids_left.wait_recv()
        pairs_left.wait_recv()

    low = lax.broadcasted_iota(jnp.int32, (EDGE, 128), 1) < HEAD
    span = 3 * EDGE
    for b in range(blocks):
        rows = slice(b * EDGE, (b + 1) * EDGE)
        keys = slice(b * EDGE, b * EDGE + span)
        key_ids = jnp.concatenate([ids_ext[b + j][0:1] for j in range(3)], axis=1)
        frame_ids = jnp.broadcast_to(ids_ext[b + 1][0:1], (EDGE, EDGE)).T[:, 0:1]
        same = frame_ids == key_ids
        allowed = jnp.concatenate([same, same], axis=0)

        def attend(p, _, rows=rows, keys=keys, allowed=allowed):
            columns = pl.ds(pl.multiple_of(p * 128, 128), 128)
            both = query[rows, columns]
            nothing = jnp.zeros_like(both)
            stacked = jnp.concatenate(
                [jnp.where(low, both, nothing), jnp.where(low, nothing, both)], axis=0
            )
            scores = lax.dot_general(
                stacked, pairs[keys, columns], NT, preferred_element_type=F32
            ) * HEAD ** (-0.5)
            scores = jnp.where(allowed, scores, MASKED)
            highest = jnp.max(scores, axis=-1, keepdims=True)
            exponent = jnp.exp(scores - highest)
            total = jnp.sum(exponent, axis=-1, keepdims=True)
            value_columns = pl.ds(pl.multiple_of(width + p * 128, 128), 128)
            mixed = jnp.dot(
                (exponent / total).astype(BF16), pairs[keys, value_columns], preferred_element_type=F32
            )
            attended[rows, columns] = jnp.where(low, mixed[:EDGE], mixed[EDGE:]).astype(BF16)
            return 0

        lax.fori_loop(0, heads_pairs, attend, 0)

    out.end()
    tokens = frames // 2
    at_row = lax.broadcasted_iota(jnp.int32, (tokens, frames), 0)
    at_frame = lax.broadcasted_iota(jnp.int32, (tokens, frames), 1)
    first = jnp.where(at_frame == 2 * at_row, 1.0, 0.0).astype(BF16)
    second = jnp.where(at_frame == 2 * at_row + 1, 1.0, 0.0).astype(BF16)

    def encode(i, _):
        columns = pl.ds(pl.multiple_of(i * tile, tile), tile)
        projected = lax.dot_general(attended[...], out_w[columns], NT, preferred_element_type=F32)
        encoded = (audio[:, columns].astype(F32) + projected).astype(BF16)
        even[:, columns] = jnp.dot(first, encoded, preferred_element_type=F32).astype(BF16)
        odd[:, columns] = jnp.dot(second, encoded, preferred_element_type=F32).astype(BF16)
        return 0

    lax.fori_loop(0, width // tile, encode, 0)
    ad_b.forward()
    ad_a.share()
    ad_a.relay()
    ad_b.share()
    ad_a.end()
    ad_b.end()

    def adapt(i, _):
        columns = pl.ds(pl.multiple_of(i * tile, tile), tile)
        thinker[:, columns] = (
            jnp.dot(even[...], adapter_w[0:width, columns], preferred_element_type=F32)
            + jnp.dot(odd[...], adapter_w[width:, columns], preferred_element_type=F32)
        ).astype(BF16)
        return 0

    lax.fori_loop(0, thinker.shape[1] // tile, adapt, 0)

    def rms_rows(i, _):
        rows = pl.ds(pl.multiple_of(i * 32, 32), 32)
        widened = thinker[rows].astype(F32)
        squares = jnp.mean(widened * widened, axis=-1, keepdims=True)
        expert_in[rows] = (widened * lax.rsqrt(squares + RMS_EPSILON) * moe_gain[...]).astype(BF16)
        return 0

    lax.fori_loop(0, tokens // 32, rms_rows, 0)

    for copy in table_copies:
        copy.wait()
    for weight in (qkv_a, qkv_b, out, ad_a, ad_b):
        weight.drain()

    @pl.when(has_right)
    def _():
        ids_right.wait_send()
        pairs_right.wait_send()

    @pl.when(has_left)
    def _():
        ids_left.wait_send()
        pairs_left.wait_send()


def expert_kernel(
    seqs,
    expert_in,
    thinker,
    tables,
    gate_hbm,
    up_hbm,
    down_hbm,
    result,
    gate_w,
    up_w,
    down_w,
    tokens_all,
    hidden,
    mine,
    theirs,
    to_other,
    incoming,
    outgoing,
    load_sem,
    tok_send,
    tok_recv,
    half_send,
    half_recv,
    sum_send,
    sum_recv,
):
    g, s = lax.axis_index("grp"), lax.axis_index("seq")
    planes = seqs // 2
    z, c = s // 2, lax.rem(s, 2)
    other = 1 - c
    rows, width = expert_in.shape
    ff = gate_w.shape[1]
    loads = [
        pltpu.make_async_copy(source, target, load_sem.at[i])
        for i, (source, target) in enumerate(((gate_hbm, gate_w), (up_hbm, up_w), (down_hbm, down_w)))
    ]
    for load in loads:
        load.start()
    greet(g, s, 1, seqs, False)

    part = rows // 2

    def span(h):
        return pl.ds(pl.multiple_of(h * part, part), part)

    def move(source, target, send, recv, plane, core):
        return pltpu.make_async_remote_copy(
            src_ref=source,
            dst_ref=target,
            send_sem=send,
            recv_sem=recv,
            device_id={"grp": g, "seq": plane * 2 + core},
            device_id_type=MESH,
        )

    def token_copy(side, origin, h, plane, own=False):
        slot = tokens_all.at[origin, c, span(h)]
        source = expert_in.at[span(h)] if own else slot
        return move(source, slot, tok_send.at[side, origin, h], tok_recv.at[0, origin, h], plane, c)

    def other_copy(origin, h, own=False):
        slot = tokens_all.at[origin, c, span(h)]
        source = expert_in.at[span(h)] if own else slot
        return move(source, slot, tok_send.at[2, origin, h], tok_recv.at[1, origin, h], z, other)

    def half_copy(origin, h):
        return move(
            to_other.at[origin, span(h)],
            theirs.at[origin, span(h)],
            half_send.at[origin, h],
            half_recv.at[origin, h],
            z,
            other,
        )

    def sum_copy(side, target, h, plane):
        return move(
            outgoing.at[side, target, span(h)],
            incoming.at[side, target, span(h)],
            sum_send.at[side, target, h],
            sum_recv.at[side, target, h],
            plane,
            c,
        )

    has_above, has_below = z < planes - 1, z > 0

    @pl.when(has_above)
    def _():
        token_copy(0, z, 0, z + 1, True).start()

    @pl.when(has_below)
    def _():
        token_copy(1, z, 0, z - 1, True).start()

    other_copy(z, 0, True).start()

    @pl.when(z == 0)
    def _():
        token_copy(0, z, 1, z + 1, True).start()

    @pl.when(z == planes - 1)
    def _():
        token_copy(1, z, 1, z - 1, True).start()

    other_copy(z, 1, True).start()
    tokens_all[z, c] = expert_in[...]
    for load in loads:
        load.wait()
    lanes = lax.broadcasted_iota(jnp.int32, (part, tables.shape[2]), 1)
    rise_tile = 384 if ff % 384 == 0 else 128
    fall_tile = 512 if width % 512 == 0 else 128

    def experts(origin, h):
        other_copy(origin, h).wait_recv()

        def rise(i, _):
            columns = pl.ds(pl.multiple_of(i * rise_tile, rise_tile), rise_tile)
            batch = tokens_all[origin, :, span(h)].reshape(2 * part, width)
            gate = jnp.dot(batch, gate_w[:, columns], preferred_element_type=F32)
            up = jnp.dot(batch, up_w[:, columns], preferred_element_type=F32)
            hidden[:, columns] = (gate / (1.0 + jnp.exp(-gate)) * up).astype(BF16)
            return 0

        lax.fori_loop(0, ff // rise_tile, rise, 0)
        share = [
            jnp.sum(jnp.where(lanes == s, tables[origin * 2 + k, span(h)], 0.0), axis=1, keepdims=True)
            for k in range(2)
        ]
        share = jnp.concatenate(share, axis=0)

        def fall(i, _):
            columns = pl.ds(pl.multiple_of(i * fall_tile, fall_tile), fall_tile)
            produced = jnp.dot(hidden[...], down_w[:, columns], preferred_element_type=F32)
            weighted = (produced.astype(BF16).astype(F32) * share).astype(BF16)
            mine[origin, span(h), columns] = jnp.where(c == 0, weighted[:part], weighted[part:])
            to_other[origin, span(h), columns] = jnp.where(c == 0, weighted[part:], weighted[:part])
            return 0

        lax.fori_loop(0, width // fall_tile, fall, 0)
        half_copy(origin, h).start()

    def take(side, origin, h):
        token_copy(side, origin, h, z).wait_recv()

        @pl.when(jnp.where(side == 0, has_above, has_below))
        def _():
            token_copy(side, origin, h, z + 1 - 2 * side).start()

        other_copy(origin, h).start()

    def send_sum(side, origin, h, starts):
        half_copy(origin, h).wait_recv()
        total = mine[origin, span(h)].astype(F32) + theirs[origin, span(h)].astype(F32)
        if starts:
            outgoing[side, origin, span(h)] = total.astype(BF16)
        else:
            sum_copy(side, origin, h, z).wait_recv()
            came = incoming[side, origin, span(h)].astype(F32)
            outgoing[side, origin, span(h)] = (total + came).astype(BF16)
        sum_copy(side, origin, h, z + 2 * side - 1).start()

    def arrival(side, t):
        reach = jnp.where(side == 0, z, planes - 1 - z)
        first = t <= reach
        distance = jnp.where(first, t, 2 * reach + 1 - t)
        valid = (t >= 1) & (t <= 2 * reach)
        return z + (2 * side - 1) * distance, jnp.where(first, 0, 1), valid, t == 2 * reach

    ends = (z == planes - 1, z == 0)
    experts(z, 0)

    def slot(t, _):
        for side in range(2):
            origin, h, valid, last = arrival(side, t)

            @pl.when(valid)
            def _(side=side, origin=origin, h=h):
                take(side, origin, h)

            @pl.when(last & (has_above, has_below)[side])
            def _(side=side):
                token_copy(side, z, 1, z + 1 - 2 * side, True).start()

        for side in range(2):
            passed = jnp.where(side == 0, planes - 1 - z, z)
            origin, h, valid, _ = arrival(side, t - 2 * passed - 1)

            @pl.when(valid & jnp.logical_not(ends[side]))
            def _(side=side, origin=origin, h=h):
                send_sum(side, origin, h, False)

        def compute(j, _):
            side = jnp.where(z >= planes // 2, j, 1 - j)
            origin, h, valid, _ = arrival(side, t)
            own = j == 2
            now = t == jnp.where(ends[0] | ends[1], 1, 2 * planes - 3)

            @pl.when(jnp.where(own, now, valid))
            def _():
                experts(jnp.where(own, z, origin), jnp.where(own, 1, h))

            @pl.when(jnp.logical_not(own) & valid & jnp.where(side == 0, ends[0], ends[1]))
            def _():
                send_sum(side, origin, h, True)

            return 0

        lax.fori_loop(0, 3, compute, 0)
        return 0

    lax.fori_loop(1, 2 * planes, slot, 0)

    @pl.when(z == 0)
    def _():
        incoming[1, z] = jnp.zeros((rows, width), BF16)

    @pl.when(z == planes - 1)
    def _():
        incoming[0, z] = jnp.zeros((rows, width), BF16)

    for h in range(2):
        half_copy(z, h).wait_recv()

        @pl.when(has_below)
        def _(h=h):
            sum_copy(1, z, h, z).wait_recv()

        @pl.when(has_above)
        def _(h=h):
            sum_copy(0, z, h, z).wait_recv()

        def finish(i, _, h=h):
            here = pl.ds(pl.multiple_of(h * part + i * 32, 32), 32)
            total = thinker[here].astype(F32) + mine[z, here].astype(F32) + theirs[z, here].astype(F32)
            total = total + incoming[0, z, here].astype(F32) + incoming[1, z, here].astype(F32)
            result[here] = total.astype(BF16)
            return 0

        lax.fori_loop(0, part // 32, finish, 0)

    def drain(origin, _):
        for h in range(2):
            other_copy(origin, h).wait_send()
            half_copy(origin, h).wait_send()

            @pl.when((origin <= z) & has_above)
            def _(h=h):
                token_copy(0, origin, h, z).wait_send()

            @pl.when((origin >= z) & has_below)
            def _(h=h):
                token_copy(1, origin, h, z).wait_send()

            @pl.when(origin > z)
            def _(h=h):
                sum_copy(1, origin, h, z).wait_send()

            @pl.when(origin < z)
            def _(h=h):
                sum_copy(0, origin, h, z).wait_send()

        return 0

    lax.fori_loop(0, planes, drain, 0)


def body(
    groups,
    seqs,
    audio,
    block_ids,
    norm_gain,
    qkv_weight,
    out_weight,
    adapter_weight,
    moe_gain,
    gate_weight,
    up_weight,
    down_weight,
    routes,
    route_weights,
):
    frames, width = audio.shape[1:]
    tokens, features = routes.shape[1], moe_gain.shape[0]
    blocks = frames // EDGE
    vmem = pl.BlockSpec(memory_space=pltpu.VMEM)
    anywhere = pl.BlockSpec(memory_space=pl.ANY)
    dma = pltpu.SemaphoreType.DMA
    events = max(13, groups - 1)
    thinker, expert_in, tables = pl.pallas_call(
        functools.partial(encoder_kernel, groups, seqs),
        out_shape=(
            jax.ShapeDtypeStruct((tokens, features), BF16),
            jax.ShapeDtypeStruct((tokens, features), BF16),
            jax.ShapeDtypeStruct((seqs, tokens, 128), F32),
        ),
        in_specs=[vmem] * 6 + [anywhere] * 3,
        out_specs=(vmem,) * 3,
        scratch_shapes=[
            pltpu.VMEM((3 * width, width), BF16),
            pltpu.VMEM((width, width), BF16),
            pltpu.VMEM((2 * width, features), BF16),
            pltpu.VMEM((frames, width), BF16),
            pltpu.VMEM((frames, width), BF16),
            pltpu.VMEM((frames + 2 * EDGE, 2 * width), BF16),
            pltpu.VMEM((blocks + 2, 8, EDGE), jnp.int32),
            pltpu.VMEM((tokens, 128), F32),
            pltpu.VMEM((frames, width), BF16),
            pltpu.VMEM((frames // 2, width), BF16),
            pltpu.VMEM((frames // 2, width), BF16),
            dma((5,)),
            dma((5, events)),
            dma((5, events)),
            dma((4,)),
            dma((4,)),
            dma((seqs - 1,)),
            dma((seqs - 1,)),
        ],
        compiler_params=pltpu.CompilerParams(
            collective_id=0, has_side_effects=True, vmem_limit_bytes=VMEM_LIMIT
        ),
        name="encoder",
    )(
        audio,
        block_ids,
        norm_gain,
        moe_gain,
        routes[0].T,
        route_weights[0].T,
        qkv_weight.T,
        out_weight.T,
        adapter_weight,
    )
    planes = seqs // 2
    ff = gate_weight.shape[2]
    block = (planes, tokens, features)
    result = pl.pallas_call(
        functools.partial(expert_kernel, seqs),
        out_shape=jax.ShapeDtypeStruct((tokens, features), BF16),
        in_specs=[vmem] * 3 + [anywhere] * 3,
        out_specs=vmem,
        scratch_shapes=[
            pltpu.VMEM((features, ff), BF16),
            pltpu.VMEM((features, ff), BF16),
            pltpu.VMEM((ff, features), BF16),
            pltpu.VMEM((planes, 2, tokens, features), BF16),
            pltpu.VMEM((tokens, ff), BF16),
            pltpu.VMEM(block, BF16),
            pltpu.VMEM(block, BF16),
            pltpu.VMEM(block, BF16),
            pltpu.VMEM((2,) + block, BF16),
            pltpu.VMEM((2,) + block, BF16),
            dma((3,)),
            dma((3, planes, 2)),
            dma((2, planes, 2)),
            dma((planes, 2)),
            dma((planes, 2)),
            dma((2, planes, 2)),
            dma((2, planes, 2)),
        ],
        compiler_params=pltpu.CompilerParams(
            collective_id=1, has_side_effects=True, vmem_limit_bytes=VMEM_LIMIT
        ),
        name="experts",
    )(expert_in, thinker, tables, gate_weight[0], up_weight[0], down_weight[0])
    return result[None]


def solution(mesh):
    placed = (
        P("grp", "seq", None),
        P("grp", "seq"),
        P(),
        P(None, "grp"),
        P(None, "grp"),
        P(None, "grp"),
        P(),
        P("seq", None, None),
        P("seq", None, None),
        P("seq", None, None),
        P("grp", "seq", None),
        P("grp", "seq", None),
    )
    return jax.shard_map(
        functools.partial(body, mesh.shape["grp"], mesh.shape["seq"]),
        mesh=mesh,
        in_specs=placed,
        out_specs=P("grp", "seq", None),
        check_vma=False,
    )
```

```python
import functools

import jax
import jax.numpy as jnp
from jax import lax
from jax.experimental import pallas as pl
from jax.experimental.pallas import tpu as pltpu
from jax.sharding import PartitionSpec as P

HEAD = 64
EDGE = 128
HALO = 112
LN_EPSILON = 1e-05
RMS_EPSILON = 1e-06
MASKED = -1e30
VMEM_LIMIT = 66_000_000
MESH = pl.DeviceIdType.MESH
BF16 = jnp.bfloat16
F32 = jnp.float32
NT = (((1,), (1,)), ((), ()))


def greet(g, s, groups, seqs, across):
    barrier = pltpu.get_barrier_semaphore()
    if across:
        for k in range(1, groups):
            pl.semaphore_signal(
                barrier, inc=1, device_id={"grp": lax.rem(g + k, groups), "seq": s}, device_id_type=MESH
            )
    for k in range(1, seqs):
        pl.semaphore_signal(
            barrier, inc=1, device_id={"grp": g, "seq": lax.rem(s + k, seqs)}, device_id_type=MESH
        )
    pl.semaphore_wait(barrier, seqs - 1 + (groups - 1 if across else 0))


def fill_table(routes, route_weights, table):
    experts = lax.broadcasted_iota(jnp.int32, table.shape, 0)
    given = route_weights[...]
    shares = given / jnp.sum(given, axis=0, keepdims=True)
    chosen = routes[...]
    table[...] = sum(
        jnp.where(experts == chosen[k : k + 1], shares[k : k + 1], 0.0) for k in range(chosen.shape[0])
    )


class Gather:
    def __init__(self, g, s, groups, seqs, shard, whole, rows, by_lanes, deep, own_sem, send_sem, recv_sem):
        self.g, self.s, self.groups = g, s, groups
        self.shard, self.whole, self.by_lanes = shard, whole, by_lanes
        self.own_sem, self.send_sem, self.recv_sem = own_sem, send_sem, recv_sem
        self.first, self.rows = rows
        self.routed = groups == 4
        self.deep = deep and self.routed and seqs % 4 == 0
        core, plane = lax.rem(s, 2), lax.rem(s // 2, 2)
        self.other = s + 1 - 2 * core
        self.paired = s + 2 - 4 * plane
        if self.deep:
            self.size = self.rows // 4
            self.start = self.first + (plane * 2 + core) * self.size
            self.paired_start = self.first + ((1 - plane) * 2 + core) * self.size
        else:
            self.size = self.rows // 2
            self.start = self.first + core * self.size
        self.cut = (self.size // 2 + 15) // 16 * 16
        self.copies = {}

    def part(self, group, first, count):
        if self.by_lanes:
            columns = self.shard.shape[1]
            start = pl.multiple_of(group * columns, 128)
            return self.whole.at[pl.ds(pl.multiple_of(first, 16), count), pl.ds(start, columns)]
        return self.whole.at[pl.ds(pl.multiple_of(group * self.shard.shape[0] + first, 16), count)]

    def source(self, first, count):
        return self.shard.at[pl.ds(pl.multiple_of(first, 16), count)]

    def send(self, event, source, target, grp, seq):
        copy = pltpu.make_async_remote_copy(
            src_ref=source,
            dst_ref=target,
            send_sem=self.send_sem.at[event],
            recv_sem=self.recv_sem.at[event],
            device_id={"grp": grp, "seq": seq},
            device_id_type=MESH,
        )
        copy.start()
        self.copies[event] = copy

    def pass_on(self, event, part, grp, seq):
        self.send(event, part, part, grp, seq)

    def got(self, *events):
        for event in events:
            self.copies[event].wait_recv()

    def xor(self, k):
        if k == 1:
            return self.g + 1 - 2 * lax.rem(self.g, 2)
        if k == 2:
            return lax.rem(self.g + 2, 4)
        return 3 - self.g

    def begin(self):
        if self.routed:
            for event, k in ((0, 1), (1, 2)):
                self.send(
                    event,
                    self.source(self.start, self.size),
                    self.part(self.g, self.start, self.size),
                    self.xor(k),
                    self.s,
                )
        else:
            for k in range(1, self.groups):
                self.send(
                    k - 1,
                    self.source(self.first, self.rows),
                    self.part(self.g, self.first, self.rows),
                    lax.rem(self.g + k, self.groups),
                    self.s,
                )
        self.own = pltpu.make_async_copy(
            self.source(self.first, self.rows), self.part(self.g, self.first, self.rows), self.own_sem
        )
        self.own.start()

    def forward(self):
        if not self.routed:
            return
        x, y = self.xor(1), self.xor(2)
        self.got(0, 1)
        self.pass_on(2, self.part(y, self.start, self.cut), x, self.s)
        self.pass_on(3, self.part(x, self.start + self.cut, self.size - self.cut), y, self.s)
        for event, k in ((0, x), (1, y)):
            near = self.part(k, self.start, self.size)
            if self.deep:
                self.pass_on(7 + event, near, self.g, self.paired)
            self.pass_on(4 + event, near, self.g, self.other)

    def share(self):
        if not self.routed:
            return
        self.got(2, 3)
        far = self.part(self.xor(3), self.start, self.size)
        if self.deep:
            self.pass_on(9, far, self.g, self.paired)
        self.pass_on(6, far, self.g, self.other)

    def relay(self):
        if not self.deep:
            return
        for event, k in ((0, 1), (1, 2), (2, 3)):
            self.got(7 + event)
            self.pass_on(10 + event, self.part(self.xor(k), self.paired_start, self.size), self.g, self.other)

    def end(self):
        self.own.wait()
        if self.deep:
            self.got(4, 5, 6, 10, 11, 12)
        elif self.routed:
            self.got(4, 5, 6)
        else:
            self.got(*range(self.groups - 1))

    def drain(self):
        for copy in self.copies.values():
            copy.wait_send()


def encoder_kernel(
    groups,
    seqs,
    audio_block,
    ids,
    gain,
    moe_gain,
    routes,
    route_weights,
    qkv_shard,
    out_shard,
    adapter_shard,
    thinker,
    expert_in,
    tables,
    qkv_w,
    out_w,
    adapter_w,
    normed,
    query,
    pairs,
    ids_ext,
    table,
    attended,
    even,
    odd,
    own_sem,
    weight_send,
    weight_recv,
    edge_send,
    edge_recv,
    tab_send,
    tab_recv,
):
    g, s = lax.axis_index("grp"), lax.axis_index("seq")
    audio = audio_block.at[0]
    frames, width = audio.shape
    heads_pairs = width // 128
    blocks = frames // EDGE
    fill_table(routes, route_weights, table)
    for b in range(blocks):
        ids_ext[b + 1] = jnp.broadcast_to(ids[0:1, b * EDGE : (b + 1) * EDGE], (8, EDGE))
    greet(g, s, groups, seqs, True)

    def gather(i, shard, whole, rows, by_lanes, deep):
        return Gather(
            g, s, groups, seqs, shard, whole, rows, by_lanes, deep, own_sem.at[i], weight_send.at[i], weight_recv.at[i]
        )

    def split(rows, at):
        return (0, at), (at, rows - at)

    qkv_rows, ad_rows = qkv_shard.shape[0], adapter_shard.shape[0]
    qkv_deep, qkv_plain = split(qkv_rows, (qkv_rows // 2 + 63) // 64 * 64)
    ad_deep, ad_plain = split(ad_rows, ad_rows // 2)
    qkv_a = gather(0, qkv_shard, qkv_w, qkv_deep, False, True)
    qkv_b = gather(1, qkv_shard, qkv_w, qkv_plain, False, False)
    out = gather(2, out_shard, out_w, (0, out_shard.shape[0]), False, False)
    ad_a = gather(3, adapter_shard, adapter_w, ad_deep, True, True)
    ad_b = gather(4, adapter_shard, adapter_w, ad_plain, True, False)
    qkv_a.begin()
    qkv_b.begin()

    table_copies = []
    for k in range(1, seqs):
        copy = pltpu.make_async_remote_copy(
            src_ref=table,
            dst_ref=tables.at[s],
            send_sem=tab_send.at[k - 1],
            recv_sem=tab_recv.at[k - 1],
            device_id={"grp": g, "seq": lax.rem(s + k, seqs)},
            device_id_type=MESH,
        )
        copy.start()
        table_copies.append(copy)
    tables[s] = table[...]

    def edge(event, source, target, step):
        return pltpu.make_async_remote_copy(
            src_ref=source,
            dst_ref=target,
            send_sem=edge_send.at[event],
            recv_sem=edge_recv.at[event],
            device_id={"grp": g, "seq": lax.rem(s + step + seqs, seqs)},
            device_id_type=MESH,
        )

    ids_right = edge(0, ids_ext.at[blocks], ids_ext.at[0], 1)
    ids_left = edge(1, ids_ext.at[1], ids_ext.at[blocks + 1], -1)
    pairs_right = edge(2, pairs.at[pl.ds(frames, EDGE)], pairs.at[pl.ds(0, EDGE)], 1)
    pairs_left = edge(3, pairs.at[pl.ds(EDGE, EDGE)], pairs.at[pl.ds(frames + EDGE, EDGE)], -1)
    has_left, has_right = s > 0, s < seqs - 1

    @pl.when(has_right)
    def _():
        ids_right.start()

    @pl.when(has_left)
    def _():
        ids_left.start()

    @pl.when(s == 0)
    def _():
        ids_ext[0] = jnp.full(ids_ext.shape[1:], -1, jnp.int32)
        pairs[0:EDGE] = jnp.zeros((EDGE, pairs.shape[1]), BF16)

    @pl.when(s == seqs - 1)
    def _():
        ids_ext[blocks + 1] = jnp.full(ids_ext.shape[1:], -1, jnp.int32)
        pairs[frames + EDGE :] = jnp.zeros((EDGE, pairs.shape[1]), BF16)

    def norm_rows(i, _):
        rows = pl.ds(pl.multiple_of(i * 64, 64), 64)
        signal = audio[rows].astype(F32)
        centred = signal - jnp.mean(signal, axis=-1, keepdims=True)
        variance = jnp.mean(centred * centred, axis=-1, keepdims=True)
        normed[rows] = (centred * lax.rsqrt(variance + LN_EPSILON) * gain[...]).astype(BF16)
        return 0

    lax.fori_loop(0, frames // 64, norm_rows, 0)

    qkv_a.forward()
    qkv_b.forward()
    out.begin()
    ad_a.begin()
    qkv_a.share()
    qkv_b.share()
    qkv_a.relay()
    qkv_a.end()
    qkv_b.end()

    tile = 256

    def project_pairs(i, _):
        source = pl.ds(pl.multiple_of(width + i * tile, tile), tile)
        columns = pl.ds(pl.multiple_of(i * tile, tile), tile)
        pairs[EDGE : EDGE + frames, columns] = lax.dot_general(
            normed[...], qkv_w[source], NT, preferred_element_type=F32
        ).astype(BF16)
        return 0

    lax.fori_loop(0, 2 * width // tile, project_pairs, 0)

    @pl.when(has_right)
    def _():
        pairs_right.start()

    @pl.when(has_left)
    def _():
        pairs_left.start()

    out.forward()
    ad_b.begin()

    def project_query(i, _):
        columns = pl.ds(pl.multiple_of(i * tile, tile), tile)
        query[:, columns] = lax.dot_general(
            normed[...], qkv_w[columns], NT, preferred_element_type=F32
        ).astype(BF16)
        return 0

    lax.fori_loop(0, width // tile, project_query, 0)
    out.share()
    ad_a.forward()

    @pl.when(has_left)
    def _():
        ids_right.wait_recv()
        pairs_right.wait_recv()

    @pl.when(has_right)
    def _():
        ids_left.wait_recv()
        pairs_left.wait_recv()

    low = lax.broadcasted_iota(jnp.int32, (EDGE, 128), 1) < HEAD
    span = 3 * EDGE
    for b in range(blocks):
        rows = slice(b * EDGE, (b + 1) * EDGE)
        keys = slice(b * EDGE, b * EDGE + span)
        key_ids = jnp.concatenate([ids_ext[b + j][0:1] for j in range(3)], axis=1)
        frame_ids = jnp.broadcast_to(ids_ext[b + 1][0:1], (EDGE, EDGE)).T[:, 0:1]
        same = frame_ids == key_ids
        allowed = jnp.concatenate([same, same], axis=0)

        def attend(p, _, rows=rows, keys=keys, allowed=allowed):
            columns = pl.ds(pl.multiple_of(p * 128, 128), 128)
            both = query[rows, columns]
            nothing = jnp.zeros_like(both)
            stacked = jnp.concatenate(
                [jnp.where(low, both, nothing), jnp.where(low, nothing, both)], axis=0
            )
            scores = lax.dot_general(
                stacked, pairs[keys, columns], NT, preferred_element_type=F32
            ) * HEAD ** (-0.5)
            scores = jnp.where(allowed, scores, MASKED)
            highest = jnp.max(scores, axis=-1, keepdims=True)
            exponent = jnp.exp(scores - highest)
            total = jnp.sum(exponent, axis=-1, keepdims=True)
            value_columns = pl.ds(pl.multiple_of(width + p * 128, 128), 128)
            mixed = jnp.dot(
                (exponent / total).astype(BF16), pairs[keys, value_columns], preferred_element_type=F32
            )
            attended[rows, columns] = jnp.where(low, mixed[:EDGE], mixed[EDGE:]).astype(BF16)
            return 0

        lax.fori_loop(0, heads_pairs, attend, 0)

    out.end()
    tokens = frames // 2
    at_row = lax.broadcasted_iota(jnp.int32, (tokens, frames), 0)
    at_frame = lax.broadcasted_iota(jnp.int32, (tokens, frames), 1)
    first = jnp.where(at_frame == 2 * at_row, 1.0, 0.0).astype(BF16)
    second = jnp.where(at_frame == 2 * at_row + 1, 1.0, 0.0).astype(BF16)

    def encode(i, _):
        columns = pl.ds(pl.multiple_of(i * tile, tile), tile)
        projected = lax.dot_general(attended[...], out_w[columns], NT, preferred_element_type=F32)
        encoded = (audio[:, columns].astype(F32) + projected).astype(BF16)
        even[:, columns] = jnp.dot(first, encoded, preferred_element_type=F32).astype(BF16)
        odd[:, columns] = jnp.dot(second, encoded, preferred_element_type=F32).astype(BF16)
        return 0

    lax.fori_loop(0, width // tile, encode, 0)
    ad_b.forward()
    ad_a.share()
    ad_a.relay()
    ad_b.share()
    ad_a.end()
    ad_b.end()

    def adapt(i, _):
        columns = pl.ds(pl.multiple_of(i * tile, tile), tile)
        thinker[:, columns] = (
            jnp.dot(even[...], adapter_w[0:width, columns], preferred_element_type=F32)
            + jnp.dot(odd[...], adapter_w[width:, columns], preferred_element_type=F32)
        ).astype(BF16)
        return 0

    lax.fori_loop(0, thinker.shape[1] // tile, adapt, 0)

    def rms_rows(i, _):
        rows = pl.ds(pl.multiple_of(i * 32, 32), 32)
        widened = thinker[rows].astype(F32)
        squares = jnp.mean(widened * widened, axis=-1, keepdims=True)
        expert_in[rows] = (widened * lax.rsqrt(squares + RMS_EPSILON) * moe_gain[...]).astype(BF16)
        return 0

    lax.fori_loop(0, tokens // 32, rms_rows, 0)

    for copy in table_copies:
        copy.wait()
    for weight in (qkv_a, qkv_b, out, ad_a, ad_b):
        weight.drain()

    @pl.when(has_right)
    def _():
        ids_right.wait_send()
        pairs_right.wait_send()

    @pl.when(has_left)
    def _():
        ids_left.wait_send()
        pairs_left.wait_send()


def attention_kernel(
    groups,
    seqs,
    audio_block,
    ids,
    gain,
    routes,
    route_weights,
    qkv_shard,
    out_shard,
    pooled,
    tables,
    qkv_w,
    out_w,
    normed,
    query,
    pairs,
    halo,
    ids_ext,
    table,
    attended,
    own_sem,
    weight_send,
    weight_recv,
    edge_send,
    edge_recv,
    tab_send,
    tab_recv,
):
    g, s = lax.axis_index("grp"), lax.axis_index("seq")
    audio = audio_block.at[0]
    frames, width = audio.shape
    blocks = frames // EDGE
    fill_table(routes, route_weights, table)
    for b in range(blocks):
        ids_ext[b + 1] = jnp.broadcast_to(ids[0:1, b * EDGE : (b + 1) * EDGE], (8, EDGE))
    greet(g, s, groups, seqs, True)

    def gather(i, shard, whole, first, rows, deep):
        return Gather(
            g, s, groups, seqs, shard, whole, (first, rows), False, deep,
            own_sem.at[i], weight_send.at[i], weight_recv.at[i],
        )

    def part(rows, share):
        return int(rows * share + 32) // 64 * 64

    qkv_rows, out_rows = qkv_shard.shape[0], out_shard.shape[0]
    one, two, deep_out = part(qkv_rows, 0.333), part(qkv_rows, 0.6), part(out_rows, 0.6)
    qkv_a = gather(0, qkv_shard, qkv_w, 0, one, True)
    qkv_b = gather(1, qkv_shard, qkv_w, one, two - one, True)
    qkv_c = gather(2, qkv_shard, qkv_w, two, qkv_rows - two, False)
    out_a = gather(3, out_shard, out_w, 0, deep_out, True)
    out_b = gather(4, out_shard, out_w, deep_out, out_rows - deep_out, False)
    qkv_a.begin()

    def edge(event, source, target, step):
        return pltpu.make_async_remote_copy(
            src_ref=source,
            dst_ref=target,
            send_sem=edge_send.at[event],
            recv_sem=edge_recv.at[event],
            device_id={"grp": g, "seq": lax.rem(s + step + seqs, seqs)},
            device_id_type=MESH,
        )

    ids_right = edge(0, ids_ext.at[blocks], ids_ext.at[0], 1)
    ids_left = edge(1, ids_ext.at[1], ids_ext.at[blocks + 1], -1)
    halo_right = edge(2, audio.at[pl.ds(frames - HALO, HALO)], halo.at[0], 1)
    halo_left = edge(3, audio.at[pl.ds(0, HALO)], halo.at[1], -1)
    has_left, has_right = s > 0, s < seqs - 1

    @pl.when(has_right)
    def _():
        ids_right.start()
        halo_right.start()

    @pl.when(has_left)
    def _():
        ids_left.start()
        halo_left.start()

    qkv_b.begin()
    qkv_c.begin()
    table_copies = []
    for k in range(1, seqs):
        copy = pltpu.make_async_remote_copy(
            src_ref=table,
            dst_ref=tables.at[s],
            send_sem=tab_send.at[k - 1],
            recv_sem=tab_recv.at[k - 1],
            device_id={"grp": g, "seq": lax.rem(s + k, seqs)},
            device_id_type=MESH,
        )
        copy.start()
        table_copies.append(copy)
    tables[s] = table[...]

    @pl.when(s == 0)
    def _():
        ids_ext[0] = jnp.full(ids_ext.shape[1:], -1, jnp.int32)
        halo[0] = jnp.zeros(halo.shape[1:], BF16)

    @pl.when(s == seqs - 1)
    def _():
        ids_ext[blocks + 1] = jnp.full(ids_ext.shape[1:], -1, jnp.int32)
        halo[1] = jnp.zeros(halo.shape[1:], BF16)

    def layer_norm(signal):
        signal = signal.astype(F32)
        centred = signal - jnp.mean(signal, axis=-1, keepdims=True)
        variance = jnp.mean(centred * centred, axis=-1, keepdims=True)
        return (centred * lax.rsqrt(variance + LN_EPSILON) * gain[...]).astype(BF16)

    def norm_rows(i, _):
        rows = pl.multiple_of(i * 64, 64)
        normed[pl.ds(EDGE + rows, 64)] = layer_norm(audio[pl.ds(rows, 64)])
        return 0

    lax.fori_loop(0, frames // 64, norm_rows, 0)
    spare = jnp.zeros((EDGE - HALO, width), BF16)
    normed[0 : EDGE - HALO] = spare
    normed[frames + EDGE + HALO :] = spare
    qkv_a.forward()

    @pl.when(has_left)
    def _():
        ids_right.wait_recv()
        halo_right.wait_recv()

    @pl.when(has_right)
    def _():
        ids_left.wait_recv()
        halo_left.wait_recv()

    def norm_halo(i, _):
        rows = pl.multiple_of(i * 16, 16)
        normed[pl.ds(EDGE - HALO + rows, 16)] = layer_norm(halo[0, pl.ds(rows, 16)])
        normed[pl.ds(EDGE + frames + rows, 16)] = layer_norm(halo[1, pl.ds(rows, 16)])
        return 0

    lax.fori_loop(0, HALO // 16, norm_halo, 0)
    qkv_b.forward()
    qkv_c.forward()
    out_a.begin()
    out_b.begin()
    qkv_a.share()
    qkv_b.share()
    qkv_a.relay()
    qkv_c.share()
    qkv_b.relay()
    qkv_a.end()
    qkv_b.end()
    qkv_c.end()
    tile = 256

    def project_pairs(i, _):
        source = pl.ds(pl.multiple_of(width + i * tile, tile), tile)
        columns = pl.ds(pl.multiple_of(i * tile, tile), tile)
        pairs[:, columns] = lax.dot_general(
            normed[...], qkv_w[source], NT, preferred_element_type=F32
        ).astype(BF16)
        return 0

    lax.fori_loop(0, 2 * width // tile, project_pairs, 0)
    out_a.forward()
    out_b.forward()

    def project_query(i, _):
        columns = pl.ds(pl.multiple_of(i * tile, tile), tile)
        query[:, columns] = lax.dot_general(
            normed[EDGE : EDGE + frames], qkv_w[columns], NT, preferred_element_type=F32
        ).astype(BF16) * BF16(HEAD ** (-0.5))
        return 0

    lax.fori_loop(0, width // tile, project_query, 0)
    out_a.share()
    out_b.share()
    low = lax.broadcasted_iota(jnp.int32, (EDGE, 128), 1) < HEAD
    span = 3 * EDGE
    for b in range(blocks):
        rows = slice(b * EDGE, (b + 1) * EDGE)
        keys = slice(b * EDGE, b * EDGE + span)
        key_ids = jnp.concatenate([ids_ext[b + j][0:1] for j in range(3)], axis=1)
        frame_ids = jnp.broadcast_to(ids_ext[b + 1][0:1], (EDGE, EDGE)).T[:, 0:1]
        same = frame_ids == key_ids
        allowed = jnp.concatenate([same, same], axis=0)

        def attend(p, _, rows=rows, keys=keys, allowed=allowed):
            columns = pl.ds(pl.multiple_of(p * 128, 128), 128)
            both = query[rows, columns]
            nothing = jnp.zeros_like(both)
            stacked = jnp.concatenate(
                [jnp.where(low, both, nothing), jnp.where(low, nothing, both)], axis=0
            )
            scores = lax.dot_general(stacked, pairs[keys, columns], NT, preferred_element_type=F32)
            scores = jnp.where(allowed, scores, MASKED)
            highest = jnp.max(scores, axis=-1, keepdims=True)
            exponent = jnp.exp(scores - highest)
            total = jnp.sum(exponent, axis=-1, keepdims=True)
            value_columns = pl.ds(pl.multiple_of(width + p * 128, 128), 128)
            mixed = jnp.dot(
                exponent.astype(BF16), pairs[keys, value_columns], preferred_element_type=F32
            ) / total
            attended[rows, columns] = jnp.where(low, mixed[:EDGE], mixed[EDGE:]).astype(BF16)
            return 0

        lax.fori_loop(0, width // 128, attend, 0, unroll=2)
        if b == 0:
            out_a.relay()

    out_a.end()
    out_b.end()
    tokens = frames // 2
    at_row = lax.broadcasted_iota(jnp.int32, (tokens, frames), 0)
    at_frame = lax.broadcasted_iota(jnp.int32, (tokens, frames), 1)
    first = jnp.where(at_frame == 2 * at_row, 1.0, 0.0).astype(BF16)
    second = jnp.where(at_frame == 2 * at_row + 1, 1.0, 0.0).astype(BF16)

    def encode(i, _):
        columns = pl.ds(pl.multiple_of(i * tile, tile), tile)
        projected = lax.dot_general(attended[...], out_w[columns], NT, preferred_element_type=F32)
        encoded = (audio[:, columns].astype(F32) + projected).astype(BF16)
        pooled[:, columns] = jnp.dot(first, encoded, preferred_element_type=F32).astype(BF16)
        pooled[:, pl.ds(pl.multiple_of(width + i * tile, tile), tile)] = jnp.dot(
            second, encoded, preferred_element_type=F32
        ).astype(BF16)
        return 0

    lax.fori_loop(0, width // tile, encode, 0)
    for copy in table_copies:
        copy.wait()
    for weight in (qkv_a, qkv_b, qkv_c, out_a, out_b):
        weight.drain()

    @pl.when(has_right)
    def _():
        ids_right.wait_send()
        halo_right.wait_send()

    @pl.when(has_left)
    def _():
        ids_left.wait_send()
        halo_left.wait_send()


def routed_kernel(groups, seqs, pooled, moe_gain, tables, adapter_hbm, gate_hbm, up_hbm, down_hbm, result, *scratch):
    adapter_w, gathered, produced, thinker, expert_in, load_sem, near_send, near_recv, back_send, back_recv = scratch[:10]
    g, s = lax.axis_index("grp"), lax.axis_index("seq")
    load = pltpu.make_async_copy(adapter_hbm, adapter_w, load_sem)
    load.start()
    greet(g, s, groups, seqs, True)
    tokens, features = thinker.shape
    columns = adapter_w.shape[1]
    part = tokens // 2
    cut = part // 2
    x, y, far = g + 1 - 2 * lax.rem(g, 2), lax.rem(g + 2, 4), 3 - g

    def send(source, target, send_sem, recv_sem, grp):
        return pltpu.make_async_remote_copy(
            src_ref=source,
            dst_ref=target,
            send_sem=send_sem,
            recv_sem=recv_sem,
            device_id={"grp": grp, "seq": s},
            device_id_type=MESH,
        )

    def pass_on(h, event, source, slot, first, count, grp):
        here = pl.ds(h * part + first, count)
        return send(
            pooled.at[here] if source == 0 else gathered.at[source - 1, here],
            gathered.at[slot - 1, here],
            near_send.at[h, event],
            near_recv.at[h, event],
            grp,
        )

    def give_back(h, k, grp):
        return send(
            produced.at[k, pl.ds(h * part, part)],
            thinker.at[pl.ds(h * part, part), pl.ds(pl.multiple_of(g * columns, 128), columns)],
            back_send.at[h, k],
            back_recv.at[h, k],
            grp,
        )

    def near(h, *events):
        plan = ((0, 1, 0, part, x), (0, 2, 0, part, y), (2, 3, 0, cut, x), (1, 3, cut, part - cut, y))
        return [pass_on(h, event, *plan[event]) for event in events]

    tile = 256 if columns % 256 == 0 else 128

    def spread(h):
        for copy in near(h, 0, 1):
            copy.start()

    def relay(h):
        for copy in near(h, 0, 1):
            copy.wait_recv()
        for copy in near(h, 2, 3):
            copy.start()

    def project(h, slots):
        here = slice(h * part, h * part + part)

        def one(i, _):
            lanes = pl.ds(pl.multiple_of(i * tile, tile), tile)
            batch = [pooled[here] if k == 0 else gathered[k - 1, here] for k in slots]
            found = jnp.dot(
                jnp.concatenate(batch, axis=0), adapter_w[:, lanes], preferred_element_type=F32
            ).astype(BF16)
            for j, k in enumerate(slots):
                value = found[j * part : (j + 1) * part]
                if k == 0:
                    thinker[here, pl.ds(pl.multiple_of(g * columns + i * tile, tile), tile)] = value
                else:
                    produced[k, here, lanes] = value
            return 0

        lax.fori_loop(0, columns // tile, one, 0)
        for k in slots:
            if k:
                give_back(h, k, (g, x, y, far)[k]).start()

    def gather_far(h):
        for copy in near(h, 2, 3):
            copy.wait_recv()

    def normalise(h):
        for k in range(1, 4):
            give_back(h, k, g).wait_recv()

        def rms_rows(i, _):
            rows = pl.ds(pl.multiple_of(h * part + i * 32, 32), 32)
            widened = thinker[rows].astype(F32)
            squares = jnp.mean(widened * widened, axis=-1, keepdims=True)
            expert_in[rows] = (widened * lax.rsqrt(squares + RMS_EPSILON) * moe_gain[...]).astype(BF16)
            return 0

        lax.fori_loop(0, part // 32, rms_rows, 0)

    def finish_sends():
        for h in range(2):
            for copy in near(h, 0, 1, 2, 3):
                copy.wait_send()
            for k in range(1, 4):
                give_back(h, k, (g, x, y, far)[k]).wait_send()

    def prepare():
        spread(0)
        load.wait()
        relay(0)
        spread(1)
        project(0, (0, 1, 2))
        gather_far(0)
        project(0, (3,))
        relay(1)
        project(1, (0, 1, 2))
        normalise(0)
        gather_far(1)
        project(1, (3,))
        normalise(1)

    expert_kernel(
        seqs, expert_in, thinker, tables, gate_hbm, up_hbm, down_hbm, result, *scratch[10:], prepare=prepare
    )
    finish_sends()


def expert_kernel(
    seqs,
    expert_in,
    thinker,
    tables,
    gate_hbm,
    up_hbm,
    down_hbm,
    result,
    gate_w,
    up_w,
    down_w,
    tokens_all,
    hidden,
    mine,
    theirs,
    to_other,
    incoming,
    outgoing,
    load_sem,
    tok_send,
    tok_recv,
    half_send,
    half_recv,
    sum_send,
    sum_recv,
    share_of,
    prepare=None,
):
    g, s = lax.axis_index("grp"), lax.axis_index("seq")
    planes = seqs // 2
    z, c = s // 2, lax.rem(s, 2)
    other = 1 - c
    rows, width = expert_in.shape
    ff = gate_w.shape[1]
    loads = [
        pltpu.make_async_copy(source, target, load_sem.at[i])
        for i, (source, target) in enumerate(((gate_hbm, gate_w), (up_hbm, up_w), (down_hbm, down_w)))
    ]
    for load in loads:
        load.start()
    if prepare is None:
        greet(g, s, 1, seqs, False)
    else:
        prepare()

    part = rows // 2

    def span(h):
        return pl.ds(pl.multiple_of(h * part, part), part)

    def move(source, target, send, recv, plane, core):
        return pltpu.make_async_remote_copy(
            src_ref=source,
            dst_ref=target,
            send_sem=send,
            recv_sem=recv,
            device_id={"grp": g, "seq": plane * 2 + core},
            device_id_type=MESH,
        )

    def token_copy(side, origin, h, plane, own=False):
        slot = tokens_all.at[origin, c, span(h)]
        source = expert_in.at[span(h)] if own else slot
        return move(source, slot, tok_send.at[side, origin, h], tok_recv.at[0, origin, h], plane, c)

    def other_copy(origin, h, own=False):
        slot = tokens_all.at[origin, c, span(h)]
        source = expert_in.at[span(h)] if own else slot
        return move(source, slot, tok_send.at[2, origin, h], tok_recv.at[1, origin, h], z, other)

    def half_copy(origin, h):
        return move(
            to_other.at[origin, span(h)],
            theirs.at[origin, span(h)],
            half_send.at[origin, h],
            half_recv.at[origin, h],
            z,
            other,
        )

    def sum_copy(side, target, h, plane):
        return move(
            outgoing.at[side, target, span(h)],
            incoming.at[side, target, span(h)],
            sum_send.at[side, target, h],
            sum_recv.at[side, target, h],
            plane,
            c,
        )

    has_above, has_below = z < planes - 1, z > 0

    @pl.when(has_above)
    def _():
        token_copy(0, z, 0, z + 1, True).start()

    @pl.when(has_below)
    def _():
        token_copy(1, z, 0, z - 1, True).start()

    other_copy(z, 0, True).start()

    @pl.when(z == 0)
    def _():
        token_copy(0, z, 1, z + 1, True).start()

    @pl.when(z == planes - 1)
    def _():
        token_copy(1, z, 1, z - 1, True).start()

    other_copy(z, 1, True).start()
    tokens_all[z, c] = expert_in[...]
    for load in loads:
        load.wait()
    for k in range(seqs):
        share_of[k] = jnp.broadcast_to(tables[k, pl.ds(s, 1)], (128, rows)).T
    rise_tile = 384 if ff % 384 == 0 else 128
    fall_tile = 512 if width % 512 == 0 else 128

    def experts(origin, h):
        other_copy(origin, h).wait_recv()

        def rise(i, _):
            columns = pl.ds(pl.multiple_of(i * rise_tile, rise_tile), rise_tile)
            batch = tokens_all[origin, :, span(h)].reshape(2 * part, width)
            gate = jnp.dot(batch, gate_w[:, columns], preferred_element_type=F32)
            up = jnp.dot(batch, up_w[:, columns], preferred_element_type=F32)
            hidden[:, columns] = (gate / (1.0 + jnp.exp(-gate)) * up).astype(BF16)
            return 0

        lax.fori_loop(0, ff // rise_tile, rise, 0)
        share = jnp.concatenate([share_of[origin * 2 + k, span(h), 0:1] for k in range(2)], axis=0)

        def fall(i, _):
            columns = pl.ds(pl.multiple_of(i * fall_tile, fall_tile), fall_tile)
            produced = jnp.dot(hidden[...], down_w[:, columns], preferred_element_type=F32)
            weighted = (produced.astype(BF16).astype(F32) * share).astype(BF16)
            mine[origin, span(h), columns] = jnp.where(c == 0, weighted[:part], weighted[part:])
            to_other[origin, span(h), columns] = jnp.where(c == 0, weighted[part:], weighted[:part])
            return 0

        lax.fori_loop(0, width // fall_tile, fall, 0)
        half_copy(origin, h).start()

    def take(side, origin, h):
        token_copy(side, origin, h, z).wait_recv()

        @pl.when(jnp.where(side == 0, has_above, has_below))
        def _():
            token_copy(side, origin, h, z + 1 - 2 * side).start()

        other_copy(origin, h).start()

    def send_sum(side, origin, h, starts):
        half_copy(origin, h).wait_recv()
        total = mine[origin, span(h)].astype(F32) + theirs[origin, span(h)].astype(F32)
        if starts:
            outgoing[side, origin, span(h)] = total.astype(BF16)
        else:
            sum_copy(side, origin, h, z).wait_recv()
            came = incoming[side, origin, span(h)].astype(F32)
            outgoing[side, origin, span(h)] = (total + came).astype(BF16)
        sum_copy(side, origin, h, z + 2 * side - 1).start()

    def arrival(side, t):
        reach = jnp.where(side == 0, z, planes - 1 - z)
        first = t <= reach
        distance = jnp.where(first, t, 2 * reach + 1 - t)
        valid = (t >= 1) & (t <= 2 * reach)
        return z + (2 * side - 1) * distance, jnp.where(first, 0, 1), valid, t == 2 * reach

    ends = (z == planes - 1, z == 0)
    experts(z, 0)

    def slot(t, _):
        for side in range(2):
            origin, h, valid, last = arrival(side, t)

            @pl.when(valid)
            def _(side=side, origin=origin, h=h):
                take(side, origin, h)

            @pl.when(last & (has_above, has_below)[side])
            def _(side=side):
                token_copy(side, z, 1, z + 1 - 2 * side, True).start()

        for side in range(2):
            passed = jnp.where(side == 0, planes - 1 - z, z)
            origin, h, valid, _ = arrival(side, t - 2 * passed - 1)

            @pl.when(valid & jnp.logical_not(ends[side]))
            def _(side=side, origin=origin, h=h):
                send_sum(side, origin, h, False)

        def compute(j, _):
            side = jnp.where(z >= planes // 2, j, 1 - j)
            origin, h, valid, _ = arrival(side, t)
            own = j == 2
            now = t == jnp.where(ends[0] | ends[1], 1, 2 * planes - 3)

            @pl.when(jnp.where(own, now, valid))
            def _():
                experts(jnp.where(own, z, origin), jnp.where(own, 1, h))

            @pl.when(jnp.logical_not(own) & valid & jnp.where(side == 0, ends[0], ends[1]))
            def _():
                send_sum(side, origin, h, True)

            return 0

        lax.fori_loop(0, 3, compute, 0)
        return 0

    lax.fori_loop(1, 2 * planes, slot, 0)

    @pl.when(z == 0)
    def _():
        incoming[1, z] = jnp.zeros((rows, width), BF16)

    @pl.when(z == planes - 1)
    def _():
        incoming[0, z] = jnp.zeros((rows, width), BF16)

    for h in range(2):
        half_copy(z, h).wait_recv()

        @pl.when(has_below)
        def _(h=h):
            sum_copy(1, z, h, z).wait_recv()

        @pl.when(has_above)
        def _(h=h):
            sum_copy(0, z, h, z).wait_recv()

        def finish(i, _, h=h):
            here = pl.ds(pl.multiple_of(h * part + i * 32, 32), 32)
            total = thinker[here].astype(F32) + mine[z, here].astype(F32) + theirs[z, here].astype(F32)
            total = total + incoming[0, z, here].astype(F32) + incoming[1, z, here].astype(F32)
            result[here] = total.astype(BF16)
            return 0

        lax.fori_loop(0, part // 32, finish, 0)

    def drain(origin, _):
        for h in range(2):
            other_copy(origin, h).wait_send()
            half_copy(origin, h).wait_send()

            @pl.when((origin <= z) & has_above)
            def _(h=h):
                token_copy(0, origin, h, z).wait_send()

            @pl.when((origin >= z) & has_below)
            def _(h=h):
                token_copy(1, origin, h, z).wait_send()

            @pl.when(origin > z)
            def _(h=h):
                sum_copy(1, origin, h, z).wait_send()

            @pl.when(origin < z)
            def _(h=h):
                sum_copy(0, origin, h, z).wait_send()

        return 0

    lax.fori_loop(0, planes, drain, 0)


def body(
    groups,
    seqs,
    audio,
    block_ids,
    norm_gain,
    qkv_weight,
    out_weight,
    adapter_weight,
    moe_gain,
    gate_weight,
    up_weight,
    down_weight,
    routes,
    route_weights,
):
    frames, width = audio.shape[1:]
    tokens, features = routes.shape[1], moe_gain.shape[0]
    blocks = frames // EDGE
    vmem = pl.BlockSpec(memory_space=pltpu.VMEM)
    anywhere = pl.BlockSpec(memory_space=pl.ANY)
    dma = pltpu.SemaphoreType.DMA
    events = max(13, groups - 1)
    planes = seqs // 2
    ff = gate_weight.shape[2]
    block = (planes, tokens, features)
    expert_scratch = [
        pltpu.VMEM((features, ff), BF16),
        pltpu.VMEM((features, ff), BF16),
        pltpu.VMEM((ff, features), BF16),
        pltpu.VMEM((planes, 2, tokens, features), BF16),
        pltpu.VMEM((tokens, ff), BF16),
        pltpu.VMEM(block, BF16),
        pltpu.VMEM(block, BF16),
        pltpu.VMEM(block, BF16),
        pltpu.VMEM((2,) + block, BF16),
        pltpu.VMEM((2,) + block, BF16),
        dma((3,)),
        dma((3, planes, 2)),
        dma((2, planes, 2)),
        dma((planes, 2)),
        dma((planes, 2)),
        dma((2, planes, 2)),
        dma((2, planes, 2)),
        pltpu.VMEM((seqs, tokens, 128), F32),
    ]
    expert_weights = (gate_weight[0], up_weight[0], down_weight[0])
    if groups == 4 and seqs % 4 == 0:
        pooled, tables = pl.pallas_call(
            functools.partial(attention_kernel, groups, seqs),
            out_shape=(
                jax.ShapeDtypeStruct((tokens, 2 * width), BF16),
                jax.ShapeDtypeStruct((seqs, seqs, tokens), F32),
            ),
            in_specs=[vmem] * 5 + [anywhere] * 2,
            out_specs=(vmem,) * 2,
            scratch_shapes=[
                pltpu.VMEM((3 * width, width), BF16),
                pltpu.VMEM((width, width), BF16),
                pltpu.VMEM((frames + 2 * EDGE, width), BF16),
                pltpu.VMEM((frames, width), BF16),
                pltpu.VMEM((frames + 2 * EDGE, 2 * width), BF16),
                pltpu.VMEM((2, HALO, width), BF16),
                pltpu.VMEM((blocks + 2, 8, EDGE), jnp.int32),
                pltpu.VMEM((seqs, tokens), F32),
                pltpu.VMEM((frames, width), BF16),
                dma((5,)),
                dma((5, events)),
                dma((5, events)),
                dma((4,)),
                dma((4,)),
                dma((seqs - 1,)),
                dma((seqs - 1,)),
            ],
            compiler_params=pltpu.CompilerParams(
                collective_id=2, has_side_effects=True, vmem_limit_bytes=VMEM_LIMIT
            ),
            name="attention",
        )(audio, block_ids, norm_gain, routes[0].T, route_weights[0].T, qkv_weight.T, out_weight.T)
        result = pl.pallas_call(
            functools.partial(routed_kernel, groups, seqs),
            out_shape=jax.ShapeDtypeStruct((tokens, features), BF16),
            in_specs=[vmem] * 3 + [anywhere] * 4,
            out_specs=vmem,
            scratch_shapes=[
                pltpu.VMEM(adapter_weight.shape, BF16),
                pltpu.VMEM((groups - 1, tokens, 2 * width), BF16),
                pltpu.VMEM((groups, tokens, adapter_weight.shape[1]), BF16),
                pltpu.VMEM((tokens, features), BF16),
                pltpu.VMEM((tokens, features), BF16),
                dma,
                dma((2, 4)),
                dma((2, 4)),
                dma((2, 4)),
                dma((2, 4)),
            ]
            + expert_scratch,
            compiler_params=pltpu.CompilerParams(
                collective_id=3, has_side_effects=True, vmem_limit_bytes=VMEM_LIMIT
            ),
            name="routed",
        )(pooled, moe_gain, tables, adapter_weight, *expert_weights)
        return result[None]
    thinker, expert_in, tables = pl.pallas_call(
        functools.partial(encoder_kernel, groups, seqs),
        out_shape=(
            jax.ShapeDtypeStruct((tokens, features), BF16),
            jax.ShapeDtypeStruct((tokens, features), BF16),
            jax.ShapeDtypeStruct((seqs, seqs, tokens), F32),
        ),
        in_specs=[vmem] * 6 + [anywhere] * 3,
        out_specs=(vmem,) * 3,
        scratch_shapes=[
            pltpu.VMEM((3 * width, width), BF16),
            pltpu.VMEM((width, width), BF16),
            pltpu.VMEM((2 * width, features), BF16),
            pltpu.VMEM((frames, width), BF16),
            pltpu.VMEM((frames, width), BF16),
            pltpu.VMEM((frames + 2 * EDGE, 2 * width), BF16),
            pltpu.VMEM((blocks + 2, 8, EDGE), jnp.int32),
            pltpu.VMEM((seqs, tokens), F32),
            pltpu.VMEM((frames, width), BF16),
            pltpu.VMEM((frames // 2, width), BF16),
            pltpu.VMEM((frames // 2, width), BF16),
            dma((5,)),
            dma((5, events)),
            dma((5, events)),
            dma((4,)),
            dma((4,)),
            dma((seqs - 1,)),
            dma((seqs - 1,)),
        ],
        compiler_params=pltpu.CompilerParams(
            collective_id=0, has_side_effects=True, vmem_limit_bytes=VMEM_LIMIT
        ),
        name="encoder",
    )(
        audio,
        block_ids,
        norm_gain,
        moe_gain,
        routes[0].T,
        route_weights[0].T,
        qkv_weight.T,
        out_weight.T,
        adapter_weight,
    )
    result = pl.pallas_call(
        functools.partial(expert_kernel, seqs),
        out_shape=jax.ShapeDtypeStruct((tokens, features), BF16),
        in_specs=[vmem] * 3 + [anywhere] * 3,
        out_specs=vmem,
        scratch_shapes=expert_scratch,
        compiler_params=pltpu.CompilerParams(
            collective_id=1, has_side_effects=True, vmem_limit_bytes=VMEM_LIMIT
        ),
        name="experts",
    )(expert_in, thinker, tables, *expert_weights)
    return result[None]


def solution(mesh):
    placed = (
        P("grp", "seq", None),
        P("grp", "seq"),
        P(),
        P(None, "grp"),
        P(None, "grp"),
        P(None, "grp"),
        P(),
        P("seq", None, None),
        P("seq", None, None),
        P("seq", None, None),
        P("grp", "seq", None),
        P("grp", "seq", None),
    )
    return jax.shard_map(
        functools.partial(body, mesh.shape["grp"], mesh.shape["seq"]),
        mesh=mesh,
        in_specs=placed,
        out_specs=P("grp", "seq", None),
        check_vma=False,
    )
```

```python
import functools

import jax
import jax.numpy as jnp
from jax import lax
from jax.experimental import pallas as pl
from jax.experimental.pallas import tpu as pltpu
from jax.sharding import PartitionSpec as P

HEAD = 64
EDGE = 128
HALO = 112
DEEP_SHARES = (0.75, 0.75, 0.625, 0.625, 0.5)
STRIPES = len(DEEP_SHARES)
LN_EPSILON = 1e-05
RMS_EPSILON = 1e-06
MASKED = -1e30
VMEM_LIMIT = 66_000_000
MESH = pl.DeviceIdType.MESH
BF16 = jnp.bfloat16
F32 = jnp.float32
NT = (((1,), (1,)), ((), ()))


def greet(g, s, groups, seqs, across):
    barrier = pltpu.get_barrier_semaphore()
    if across:
        for k in range(1, groups):
            pl.semaphore_signal(
                barrier, inc=1, device_id={"grp": lax.rem(g + k, groups), "seq": s}, device_id_type=MESH
            )
    for k in range(1, seqs):
        pl.semaphore_signal(
            barrier, inc=1, device_id={"grp": g, "seq": lax.rem(s + k, seqs)}, device_id_type=MESH
        )
    pl.semaphore_wait(barrier, seqs - 1 + (groups - 1 if across else 0))


def fill_table(routes, route_weights, table):
    experts = lax.broadcasted_iota(jnp.int32, table.shape, 0)
    given = route_weights[...]
    shares = given / jnp.sum(given, axis=0, keepdims=True)
    chosen = routes[...]
    table[...] = sum(
        jnp.where(experts == chosen[k : k + 1], shares[k : k + 1], 0.0) for k in range(chosen.shape[0])
    )


class Gather:
    def __init__(self, g, s, groups, seqs, shard, whole, rows, by_lanes, deep, own_sem, send_sem, recv_sem):
        self.g, self.s, self.groups = g, s, groups
        self.shard, self.whole, self.by_lanes = shard, whole, by_lanes
        self.own_sem, self.send_sem, self.recv_sem = own_sem, send_sem, recv_sem
        self.first, self.rows = rows
        self.routed = groups == 4
        self.deep = deep and self.routed and seqs % 4 == 0
        core, plane = lax.rem(s, 2), lax.rem(s // 2, 2)
        self.other = s + 1 - 2 * core
        self.paired = s + 2 - 4 * plane
        if self.deep:
            self.size = self.rows // 4
            self.start = self.first + (plane * 2 + core) * self.size
            self.paired_start = self.first + ((1 - plane) * 2 + core) * self.size
        else:
            self.size = self.rows // 2
            self.start = self.first + core * self.size
        self.cut = (self.size // 2 + 15) // 16 * 16
        self.copies = {}

    def part(self, group, first, count):
        if self.by_lanes:
            columns = self.shard.shape[1]
            start = pl.multiple_of(group * columns, 128)
            return self.whole.at[pl.ds(pl.multiple_of(first, 16), count), pl.ds(start, columns)]
        return self.whole.at[pl.ds(pl.multiple_of(group * self.shard.shape[0] + first, 16), count)]

    def source(self, first, count):
        return self.shard.at[pl.ds(pl.multiple_of(first, 16), count)]

    def send(self, event, source, target, grp, seq):
        copy = pltpu.make_async_remote_copy(
            src_ref=source,
            dst_ref=target,
            send_sem=self.send_sem.at[event],
            recv_sem=self.recv_sem.at[event],
            device_id={"grp": grp, "seq": seq},
            device_id_type=MESH,
        )
        copy.start()
        self.copies[event] = copy

    def pass_on(self, event, part, grp, seq):
        self.send(event, part, part, grp, seq)

    def got(self, *events):
        for event in events:
            self.copies[event].wait_recv()

    def xor(self, k):
        if k == 1:
            return self.g + 1 - 2 * lax.rem(self.g, 2)
        if k == 2:
            return lax.rem(self.g + 2, 4)
        return 3 - self.g

    def begin(self):
        if self.routed:
            for event, k in ((0, 1), (1, 2)):
                self.send(
                    event,
                    self.source(self.start, self.size),
                    self.part(self.g, self.start, self.size),
                    self.xor(k),
                    self.s,
                )
        else:
            for k in range(1, self.groups):
                self.send(
                    k - 1,
                    self.source(self.first, self.rows),
                    self.part(self.g, self.first, self.rows),
                    lax.rem(self.g + k, self.groups),
                    self.s,
                )
        self.own = pltpu.make_async_copy(
            self.source(self.first, self.rows), self.part(self.g, self.first, self.rows), self.own_sem
        )
        self.own.start()

    def forward(self):
        if not self.routed:
            return
        x, y = self.xor(1), self.xor(2)
        self.got(0, 1)
        self.pass_on(2, self.part(y, self.start, self.cut), x, self.s)
        self.pass_on(3, self.part(x, self.start + self.cut, self.size - self.cut), y, self.s)
        for event, k in ((0, x), (1, y)):
            near = self.part(k, self.start, self.size)
            if self.deep:
                self.pass_on(7 + event, near, self.g, self.paired)
            self.pass_on(4 + event, near, self.g, self.other)

    def share(self):
        if not self.routed:
            return
        self.got(2, 3)
        far = self.part(self.xor(3), self.start, self.size)
        if self.deep:
            self.pass_on(9, far, self.g, self.paired)
        self.pass_on(6, far, self.g, self.other)

    def relay(self):
        if not self.deep:
            return
        for event, k in ((0, 1), (1, 2), (2, 3)):
            self.got(7 + event)
            self.pass_on(10 + event, self.part(self.xor(k), self.paired_start, self.size), self.g, self.other)

    def end(self):
        self.own.wait()
        if self.deep:
            self.got(4, 5, 6, 10, 11, 12)
        elif self.routed:
            self.got(4, 5, 6)
        else:
            self.got(*range(self.groups - 1))

    def drain(self):
        for copy in self.copies.values():
            copy.wait_send()


def encoder_kernel(
    groups,
    seqs,
    audio_block,
    ids,
    gain,
    moe_gain,
    routes,
    route_weights,
    qkv_shard,
    out_shard,
    adapter_shard,
    thinker,
    expert_in,
    tables,
    qkv_w,
    out_w,
    adapter_w,
    normed,
    query,
    pairs,
    ids_ext,
    table,
    attended,
    even,
    odd,
    own_sem,
    weight_send,
    weight_recv,
    edge_send,
    edge_recv,
    tab_send,
    tab_recv,
):
    g, s = lax.axis_index("grp"), lax.axis_index("seq")
    audio = audio_block.at[0]
    frames, width = audio.shape
    heads_pairs = width // 128
    blocks = frames // EDGE
    fill_table(routes, route_weights, table)
    for b in range(blocks):
        ids_ext[b + 1] = jnp.broadcast_to(ids[0:1, b * EDGE : (b + 1) * EDGE], (8, EDGE))
    greet(g, s, groups, seqs, True)

    def gather(i, shard, whole, rows, by_lanes, deep):
        return Gather(
            g, s, groups, seqs, shard, whole, rows, by_lanes, deep, own_sem.at[i], weight_send.at[i], weight_recv.at[i]
        )

    def split(rows, at):
        return (0, at), (at, rows - at)

    qkv_rows, ad_rows = qkv_shard.shape[0], adapter_shard.shape[0]
    qkv_deep, qkv_plain = split(qkv_rows, (qkv_rows // 2 + 63) // 64 * 64)
    ad_deep, ad_plain = split(ad_rows, ad_rows // 2)
    qkv_a = gather(0, qkv_shard, qkv_w, qkv_deep, False, True)
    qkv_b = gather(1, qkv_shard, qkv_w, qkv_plain, False, False)
    out = gather(2, out_shard, out_w, (0, out_shard.shape[0]), False, False)
    ad_a = gather(3, adapter_shard, adapter_w, ad_deep, True, True)
    ad_b = gather(4, adapter_shard, adapter_w, ad_plain, True, False)
    qkv_a.begin()
    qkv_b.begin()

    table_copies = []
    for k in range(1, seqs):
        copy = pltpu.make_async_remote_copy(
            src_ref=table,
            dst_ref=tables.at[s],
            send_sem=tab_send.at[k - 1],
            recv_sem=tab_recv.at[k - 1],
            device_id={"grp": g, "seq": lax.rem(s + k, seqs)},
            device_id_type=MESH,
        )
        copy.start()
        table_copies.append(copy)
    tables[s] = table[...]

    def edge(event, source, target, step):
        return pltpu.make_async_remote_copy(
            src_ref=source,
            dst_ref=target,
            send_sem=edge_send.at[event],
            recv_sem=edge_recv.at[event],
            device_id={"grp": g, "seq": lax.rem(s + step + seqs, seqs)},
            device_id_type=MESH,
        )

    ids_right = edge(0, ids_ext.at[blocks], ids_ext.at[0], 1)
    ids_left = edge(1, ids_ext.at[1], ids_ext.at[blocks + 1], -1)
    pairs_right = edge(2, pairs.at[pl.ds(frames, EDGE)], pairs.at[pl.ds(0, EDGE)], 1)
    pairs_left = edge(3, pairs.at[pl.ds(EDGE, EDGE)], pairs.at[pl.ds(frames + EDGE, EDGE)], -1)
    has_left, has_right = s > 0, s < seqs - 1

    @pl.when(has_right)
    def _():
        ids_right.start()

    @pl.when(has_left)
    def _():
        ids_left.start()

    @pl.when(s == 0)
    def _():
        ids_ext[0] = jnp.full(ids_ext.shape[1:], -1, jnp.int32)
        pairs[0:EDGE] = jnp.zeros((EDGE, pairs.shape[1]), BF16)

    @pl.when(s == seqs - 1)
    def _():
        ids_ext[blocks + 1] = jnp.full(ids_ext.shape[1:], -1, jnp.int32)
        pairs[frames + EDGE :] = jnp.zeros((EDGE, pairs.shape[1]), BF16)

    def norm_rows(i, _):
        rows = pl.ds(pl.multiple_of(i * 64, 64), 64)
        signal = audio[rows].astype(F32)
        centred = signal - jnp.mean(signal, axis=-1, keepdims=True)
        variance = jnp.mean(centred * centred, axis=-1, keepdims=True)
        normed[rows] = (centred * lax.rsqrt(variance + LN_EPSILON) * gain[...]).astype(BF16)
        return 0

    lax.fori_loop(0, frames // 64, norm_rows, 0)

    qkv_a.forward()
    qkv_b.forward()
    out.begin()
    ad_a.begin()
    qkv_a.share()
    qkv_b.share()
    qkv_a.relay()
    qkv_a.end()
    qkv_b.end()

    tile = 256

    def project_pairs(i, _):
        source = pl.ds(pl.multiple_of(width + i * tile, tile), tile)
        columns = pl.ds(pl.multiple_of(i * tile, tile), tile)
        pairs[EDGE : EDGE + frames, columns] = lax.dot_general(
            normed[...], qkv_w[source], NT, preferred_element_type=F32
        ).astype(BF16)
        return 0

    lax.fori_loop(0, 2 * width // tile, project_pairs, 0)

    @pl.when(has_right)
    def _():
        pairs_right.start()

    @pl.when(has_left)
    def _():
        pairs_left.start()

    out.forward()
    ad_b.begin()

    def project_query(i, _):
        columns = pl.ds(pl.multiple_of(i * tile, tile), tile)
        query[:, columns] = lax.dot_general(
            normed[...], qkv_w[columns], NT, preferred_element_type=F32
        ).astype(BF16)
        return 0

    lax.fori_loop(0, width // tile, project_query, 0)
    out.share()
    ad_a.forward()

    @pl.when(has_left)
    def _():
        ids_right.wait_recv()
        pairs_right.wait_recv()

    @pl.when(has_right)
    def _():
        ids_left.wait_recv()
        pairs_left.wait_recv()

    low = lax.broadcasted_iota(jnp.int32, (EDGE, 128), 1) < HEAD
    span = 3 * EDGE
    for b in range(blocks):
        rows = slice(b * EDGE, (b + 1) * EDGE)
        keys = slice(b * EDGE, b * EDGE + span)
        key_ids = jnp.concatenate([ids_ext[b + j][0:1] for j in range(3)], axis=1)
        frame_ids = jnp.broadcast_to(ids_ext[b + 1][0:1], (EDGE, EDGE)).T[:, 0:1]
        same = frame_ids == key_ids
        allowed = jnp.concatenate([same, same], axis=0)

        def attend(p, _, rows=rows, keys=keys, allowed=allowed):
            columns = pl.ds(pl.multiple_of(p * 128, 128), 128)
            both = query[rows, columns]
            nothing = jnp.zeros_like(both)
            stacked = jnp.concatenate(
                [jnp.where(low, both, nothing), jnp.where(low, nothing, both)], axis=0
            )
            scores = lax.dot_general(
                stacked, pairs[keys, columns], NT, preferred_element_type=F32
            ) * HEAD ** (-0.5)
            scores = jnp.where(allowed, scores, MASKED)
            highest = jnp.max(scores, axis=-1, keepdims=True)
            exponent = jnp.exp(scores - highest)
            total = jnp.sum(exponent, axis=-1, keepdims=True)
            value_columns = pl.ds(pl.multiple_of(width + p * 128, 128), 128)
            mixed = jnp.dot(
                (exponent / total).astype(BF16), pairs[keys, value_columns], preferred_element_type=F32
            )
            attended[rows, columns] = jnp.where(low, mixed[:EDGE], mixed[EDGE:]).astype(BF16)
            return 0

        lax.fori_loop(0, heads_pairs, attend, 0)

    out.end()
    tokens = frames // 2
    at_row = lax.broadcasted_iota(jnp.int32, (tokens, frames), 0)
    at_frame = lax.broadcasted_iota(jnp.int32, (tokens, frames), 1)
    first = jnp.where(at_frame == 2 * at_row, 1.0, 0.0).astype(BF16)
    second = jnp.where(at_frame == 2 * at_row + 1, 1.0, 0.0).astype(BF16)

    def encode(i, _):
        columns = pl.ds(pl.multiple_of(i * tile, tile), tile)
        projected = lax.dot_general(attended[...], out_w[columns], NT, preferred_element_type=F32)
        encoded = (audio[:, columns].astype(F32) + projected).astype(BF16)
        even[:, columns] = jnp.dot(first, encoded, preferred_element_type=F32).astype(BF16)
        odd[:, columns] = jnp.dot(second, encoded, preferred_element_type=F32).astype(BF16)
        return 0

    lax.fori_loop(0, width // tile, encode, 0)
    ad_b.forward()
    ad_a.share()
    ad_a.relay()
    ad_b.share()
    ad_a.end()
    ad_b.end()

    def adapt(i, _):
        columns = pl.ds(pl.multiple_of(i * tile, tile), tile)
        thinker[:, columns] = (
            jnp.dot(even[...], adapter_w[0:width, columns], preferred_element_type=F32)
            + jnp.dot(odd[...], adapter_w[width:, columns], preferred_element_type=F32)
        ).astype(BF16)
        return 0

    lax.fori_loop(0, thinker.shape[1] // tile, adapt, 0)

    def rms_rows(i, _):
        rows = pl.ds(pl.multiple_of(i * 32, 32), 32)
        widened = thinker[rows].astype(F32)
        squares = jnp.mean(widened * widened, axis=-1, keepdims=True)
        expert_in[rows] = (widened * lax.rsqrt(squares + RMS_EPSILON) * moe_gain[...]).astype(BF16)
        return 0

    lax.fori_loop(0, tokens // 32, rms_rows, 0)

    for copy in table_copies:
        copy.wait()
    for weight in (qkv_a, qkv_b, out, ad_a, ad_b):
        weight.drain()

    @pl.when(has_right)
    def _():
        ids_right.wait_send()
        pairs_right.wait_send()

    @pl.when(has_left)
    def _():
        ids_left.wait_send()
        pairs_left.wait_send()


def fused_kernel(
    groups,
    seqs,
    audio_block,
    ids,
    gain,
    moe_gain,
    routes,
    route_weights,
    qkv_shard,
    out_shard,
    adapter_shard,
    gate_hbm,
    up_hbm,
    down_hbm,
    result,
    thinker,
    expert_in,
    tables,
    *scratch,
):
    def prepare():
        encode_tokens(
            groups,
            seqs,
            audio_block,
            ids,
            gain,
            moe_gain,
            routes,
            route_weights,
            qkv_shard,
            out_shard,
            adapter_shard,
            thinker,
            expert_in,
            tables,
            *scratch[:19],
        )

    expert_kernel(
        seqs, expert_in, thinker, tables, gate_hbm, up_hbm, down_hbm, result, *scratch[19:], prepare=prepare
    )


def encode_tokens(
    groups,
    seqs,
    audio_block,
    ids,
    gain,
    moe_gain,
    routes,
    route_weights,
    qkv_shard,
    out_shard,
    adapter_shard,
    thinker,
    expert_in,
    tables,
    qkv_w,
    out_w,
    adapter_w,
    normed,
    query,
    pairs,
    halo,
    ids_ext,
    table,
    attended,
    pooled,
    summed,
    own_sem,
    weight_send,
    weight_recv,
    edge_send,
    edge_recv,
    tab_send,
    tab_recv,
):
    g, s = lax.axis_index("grp"), lax.axis_index("seq")
    audio = audio_block.at[0]
    frames, width = audio.shape
    blocks = frames // EDGE
    fill_table(routes, route_weights, table)
    for b in range(blocks):
        ids_ext[b + 1] = jnp.broadcast_to(ids[0:1, b * EDGE : (b + 1) * EDGE], (8, EDGE))
    greet(g, s, groups, seqs, True)

    def gather(i, shard, whole, first, rows, deep, by_lanes=False):
        return Gather(
            g, s, groups, seqs, shard, whole, (first, rows), by_lanes, deep,
            own_sem.at[i], weight_send.at[i], weight_recv.at[i],
        )

    def part(rows, share):
        return int(rows * share + 32) // 64 * 64

    qkv_rows, out_rows = qkv_shard.shape[0], out_shard.shape[0]
    one, two, deep_out = part(qkv_rows, 0.333), part(qkv_rows, 0.6), part(out_rows, 0.6)
    qkv_a = gather(0, qkv_shard, qkv_w, 0, one, True)
    qkv_b = gather(1, qkv_shard, qkv_w, one, two - one, True)
    qkv_c = gather(2, qkv_shard, qkv_w, two, qkv_rows - two, False)
    out_a = gather(3, out_shard, out_w, 0, deep_out, True)
    out_b = gather(4, out_shard, out_w, deep_out, out_rows - deep_out, False)
    ad_rows = adapter_shard.shape[0]
    stripe = ad_rows // STRIPES
    stripes = []
    for k, share in enumerate(DEEP_SHARES):
        first, deep = k * stripe, part(stripe, share)
        stripes.append(
            (
                gather(5 + 2 * k, adapter_shard, adapter_w, first, deep, True, True),
                gather(6 + 2 * k, adapter_shard, adapter_w, first + deep, stripe - deep, False, True),
            )
        )

    def begin(k):
        for one in stripes[k]:
            one.begin()

    def forward(k):
        for one in stripes[k]:
            one.forward()

    def share(k):
        for one in stripes[k]:
            one.share()

    def relay(k):
        for one in stripes[k]:
            one.relay()

    def end(k):
        for one in stripes[k]:
            one.end()

    qkv_a.begin()

    def edge(event, source, target, step):
        return pltpu.make_async_remote_copy(
            src_ref=source,
            dst_ref=target,
            send_sem=edge_send.at[event],
            recv_sem=edge_recv.at[event],
            device_id={"grp": g, "seq": lax.rem(s + step + seqs, seqs)},
            device_id_type=MESH,
        )

    ids_right = edge(0, ids_ext.at[blocks], ids_ext.at[0], 1)
    ids_left = edge(1, ids_ext.at[1], ids_ext.at[blocks + 1], -1)
    halo_right = edge(2, audio.at[pl.ds(frames - HALO, HALO)], halo.at[0], 1)
    halo_left = edge(3, audio.at[pl.ds(0, HALO)], halo.at[1], -1)
    has_left, has_right = s > 0, s < seqs - 1

    @pl.when(has_right)
    def _():
        ids_right.start()
        halo_right.start()

    @pl.when(has_left)
    def _():
        ids_left.start()
        halo_left.start()

    qkv_b.begin()
    qkv_c.begin()
    table_copies = []
    for k in range(1, seqs):
        copy = pltpu.make_async_remote_copy(
            src_ref=table,
            dst_ref=tables.at[s],
            send_sem=tab_send.at[k - 1],
            recv_sem=tab_recv.at[k - 1],
            device_id={"grp": g, "seq": lax.rem(s + k, seqs)},
            device_id_type=MESH,
        )
        copy.start()
        table_copies.append(copy)
    tables[s] = table[...]

    @pl.when(s == 0)
    def _():
        ids_ext[0] = jnp.full(ids_ext.shape[1:], -1, jnp.int32)
        halo[0] = jnp.zeros(halo.shape[1:], BF16)

    @pl.when(s == seqs - 1)
    def _():
        ids_ext[blocks + 1] = jnp.full(ids_ext.shape[1:], -1, jnp.int32)
        halo[1] = jnp.zeros(halo.shape[1:], BF16)

    def layer_norm(signal):
        signal = signal.astype(F32)
        centred = signal - jnp.mean(signal, axis=-1, keepdims=True)
        variance = jnp.mean(centred * centred, axis=-1, keepdims=True)
        return (centred * lax.rsqrt(variance + LN_EPSILON) * gain[...]).astype(BF16)

    def norm_rows(i, _):
        rows = pl.multiple_of(i * 64, 64)
        normed[pl.ds(EDGE + rows, 64)] = layer_norm(audio[pl.ds(rows, 64)])
        return 0

    lax.fori_loop(0, frames // 64, norm_rows, 0)
    spare = jnp.zeros((EDGE - HALO, width), BF16)
    normed[0 : EDGE - HALO] = spare
    normed[frames + EDGE + HALO :] = spare
    qkv_a.forward()

    @pl.when(has_left)
    def _():
        ids_right.wait_recv()
        halo_right.wait_recv()

    @pl.when(has_right)
    def _():
        ids_left.wait_recv()
        halo_left.wait_recv()

    def norm_halo(i, _):
        rows = pl.multiple_of(i * 16, 16)
        normed[pl.ds(EDGE - HALO + rows, 16)] = layer_norm(halo[0, pl.ds(rows, 16)])
        normed[pl.ds(EDGE + frames + rows, 16)] = layer_norm(halo[1, pl.ds(rows, 16)])
        return 0

    lax.fori_loop(0, HALO // 16, norm_halo, 0)
    qkv_b.forward()
    qkv_c.forward()
    out_a.begin()
    out_b.begin()
    qkv_a.share()
    qkv_b.share()
    begin(0)
    qkv_a.relay()
    qkv_c.share()
    qkv_b.relay()
    qkv_a.end()
    qkv_b.end()
    qkv_c.end()
    tile = 256

    def project_pairs(i, _):
        source = pl.ds(pl.multiple_of(width + i * tile, tile), tile)
        columns = pl.ds(pl.multiple_of(i * tile, tile), tile)
        pairs[:, columns] = lax.dot_general(
            normed[...], qkv_w[source], NT, preferred_element_type=F32
        ).astype(BF16)
        return 0

    lax.fori_loop(0, 2 * width // tile, project_pairs, 0)
    out_a.forward()
    out_b.forward()
    begin(1)

    def project_query(i, _):
        columns = pl.ds(pl.multiple_of(i * tile, tile), tile)
        query[:, columns] = lax.dot_general(
            normed[EDGE : EDGE + frames], qkv_w[columns], NT, preferred_element_type=F32
        ).astype(BF16) * BF16(HEAD ** (-0.5))
        return 0

    lax.fori_loop(0, width // tile, project_query, 0)
    forward(0)
    begin(2)
    low = lax.broadcasted_iota(jnp.int32, (EDGE, 128), 1) < HEAD
    span = 3 * EDGE
    for b in range(blocks):
        rows = slice(b * EDGE, (b + 1) * EDGE)
        keys = slice(b * EDGE, b * EDGE + span)
        key_ids = jnp.concatenate([ids_ext[b + j][0:1] for j in range(3)], axis=1)
        frame_ids = jnp.broadcast_to(ids_ext[b + 1][0:1], (EDGE, EDGE)).T[:, 0:1]
        same = frame_ids == key_ids
        allowed = jnp.concatenate([same, same], axis=0)

        def attend(p, _, rows=rows, keys=keys, allowed=allowed):
            columns = pl.ds(pl.multiple_of(p * 128, 128), 128)
            both = query[rows, columns]
            nothing = jnp.zeros_like(both)
            stacked = jnp.concatenate(
                [jnp.where(low, both, nothing), jnp.where(low, nothing, both)], axis=0
            )
            scores = lax.dot_general(stacked, pairs[keys, columns], NT, preferred_element_type=F32)
            scores = jnp.where(allowed, scores, MASKED)
            highest = jnp.max(scores, axis=-1, keepdims=True)
            exponent = jnp.exp(scores - highest)
            total = jnp.sum(exponent, axis=-1, keepdims=True)
            value_columns = pl.ds(pl.multiple_of(width + p * 128, 128), 128)
            mixed = jnp.dot(
                exponent.astype(BF16), pairs[keys, value_columns], preferred_element_type=F32
            ) / total
            attended[rows, columns] = jnp.where(low, mixed[:EDGE], mixed[EDGE:]).astype(BF16)
            return 0

        middle = width // 256
        lax.fori_loop(0, middle, attend, 0)
        if b == 0:
            out_a.share()
            out_b.share()
        else:
            out_a.relay()
            forward(2)
            begin(4)
            share(1)
        lax.fori_loop(middle, width // 128, attend, 0)
        if b == 0:
            forward(1)
            begin(3)
            share(0)

    out_a.end()
    out_b.end()
    relay(0)
    forward(3)
    share(2)
    tokens = frames // 2
    at_row = lax.broadcasted_iota(jnp.int32, (tokens, frames), 0)
    at_frame = lax.broadcasted_iota(jnp.int32, (tokens, frames), 1)
    first = jnp.where(at_frame == 2 * at_row, 1.0, 0.0).astype(BF16)
    second = jnp.where(at_frame == 2 * at_row + 1, 1.0, 0.0).astype(BF16)

    def encode(i, _):
        columns = pl.ds(pl.multiple_of(i * tile, tile), tile)
        projected = lax.dot_general(attended[...], out_w[columns], NT, preferred_element_type=F32)
        encoded = (audio[:, columns].astype(F32) + projected).astype(BF16)
        pooled[:, columns] = jnp.dot(first, encoded, preferred_element_type=F32).astype(BF16)
        pooled[:, pl.ds(pl.multiple_of(width + i * tile, tile), tile)] = jnp.dot(
            second, encoded, preferred_element_type=F32
        ).astype(BF16)
        return 0

    lax.fori_loop(0, width // tile, encode, 0)

    def adapt(k):
        here = slice(k * stripe, (k + 1) * stripe)

        def one(i, _):
            columns = pl.ds(pl.multiple_of(i * tile, tile), tile)
            found = jnp.dot(pooled[:, here], adapter_w[here, columns], preferred_element_type=F32)
            if k:
                found = found + summed[:, columns]
            if k < STRIPES - 1:
                summed[:, columns] = found
            else:
                thinker[:, columns] = found.astype(BF16)
            return 0

        lax.fori_loop(0, thinker.shape[1] // tile, one, 0)

    relay(1)
    forward(4)
    share(3)
    end(0)
    adapt(0)
    relay(2)
    end(1)
    adapt(1)
    share(4)
    relay(3)
    end(2)
    adapt(2)
    relay(4)
    end(3)
    adapt(3)
    end(4)
    adapt(4)

    def rms_rows(i, _):
        rows = pl.ds(pl.multiple_of(i * 32, 32), 32)
        widened = thinker[rows].astype(F32)
        squares = jnp.mean(widened * widened, axis=-1, keepdims=True)
        expert_in[rows] = (widened * lax.rsqrt(squares + RMS_EPSILON) * moe_gain[...]).astype(BF16)
        return 0

    lax.fori_loop(0, tokens // 32, rms_rows, 0)
    for copy in table_copies:
        copy.wait()
    for weight in (qkv_a, qkv_b, qkv_c, out_a, out_b, *sum(stripes, ())):
        weight.drain()

    @pl.when(has_right)
    def _():
        ids_right.wait_send()
        halo_right.wait_send()

    @pl.when(has_left)
    def _():
        ids_left.wait_send()
        halo_left.wait_send()


def expert_kernel(
    seqs,
    expert_in,
    thinker,
    tables,
    gate_hbm,
    up_hbm,
    down_hbm,
    result,
    gate_w,
    up_w,
    down_w,
    tokens_all,
    hidden,
    mine,
    theirs,
    to_other,
    incoming,
    outgoing,
    load_sem,
    tok_send,
    tok_recv,
    half_send,
    half_recv,
    sum_send,
    sum_recv,
    share_of,
    prepare=None,
):
    g, s = lax.axis_index("grp"), lax.axis_index("seq")
    planes = seqs // 2
    z, c = s // 2, lax.rem(s, 2)
    other = 1 - c
    rows, width = expert_in.shape
    ff = gate_w.shape[1]
    loads = [
        pltpu.make_async_copy(source, target, load_sem.at[i])
        for i, (source, target) in enumerate(((gate_hbm, gate_w), (up_hbm, up_w), (down_hbm, down_w)))
    ]
    for load in loads:
        load.start()
    if prepare is None:
        greet(g, s, 1, seqs, False)
    else:
        prepare()

    part = rows // 2

    def span(h):
        return pl.ds(pl.multiple_of(h * part, part), part)

    def move(source, target, send, recv, plane, core):
        return pltpu.make_async_remote_copy(
            src_ref=source,
            dst_ref=target,
            send_sem=send,
            recv_sem=recv,
            device_id={"grp": g, "seq": plane * 2 + core},
            device_id_type=MESH,
        )

    def token_copy(side, origin, h, plane, own=False):
        slot = tokens_all.at[origin, c, span(h)]
        source = expert_in.at[span(h)] if own else slot
        return move(source, slot, tok_send.at[side, origin, h], tok_recv.at[0, origin, h], plane, c)

    def other_copy(origin, h, own=False):
        slot = tokens_all.at[origin, c, span(h)]
        source = expert_in.at[span(h)] if own else slot
        return move(source, slot, tok_send.at[2, origin, h], tok_recv.at[1, origin, h], z, other)

    def half_copy(origin, h):
        return move(
            to_other.at[origin, span(h)],
            theirs.at[origin, span(h)],
            half_send.at[origin, h],
            half_recv.at[origin, h],
            z,
            other,
        )

    def sum_copy(side, target, h, plane):
        return move(
            outgoing.at[side, target, span(h)],
            incoming.at[side, target, span(h)],
            sum_send.at[side, target, h],
            sum_recv.at[side, target, h],
            plane,
            c,
        )

    has_above, has_below = z < planes - 1, z > 0

    @pl.when(has_above)
    def _():
        token_copy(0, z, 0, z + 1, True).start()

    @pl.when(has_below)
    def _():
        token_copy(1, z, 0, z - 1, True).start()

    other_copy(z, 0, True).start()

    @pl.when(z == 0)
    def _():
        token_copy(0, z, 1, z + 1, True).start()

    @pl.when(z == planes - 1)
    def _():
        token_copy(1, z, 1, z - 1, True).start()

    other_copy(z, 1, True).start()
    tokens_all[z, c] = expert_in[...]
    for load in loads:
        load.wait()
    for k in range(seqs):
        share_of[k] = jnp.broadcast_to(tables[k, pl.ds(s, 1)], (128, rows)).T
    rise_tile = 384 if ff % 384 == 0 else 128
    fall_tile = 512 if width % 512 == 0 else 128

    def experts(origin, h):
        other_copy(origin, h).wait_recv()

        def rise(i, _):
            columns = pl.ds(pl.multiple_of(i * rise_tile, rise_tile), rise_tile)
            batch = tokens_all[origin, :, span(h)].reshape(2 * part, width)
            gate = jnp.dot(batch, gate_w[:, columns], preferred_element_type=F32)
            up = jnp.dot(batch, up_w[:, columns], preferred_element_type=F32)
            hidden[:, columns] = (gate / (1.0 + jnp.exp(-gate)) * up).astype(BF16)
            return 0

        lax.fori_loop(0, ff // rise_tile, rise, 0)
        share = jnp.concatenate([share_of[origin * 2 + k, span(h), 0:1] for k in range(2)], axis=0)

        def fall(i, _):
            columns = pl.ds(pl.multiple_of(i * fall_tile, fall_tile), fall_tile)
            produced = jnp.dot(hidden[...], down_w[:, columns], preferred_element_type=F32)
            weighted = (produced.astype(BF16).astype(F32) * share).astype(BF16)
            mine[origin, span(h), columns] = jnp.where(c == 0, weighted[:part], weighted[part:])
            to_other[origin, span(h), columns] = jnp.where(c == 0, weighted[part:], weighted[:part])
            return 0

        lax.fori_loop(0, width // fall_tile, fall, 0)
        half_copy(origin, h).start()

    def take(side, origin, h):
        token_copy(side, origin, h, z).wait_recv()

        @pl.when(jnp.where(side == 0, has_above, has_below))
        def _():
            token_copy(side, origin, h, z + 1 - 2 * side).start()

        other_copy(origin, h).start()

    def send_sum(side, origin, h, starts):
        half_copy(origin, h).wait_recv()
        total = mine[origin, span(h)].astype(F32) + theirs[origin, span(h)].astype(F32)
        if starts:
            outgoing[side, origin, span(h)] = total.astype(BF16)
        else:
            sum_copy(side, origin, h, z).wait_recv()
            came = incoming[side, origin, span(h)].astype(F32)
            outgoing[side, origin, span(h)] = (total + came).astype(BF16)
        sum_copy(side, origin, h, z + 2 * side - 1).start()

    def arrival(side, t):
        reach = jnp.where(side == 0, z, planes - 1 - z)
        first = t <= reach
        distance = jnp.where(first, t, 2 * reach + 1 - t)
        valid = (t >= 1) & (t <= 2 * reach)
        return z + (2 * side - 1) * distance, jnp.where(first, 0, 1), valid, t == 2 * reach

    ends = (z == planes - 1, z == 0)
    experts(z, 0)

    def slot(t, _):
        for side in range(2):
            origin, h, valid, last = arrival(side, t)

            @pl.when(valid)
            def _(side=side, origin=origin, h=h):
                take(side, origin, h)

            @pl.when(last & (has_above, has_below)[side])
            def _(side=side):
                token_copy(side, z, 1, z + 1 - 2 * side, True).start()

        for side in range(2):
            passed = jnp.where(side == 0, planes - 1 - z, z)
            origin, h, valid, _ = arrival(side, t - 2 * passed - 1)

            @pl.when(valid & jnp.logical_not(ends[side]))
            def _(side=side, origin=origin, h=h):
                send_sum(side, origin, h, False)

        def compute(j, _):
            side = jnp.where(z >= planes // 2, j, 1 - j)
            origin, h, valid, _ = arrival(side, t)
            own = j == 2
            now = t == jnp.where(ends[0] | ends[1], 1, 2 * planes - 3)

            @pl.when(jnp.where(own, now, valid))
            def _():
                experts(jnp.where(own, z, origin), jnp.where(own, 1, h))

            @pl.when(jnp.logical_not(own) & valid & jnp.where(side == 0, ends[0], ends[1]))
            def _():
                send_sum(side, origin, h, True)

            return 0

        lax.fori_loop(0, 3, compute, 0)
        return 0

    lax.fori_loop(1, 2 * planes, slot, 0)

    @pl.when(z == 0)
    def _():
        incoming[1, z] = jnp.zeros((rows, width), BF16)

    @pl.when(z == planes - 1)
    def _():
        incoming[0, z] = jnp.zeros((rows, width), BF16)

    for h in range(2):
        half_copy(z, h).wait_recv()

        @pl.when(has_below)
        def _(h=h):
            sum_copy(1, z, h, z).wait_recv()

        @pl.when(has_above)
        def _(h=h):
            sum_copy(0, z, h, z).wait_recv()

        def finish(i, _, h=h):
            here = pl.ds(pl.multiple_of(h * part + i * 32, 32), 32)
            total = thinker[here].astype(F32) + mine[z, here].astype(F32) + theirs[z, here].astype(F32)
            total = total + incoming[0, z, here].astype(F32) + incoming[1, z, here].astype(F32)
            result[here] = total.astype(BF16)
            return 0

        lax.fori_loop(0, part // 32, finish, 0)

    def drain(origin, _):
        for h in range(2):
            other_copy(origin, h).wait_send()
            half_copy(origin, h).wait_send()

            @pl.when((origin <= z) & has_above)
            def _(h=h):
                token_copy(0, origin, h, z).wait_send()

            @pl.when((origin >= z) & has_below)
            def _(h=h):
                token_copy(1, origin, h, z).wait_send()

            @pl.when(origin > z)
            def _(h=h):
                sum_copy(1, origin, h, z).wait_send()

            @pl.when(origin < z)
            def _(h=h):
                sum_copy(0, origin, h, z).wait_send()

        return 0

    lax.fori_loop(0, planes, drain, 0)


def body(
    groups,
    seqs,
    audio,
    block_ids,
    norm_gain,
    qkv_weight,
    out_weight,
    adapter_weight,
    moe_gain,
    gate_weight,
    up_weight,
    down_weight,
    routes,
    route_weights,
):
    frames, width = audio.shape[1:]
    tokens, features = routes.shape[1], moe_gain.shape[0]
    blocks = frames // EDGE
    vmem = pl.BlockSpec(memory_space=pltpu.VMEM)
    anywhere = pl.BlockSpec(memory_space=pl.ANY)
    dma = pltpu.SemaphoreType.DMA
    events = max(13, groups - 1)
    planes = seqs // 2
    ff = gate_weight.shape[2]
    block = (planes, tokens, features)
    expert_scratch = [
        pltpu.VMEM((features, ff), BF16),
        pltpu.VMEM((features, ff), BF16),
        pltpu.VMEM((ff, features), BF16),
        pltpu.VMEM((planes, 2, tokens, features), BF16),
        pltpu.VMEM((tokens, ff), BF16),
        pltpu.VMEM(block, BF16),
        pltpu.VMEM(block, BF16),
        pltpu.VMEM(block, BF16),
        pltpu.VMEM((2,) + block, BF16),
        pltpu.VMEM((2,) + block, BF16),
        dma((3,)),
        dma((3, planes, 2)),
        dma((2, planes, 2)),
        dma((planes, 2)),
        dma((planes, 2)),
        dma((2, planes, 2)),
        dma((2, planes, 2)),
        pltpu.VMEM((seqs, tokens, 128), F32),
    ]
    expert_weights = (gate_weight[0], up_weight[0], down_weight[0])
    if groups == 4 and seqs == 8:
        gathers = 5 + 2 * STRIPES
        result = pl.pallas_call(
            functools.partial(fused_kernel, groups, seqs),
            out_shape=jax.ShapeDtypeStruct((tokens, features), BF16),
            in_specs=[vmem] * 6 + [anywhere] * 6,
            out_specs=vmem,
            scratch_shapes=[
                pltpu.VMEM((tokens, features), BF16),
                pltpu.VMEM((tokens, features), BF16),
                pltpu.VMEM((seqs, seqs, tokens), F32),
                pltpu.VMEM((3 * width, width), BF16),
                pltpu.VMEM((width, width), BF16),
                pltpu.VMEM((2 * width, features), BF16),
                pltpu.VMEM((frames + 2 * EDGE, width), BF16),
                pltpu.VMEM((frames, width), BF16),
                pltpu.VMEM((frames + 2 * EDGE, 2 * width), BF16),
                pltpu.VMEM((2, HALO, width), BF16),
                pltpu.VMEM((blocks + 2, 8, EDGE), jnp.int32),
                pltpu.VMEM((seqs, tokens), F32),
                pltpu.VMEM((frames, width), BF16),
                pltpu.VMEM((tokens, 2 * width), BF16),
                pltpu.VMEM((tokens, features), F32),
                dma((gathers,)),
                dma((gathers, events)),
                dma((gathers, events)),
                dma((4,)),
                dma((4,)),
                dma((seqs - 1,)),
                dma((seqs - 1,)),
            ]
            + expert_scratch,
            compiler_params=pltpu.CompilerParams(
                collective_id=2, has_side_effects=True, vmem_limit_bytes=VMEM_LIMIT
            ),
            name="fused",
        )(
            audio,
            block_ids,
            norm_gain,
            moe_gain,
            routes[0].T,
            route_weights[0].T,
            qkv_weight.T,
            out_weight.T,
            adapter_weight,
            *expert_weights,
        )
        return result[None]
    thinker, expert_in, tables = pl.pallas_call(
        functools.partial(encoder_kernel, groups, seqs),
        out_shape=(
            jax.ShapeDtypeStruct((tokens, features), BF16),
            jax.ShapeDtypeStruct((tokens, features), BF16),
            jax.ShapeDtypeStruct((seqs, seqs, tokens), F32),
        ),
        in_specs=[vmem] * 6 + [anywhere] * 3,
        out_specs=(vmem,) * 3,
        scratch_shapes=[
            pltpu.VMEM((3 * width, width), BF16),
            pltpu.VMEM((width, width), BF16),
            pltpu.VMEM((2 * width, features), BF16),
            pltpu.VMEM((frames, width), BF16),
            pltpu.VMEM((frames, width), BF16),
            pltpu.VMEM((frames + 2 * EDGE, 2 * width), BF16),
            pltpu.VMEM((blocks + 2, 8, EDGE), jnp.int32),
            pltpu.VMEM((seqs, tokens), F32),
            pltpu.VMEM((frames, width), BF16),
            pltpu.VMEM((frames // 2, width), BF16),
            pltpu.VMEM((frames // 2, width), BF16),
            dma((5,)),
            dma((5, events)),
            dma((5, events)),
            dma((4,)),
            dma((4,)),
            dma((seqs - 1,)),
            dma((seqs - 1,)),
        ],
        compiler_params=pltpu.CompilerParams(
            collective_id=0, has_side_effects=True, vmem_limit_bytes=VMEM_LIMIT
        ),
        name="encoder",
    )(
        audio,
        block_ids,
        norm_gain,
        moe_gain,
        routes[0].T,
        route_weights[0].T,
        qkv_weight.T,
        out_weight.T,
        adapter_weight,
    )
    result = pl.pallas_call(
        functools.partial(expert_kernel, seqs),
        out_shape=jax.ShapeDtypeStruct((tokens, features), BF16),
        in_specs=[vmem] * 3 + [anywhere] * 3,
        out_specs=vmem,
        scratch_shapes=expert_scratch,
        compiler_params=pltpu.CompilerParams(
            collective_id=1, has_side_effects=True, vmem_limit_bytes=VMEM_LIMIT
        ),
        name="experts",
    )(expert_in, thinker, tables, *expert_weights)
    return result[None]


def solution(mesh):
    placed = (
        P("grp", "seq", None),
        P("grp", "seq"),
        P(),
        P(None, "grp"),
        P(None, "grp"),
        P(None, "grp"),
        P(),
        P("seq", None, None),
        P("seq", None, None),
        P("seq", None, None),
        P("grp", "seq", None),
        P("grp", "seq", None),
    )
    return jax.shard_map(
        functools.partial(body, mesh.shape["grp"], mesh.shape["seq"]),
        mesh=mesh,
        in_specs=placed,
        out_specs=P("grp", "seq", None),
        check_vma=False,
    )
```

```python
import functools

import jax
import jax.numpy as jnp
from jax import lax
from jax.experimental import pallas as pl
from jax.experimental.pallas import tpu as pltpu
from jax.sharding import PartitionSpec as P

HEAD = 64
EDGE = 128
HALO = 112
QKV_PLAN = ((5, 0), (4, 0), (0, 6))
OUT_PLAN = ((3, 2),)
ADAPTER_PARTS = 4
STEPS = (
    (("begin", 0), ),
    (("begin", 1), ),
    (("forward", 0), ("begin", 2), ),
    (("forward", 1), ("share", 0), ("forward", 2), ("begin", 3), ("begin", 4), ("share", 1), ("relay", 0), ("share", 2), ("relay", 1), ("end", 0), ("end", 1), ("end", 2), ),
    (("forward", 3), ("begin", 5), ),
    (),
    (("forward", 4), ("begin", 6), ),
    (),
    (("share", 3), ),
    (),
    (),
    (("forward", 5), ("begin", 7), ("relay", 4), ),
    (),
    (("relay", 3), ("forward", 6), ),
    (),
    (),
    (("forward", 7), ("relay", 5), ),
    (),
    (("relay", 6), ("relay", 7), ),
)
LN_EPSILON = 1e-05
RMS_EPSILON = 1e-06
MASKED = -1e30
VMEM_LIMIT = 66_000_000
MESH = pl.DeviceIdType.MESH
BF16 = jnp.bfloat16
F32 = jnp.float32
NT = (((1,), (1,)), ((), ()))


def greet(g, s, groups, seqs, across):
    barrier = pltpu.get_barrier_semaphore()
    if across:
        for k in range(1, groups):
            pl.semaphore_signal(
                barrier, inc=1, device_id={"grp": lax.rem(g + k, groups), "seq": s}, device_id_type=MESH
            )
    for k in range(1, seqs):
        pl.semaphore_signal(
            barrier, inc=1, device_id={"grp": g, "seq": lax.rem(s + k, seqs)}, device_id_type=MESH
        )
    pl.semaphore_wait(barrier, seqs - 1 + (groups - 1 if across else 0))


def fill_table(routes, route_weights, table):
    experts = lax.broadcasted_iota(jnp.int32, table.shape, 0)
    given = route_weights[...]
    shares = given / jnp.sum(given, axis=0, keepdims=True)
    chosen = routes[...]
    table[...] = sum(
        jnp.where(experts == chosen[k : k + 1], shares[k : k + 1], 0.0) for k in range(chosen.shape[0])
    )


class Gather:
    def __init__(self, g, s, groups, seqs, shard, whole, rows, by_lanes, deep, own_sem, send_sem, recv_sem):
        self.g, self.s, self.groups = g, s, groups
        self.shard, self.whole, self.by_lanes = shard, whole, by_lanes
        self.own_sem, self.send_sem, self.recv_sem = own_sem, send_sem, recv_sem
        self.first, self.rows = rows
        self.routed = groups == 4
        self.deep = deep and self.routed and seqs % 4 == 0
        core, plane = lax.rem(s, 2), lax.rem(s // 2, 2)
        self.other = s + 1 - 2 * core
        self.paired = s + 2 - 4 * plane
        if self.deep:
            self.size = self.rows // 4
            self.start = self.first + (plane * 2 + core) * self.size
            self.paired_start = self.first + ((1 - plane) * 2 + core) * self.size
        else:
            self.size = self.rows // 2
            self.start = self.first + core * self.size
        self.cut = (self.size // 2 + 15) // 16 * 16
        self.copies = {}

    def part(self, group, first, count):
        if self.by_lanes:
            columns = self.shard.shape[1]
            start = pl.multiple_of(group * columns, 128)
            return self.whole.at[pl.ds(pl.multiple_of(first, 16), count), pl.ds(start, columns)]
        return self.whole.at[pl.ds(pl.multiple_of(group * self.shard.shape[0] + first, 16), count)]

    def source(self, first, count):
        return self.shard.at[pl.ds(pl.multiple_of(first, 16), count)]

    def send(self, event, source, target, grp, seq):
        copy = pltpu.make_async_remote_copy(
            src_ref=source,
            dst_ref=target,
            send_sem=self.send_sem.at[event],
            recv_sem=self.recv_sem.at[event],
            device_id={"grp": grp, "seq": seq},
            device_id_type=MESH,
        )
        copy.start()
        self.copies[event] = copy

    def pass_on(self, event, part, grp, seq):
        self.send(event, part, part, grp, seq)

    def got(self, *events):
        for event in events:
            self.copies[event].wait_recv()

    def xor(self, k):
        if k == 1:
            return self.g + 1 - 2 * lax.rem(self.g, 2)
        if k == 2:
            return lax.rem(self.g + 2, 4)
        return 3 - self.g

    def begin(self):
        if self.routed:
            for event, k in ((0, 1), (1, 2)):
                self.send(
                    event,
                    self.source(self.start, self.size),
                    self.part(self.g, self.start, self.size),
                    self.xor(k),
                    self.s,
                )
        else:
            for k in range(1, self.groups):
                self.send(
                    k - 1,
                    self.source(self.first, self.rows),
                    self.part(self.g, self.first, self.rows),
                    lax.rem(self.g + k, self.groups),
                    self.s,
                )
        self.own = pltpu.make_async_copy(
            self.source(self.first, self.rows), self.part(self.g, self.first, self.rows), self.own_sem
        )
        self.own.start()

    def forward(self):
        if not self.routed:
            return
        x, y = self.xor(1), self.xor(2)
        self.got(0, 1)
        self.pass_on(2, self.part(y, self.start, self.cut), x, self.s)
        self.pass_on(3, self.part(x, self.start + self.cut, self.size - self.cut), y, self.s)
        for event, k in ((0, x), (1, y)):
            near = self.part(k, self.start, self.size)
            if self.deep:
                self.pass_on(7 + event, near, self.g, self.paired)
            self.pass_on(4 + event, near, self.g, self.other)

    def share(self):
        if not self.routed:
            return
        self.got(2, 3)
        far = self.part(self.xor(3), self.start, self.size)
        if self.deep:
            self.pass_on(9, far, self.g, self.paired)
        self.pass_on(6, far, self.g, self.other)

    def relay(self):
        if not self.deep:
            return
        for event, k in ((0, 1), (1, 2), (2, 3)):
            self.got(7 + event)
            self.pass_on(10 + event, self.part(self.xor(k), self.paired_start, self.size), self.g, self.other)

    def end(self):
        self.own.wait()
        if self.deep:
            self.got(4, 5, 6, 10, 11, 12)
        elif self.routed:
            self.got(4, 5, 6)
        else:
            self.got(*range(self.groups - 1))

    def drain(self):
        for copy in self.copies.values():
            copy.wait_send()


class PairShare:
    def __init__(self, g, s, shard, whole, first, rows, send_sem, recv_sem):
        self.g, self.s, self.shard, self.whole = g, s, shard, whole
        self.send_sem, self.recv_sem = send_sem, recv_sem
        core, plane = lax.rem(s, 2), lax.rem(s // 2, 2)
        self.other, self.paired = s + 1 - 2 * core, s + 2 - 4 * plane
        self.size = rows // 4
        self.here = self.span(first + (plane * 2 + core) * self.size)
        self.there = self.span(first + ((1 - plane) * 2 + core) * self.size)
        self.copies = {}

    def span(self, first):
        return pl.ds(pl.multiple_of(first, 16), self.size)

    def send(self, event, source, rows, grp, seq):
        copy = pltpu.make_async_remote_copy(
            src_ref=source.at[rows],
            dst_ref=self.whole.at[rows],
            send_sem=self.send_sem.at[event],
            recv_sem=self.recv_sem.at[event],
            device_id={"grp": grp, "seq": seq},
            device_id_type=MESH,
        )
        copy.start()
        self.copies[event] = copy

    def begin(self):
        self.send(0, self.shard, self.here, lax.rem(self.g + 2, 4), self.s)

    def forward(self):
        self.copies[0].wait_recv()
        self.send(1, self.whole, self.here, self.g, self.paired)
        self.send(2, self.whole, self.here, self.g, self.other)

    def share(self):
        pass

    def relay(self):
        self.copies[1].wait_recv()
        self.send(3, self.whole, self.there, self.g, self.other)

    def end(self):
        self.copies[2].wait_recv()
        self.copies[3].wait_recv()

    def drain(self):
        for copy in self.copies.values():
            copy.wait_send()


def encoder_kernel(
    groups,
    seqs,
    audio_block,
    ids,
    gain,
    moe_gain,
    routes,
    route_weights,
    qkv_shard,
    out_shard,
    adapter_shard,
    thinker,
    expert_in,
    tables,
    qkv_w,
    out_w,
    adapter_w,
    normed,
    query,
    pairs,
    ids_ext,
    table,
    attended,
    even,
    odd,
    own_sem,
    weight_send,
    weight_recv,
    edge_send,
    edge_recv,
    tab_send,
    tab_recv,
):
    g, s = lax.axis_index("grp"), lax.axis_index("seq")
    audio = audio_block.at[0]
    frames, width = audio.shape
    heads_pairs = width // 128
    blocks = frames // EDGE
    fill_table(routes, route_weights, table)
    for b in range(blocks):
        ids_ext[b + 1] = jnp.broadcast_to(ids[0:1, b * EDGE : (b + 1) * EDGE], (8, EDGE))
    greet(g, s, groups, seqs, True)

    def gather(i, shard, whole, rows, by_lanes, deep):
        return Gather(
            g, s, groups, seqs, shard, whole, rows, by_lanes, deep, own_sem.at[i], weight_send.at[i], weight_recv.at[i]
        )

    def split(rows, at):
        return (0, at), (at, rows - at)

    qkv_rows, ad_rows = qkv_shard.shape[0], adapter_shard.shape[0]
    qkv_deep, qkv_plain = split(qkv_rows, (qkv_rows // 2 + 63) // 64 * 64)
    ad_deep, ad_plain = split(ad_rows, ad_rows // 2)
    qkv_a = gather(0, qkv_shard, qkv_w, qkv_deep, False, True)
    qkv_b = gather(1, qkv_shard, qkv_w, qkv_plain, False, False)
    out = gather(2, out_shard, out_w, (0, out_shard.shape[0]), False, False)
    ad_a = gather(3, adapter_shard, adapter_w, ad_deep, True, True)
    ad_b = gather(4, adapter_shard, adapter_w, ad_plain, True, False)
    qkv_a.begin()
    qkv_b.begin()

    table_copies = []
    for k in range(1, seqs):
        copy = pltpu.make_async_remote_copy(
            src_ref=table,
            dst_ref=tables.at[s],
            send_sem=tab_send.at[k - 1],
            recv_sem=tab_recv.at[k - 1],
            device_id={"grp": g, "seq": lax.rem(s + k, seqs)},
            device_id_type=MESH,
        )
        copy.start()
        table_copies.append(copy)
    tables[s] = table[...]

    def edge(event, source, target, step):
        return pltpu.make_async_remote_copy(
            src_ref=source,
            dst_ref=target,
            send_sem=edge_send.at[event],
            recv_sem=edge_recv.at[event],
            device_id={"grp": g, "seq": lax.rem(s + step + seqs, seqs)},
            device_id_type=MESH,
        )

    ids_right = edge(0, ids_ext.at[blocks], ids_ext.at[0], 1)
    ids_left = edge(1, ids_ext.at[1], ids_ext.at[blocks + 1], -1)
    pairs_right = edge(2, pairs.at[pl.ds(frames, EDGE)], pairs.at[pl.ds(0, EDGE)], 1)
    pairs_left = edge(3, pairs.at[pl.ds(EDGE, EDGE)], pairs.at[pl.ds(frames + EDGE, EDGE)], -1)
    has_left, has_right = s > 0, s < seqs - 1

    @pl.when(has_right)
    def _():
        ids_right.start()

    @pl.when(has_left)
    def _():
        ids_left.start()

    @pl.when(s == 0)
    def _():
        ids_ext[0] = jnp.full(ids_ext.shape[1:], -1, jnp.int32)
        pairs[0:EDGE] = jnp.zeros((EDGE, pairs.shape[1]), BF16)

    @pl.when(s == seqs - 1)
    def _():
        ids_ext[blocks + 1] = jnp.full(ids_ext.shape[1:], -1, jnp.int32)
        pairs[frames + EDGE :] = jnp.zeros((EDGE, pairs.shape[1]), BF16)

    def norm_rows(i, _):
        rows = pl.ds(pl.multiple_of(i * 64, 64), 64)
        signal = audio[rows].astype(F32)
        centred = signal - jnp.mean(signal, axis=-1, keepdims=True)
        variance = jnp.mean(centred * centred, axis=-1, keepdims=True)
        normed[rows] = (centred * lax.rsqrt(variance + LN_EPSILON) * gain[...]).astype(BF16)
        return 0

    lax.fori_loop(0, frames // 64, norm_rows, 0)

    qkv_a.forward()
    qkv_b.forward()
    out.begin()
    ad_a.begin()
    qkv_a.share()
    qkv_b.share()
    qkv_a.relay()
    qkv_a.end()
    qkv_b.end()

    tile = 256

    def project_pairs(i, _):
        source = pl.ds(pl.multiple_of(width + i * tile, tile), tile)
        columns = pl.ds(pl.multiple_of(i * tile, tile), tile)
        pairs[EDGE : EDGE + frames, columns] = lax.dot_general(
            normed[...], qkv_w[source], NT, preferred_element_type=F32
        ).astype(BF16)
        return 0

    lax.fori_loop(0, 2 * width // tile, project_pairs, 0)

    @pl.when(has_right)
    def _():
        pairs_right.start()

    @pl.when(has_left)
    def _():
        pairs_left.start()

    out.forward()
    ad_b.begin()

    def project_query(i, _):
        columns = pl.ds(pl.multiple_of(i * tile, tile), tile)
        query[:, columns] = lax.dot_general(
            normed[...], qkv_w[columns], NT, preferred_element_type=F32
        ).astype(BF16)
        return 0

    lax.fori_loop(0, width // tile, project_query, 0)
    out.share()
    ad_a.forward()

    @pl.when(has_left)
    def _():
        ids_right.wait_recv()
        pairs_right.wait_recv()

    @pl.when(has_right)
    def _():
        ids_left.wait_recv()
        pairs_left.wait_recv()

    low = lax.broadcasted_iota(jnp.int32, (EDGE, 128), 1) < HEAD
    span = 3 * EDGE
    for b in range(blocks):
        rows = slice(b * EDGE, (b + 1) * EDGE)
        keys = slice(b * EDGE, b * EDGE + span)
        key_ids = jnp.concatenate([ids_ext[b + j][0:1] for j in range(3)], axis=1)
        frame_ids = jnp.broadcast_to(ids_ext[b + 1][0:1], (EDGE, EDGE)).T[:, 0:1]
        same = frame_ids == key_ids
        allowed = jnp.concatenate([same, same], axis=0)

        def attend(p, _, rows=rows, keys=keys, allowed=allowed):
            columns = pl.ds(pl.multiple_of(p * 128, 128), 128)
            both = query[rows, columns]
            nothing = jnp.zeros_like(both)
            stacked = jnp.concatenate(
                [jnp.where(low, both, nothing), jnp.where(low, nothing, both)], axis=0
            )
            scores = lax.dot_general(
                stacked, pairs[keys, columns], NT, preferred_element_type=F32
            ) * HEAD ** (-0.5)
            scores = jnp.where(allowed, scores, MASKED)
            highest = jnp.max(scores, axis=-1, keepdims=True)
            exponent = jnp.exp(scores - highest)
            total = jnp.sum(exponent, axis=-1, keepdims=True)
            value_columns = pl.ds(pl.multiple_of(width + p * 128, 128), 128)
            mixed = jnp.dot(
                (exponent / total).astype(BF16), pairs[keys, value_columns], preferred_element_type=F32
            )
            attended[rows, columns] = jnp.where(low, mixed[:EDGE], mixed[EDGE:]).astype(BF16)
            return 0

        lax.fori_loop(0, heads_pairs, attend, 0)

    out.end()
    tokens = frames // 2
    at_row = lax.broadcasted_iota(jnp.int32, (tokens, frames), 0)
    at_frame = lax.broadcasted_iota(jnp.int32, (tokens, frames), 1)
    first = jnp.where(at_frame == 2 * at_row, 1.0, 0.0).astype(BF16)
    second = jnp.where(at_frame == 2 * at_row + 1, 1.0, 0.0).astype(BF16)

    def encode(i, _):
        columns = pl.ds(pl.multiple_of(i * tile, tile), tile)
        projected = lax.dot_general(attended[...], out_w[columns], NT, preferred_element_type=F32)
        encoded = (audio[:, columns].astype(F32) + projected).astype(BF16)
        even[:, columns] = jnp.dot(first, encoded, preferred_element_type=F32).astype(BF16)
        odd[:, columns] = jnp.dot(second, encoded, preferred_element_type=F32).astype(BF16)
        return 0

    lax.fori_loop(0, width // tile, encode, 0)
    ad_b.forward()
    ad_a.share()
    ad_a.relay()
    ad_b.share()
    ad_a.end()
    ad_b.end()

    def adapt(i, _):
        columns = pl.ds(pl.multiple_of(i * tile, tile), tile)
        thinker[:, columns] = (
            jnp.dot(even[...], adapter_w[0:width, columns], preferred_element_type=F32)
            + jnp.dot(odd[...], adapter_w[width:, columns], preferred_element_type=F32)
        ).astype(BF16)
        return 0

    lax.fori_loop(0, thinker.shape[1] // tile, adapt, 0)

    def rms_rows(i, _):
        rows = pl.ds(pl.multiple_of(i * 32, 32), 32)
        widened = thinker[rows].astype(F32)
        squares = jnp.mean(widened * widened, axis=-1, keepdims=True)
        expert_in[rows] = (widened * lax.rsqrt(squares + RMS_EPSILON) * moe_gain[...]).astype(BF16)
        return 0

    lax.fori_loop(0, tokens // 32, rms_rows, 0)

    for copy in table_copies:
        copy.wait()
    for weight in (qkv_a, qkv_b, out, ad_a, ad_b):
        weight.drain()

    @pl.when(has_right)
    def _():
        ids_right.wait_send()
        pairs_right.wait_send()

    @pl.when(has_left)
    def _():
        ids_left.wait_send()
        pairs_left.wait_send()


def fused_kernel(
    groups,
    seqs,
    audio_block,
    ids,
    gain,
    moe_gain,
    routes,
    route_weights,
    qkv_shard,
    out_shard,
    adapter_shard,
    gate_hbm,
    up_hbm,
    down_hbm,
    result,
    thinker,
    expert_in,
    tables,
    *scratch,
):
    def prepare(start_loads):
        return encode_tokens(
            start_loads,
            groups,
            seqs,
            audio_block,
            ids,
            gain,
            moe_gain,
            routes,
            route_weights,
            qkv_shard,
            out_shard,
            adapter_shard,
            thinker,
            expert_in,
            tables,
            *scratch[:32],
        )

    expert_kernel(
        seqs, expert_in, thinker, tables, gate_hbm, up_hbm, down_hbm, result, *scratch[32:], prepare=prepare
    )


def encode_tokens(
    start_loads,
    groups,
    seqs,
    audio_hbm,
    ids_hbm,
    gain_hbm,
    moe_gain_hbm,
    routes_hbm,
    route_weights_hbm,
    qkv_shard,
    out_shard,
    adapter_shard,
    thinker,
    expert_in,
    tables,
    audio,
    ids,
    gain,
    moe_gain,
    routes,
    route_weights,
    input_sem,
    qkv_w,
    out_w,
    adapter_w,
    normed,
    query,
    pairs,
    halo,
    ids_ext,
    table,
    attended,
    pooled,
    partner,
    produced,
    adapter_sem,
    own_sem,
    weight_send,
    weight_recv,
    pair_send,
    pair_recv,
    swap_send,
    swap_recv,
    edge_send,
    edge_recv,
    tab_send,
    tab_recv,
):
    g, s = lax.axis_index("grp"), lax.axis_index("seq")
    frames, width = audio.shape
    blocks = frames // EDGE
    inputs = [
        pltpu.make_async_copy(source, target, input_sem.at[i])
        for i, (source, target) in enumerate(
            (
                (audio_hbm.at[0], audio),
                (ids_hbm, ids),
                (gain_hbm, gain),
                (moe_gain_hbm, moe_gain),
                (routes_hbm, routes),
                (route_weights_hbm, route_weights),
            )
        )
    ]
    for load in inputs:
        load.start()
    greet(g, s, groups, seqs, True)

    def gather(i, shard, whole, first, rows, deep, by_lanes=False):
        return Gather(
            g, s, groups, seqs, shard, whole, (first, rows), by_lanes, deep,
            own_sem.at[i], weight_send.at[i], weight_recv.at[i],
        )

    items, count = [], 0
    for shard, whole, by_lanes, plan in (
        (qkv_shard, qkv_w, False, QKV_PLAN),
        (out_shard, out_w, False, OUT_PLAN),
    ):
        units, first = sum(sum(pair) for pair in plan), 0
        for pair in plan:
            item = []
            for deep, share in ((True, pair[0]), (False, pair[1])):
                if share:
                    rows = shard.shape[0] * share // units
                    item.append(gather(count, shard, whole, first, rows, deep, by_lanes))
                    first, count = first + rows, count + 1
            items.append(item)
    stripe = adapter_shard.shape[0] // ADAPTER_PARTS
    for k in range(ADAPTER_PARTS):
        items.append(
            [PairShare(g, s, adapter_shard, adapter_w.at[1], k * stripe, stripe, pair_send.at[k], pair_recv.at[k])]
        )
    own_adapter = pltpu.make_async_copy(adapter_shard, adapter_w.at[0], adapter_sem)

    def steps(point):
        for what, k in STEPS[point]:
            for one in items[k]:
                getattr(one, what)()

    steps(0)

    def edge(event, source, target, step):
        return pltpu.make_async_remote_copy(
            src_ref=source,
            dst_ref=target,
            send_sem=edge_send.at[event],
            recv_sem=edge_recv.at[event],
            device_id={"grp": g, "seq": lax.rem(s + step + seqs, seqs)},
            device_id_type=MESH,
        )

    ids_right = edge(0, ids_ext.at[blocks], ids_ext.at[0], 1)
    ids_left = edge(1, ids_ext.at[1], ids_ext.at[blocks + 1], -1)
    halo_right = edge(2, audio_hbm.at[0, pl.ds(frames - HALO, HALO)], halo.at[0], 1)
    halo_left = edge(3, audio_hbm.at[0, pl.ds(0, HALO)], halo.at[1], -1)
    has_left, has_right = s > 0, s < seqs - 1

    @pl.when(has_right)
    def _():
        halo_right.start()

    @pl.when(has_left)
    def _():
        halo_left.start()

    steps(1)
    for load in inputs:
        load.wait()
    for b in range(blocks):
        ids_ext[b + 1] = jnp.broadcast_to(ids[0:1, b * EDGE : (b + 1) * EDGE], (8, EDGE))

    @pl.when(has_right)
    def _():
        ids_right.start()

    @pl.when(has_left)
    def _():
        ids_left.start()

    fill_table(routes, route_weights, table)
    table_copies = []
    for k in range(1, seqs):
        copy = pltpu.make_async_remote_copy(
            src_ref=table,
            dst_ref=tables.at[s],
            send_sem=tab_send.at[k - 1],
            recv_sem=tab_recv.at[k - 1],
            device_id={"grp": g, "seq": lax.rem(s + k, seqs)},
            device_id_type=MESH,
        )
        copy.start()
        table_copies.append(copy)
    tables[s] = table[...]
    own_adapter.start()
    start_loads()

    @pl.when(s == 0)
    def _():
        ids_ext[0] = jnp.full(ids_ext.shape[1:], -1, jnp.int32)
        halo[0] = jnp.zeros(halo.shape[1:], BF16)

    @pl.when(s == seqs - 1)
    def _():
        ids_ext[blocks + 1] = jnp.full(ids_ext.shape[1:], -1, jnp.int32)
        halo[1] = jnp.zeros(halo.shape[1:], BF16)

    def layer_norm(signal):
        signal = signal.astype(F32)
        centred = signal - jnp.mean(signal, axis=-1, keepdims=True)
        variance = jnp.mean(centred * centred, axis=-1, keepdims=True)
        return (centred * lax.rsqrt(variance + LN_EPSILON) * gain[...]).astype(BF16)

    def norm_rows(i, _):
        rows = pl.multiple_of(i * 64, 64)
        normed[pl.ds(EDGE + rows, 64)] = layer_norm(audio[pl.ds(rows, 64)])
        return 0

    lax.fori_loop(0, frames // 64, norm_rows, 0)
    spare = jnp.zeros((EDGE - HALO, width), BF16)
    normed[0 : EDGE - HALO] = spare
    normed[frames + EDGE + HALO :] = spare
    steps(2)

    @pl.when(has_left)
    def _():
        ids_right.wait_recv()
        halo_right.wait_recv()

    @pl.when(has_right)
    def _():
        ids_left.wait_recv()
        halo_left.wait_recv()

    def norm_halo(i, _):
        rows = pl.multiple_of(i * 16, 16)
        normed[pl.ds(EDGE - HALO + rows, 16)] = layer_norm(halo[0, pl.ds(rows, 16)])
        normed[pl.ds(EDGE + frames + rows, 16)] = layer_norm(halo[1, pl.ds(rows, 16)])
        return 0

    lax.fori_loop(0, HALO // 16, norm_halo, 0)
    steps(3)
    tile = 256

    def project_pairs(i, _):
        source = pl.ds(pl.multiple_of(width + i * tile, tile), tile)
        columns = pl.ds(pl.multiple_of(i * tile, tile), tile)
        pairs[:, columns] = lax.dot_general(
            normed[...], qkv_w[source], NT, preferred_element_type=F32
        ).astype(BF16)
        return 0

    half = width // tile
    lax.fori_loop(0, half, project_pairs, 0)
    steps(4)
    lax.fori_loop(half, 2 * half, project_pairs, 0)
    steps(5)

    def project_query(i, _):
        columns = pl.ds(pl.multiple_of(i * tile, tile), tile)
        query[:, columns] = lax.dot_general(
            normed[EDGE : EDGE + frames], qkv_w[columns], NT, preferred_element_type=F32
        ).astype(BF16) * BF16(HEAD ** (-0.5))
        return 0

    lax.fori_loop(0, half, project_query, 0)
    steps(6)
    low = lax.broadcasted_iota(jnp.int32, (EDGE, 128), 1) < HEAD
    span = 3 * EDGE
    for b in range(blocks):
        rows = slice(b * EDGE, (b + 1) * EDGE)
        keys = slice(b * EDGE, b * EDGE + span)
        key_ids = jnp.concatenate([ids_ext[b + j][0:1] for j in range(3)], axis=1)
        frame_ids = jnp.broadcast_to(ids_ext[b + 1][0:1], (EDGE, EDGE)).T[:, 0:1]
        same = frame_ids == key_ids
        allowed = jnp.concatenate([same, same], axis=0)

        def attend(p, _, rows=rows, keys=keys, allowed=allowed):
            columns = pl.ds(pl.multiple_of(p * 128, 128), 128)
            both = query[rows, columns]
            nothing = jnp.zeros_like(both)
            stacked = jnp.concatenate(
                [jnp.where(low, both, nothing), jnp.where(low, nothing, both)], axis=0
            )
            scores = lax.dot_general(stacked, pairs[keys, columns], NT, preferred_element_type=F32)
            scores = jnp.where(allowed, scores, MASKED)
            highest = jnp.max(scores, axis=-1, keepdims=True)
            exponent = jnp.exp(scores - highest)
            total = jnp.sum(exponent, axis=-1, keepdims=True)
            value_columns = pl.ds(pl.multiple_of(width + p * 128, 128), 128)
            mixed = jnp.dot(
                exponent.astype(BF16), pairs[keys, value_columns], preferred_element_type=F32
            ) / total
            attended[rows, columns] = jnp.where(low, mixed[:EDGE], mixed[EDGE:]).astype(BF16)
            return 0

        heads_pairs = width // 128
        cuts = [heads_pairs * k // 4 for k in range(5)]
        for k in range(4):
            lax.fori_loop(cuts[k], cuts[k + 1], attend, 0)
            steps(7 + 4 * b + k)

    for one in items[len(QKV_PLAN)]:
        one.end()
    steps(15)
    tokens = frames // 2
    part = tokens // 2
    x, y = g + 1 - 2 * lax.rem(g, 2), lax.rem(g + 2, 4)
    columns_here = adapter_shard.shape[1]
    at_row = lax.broadcasted_iota(jnp.int32, (part, EDGE), 0)
    at_frame = lax.broadcasted_iota(jnp.int32, (part, EDGE), 1)
    first = jnp.where(at_frame == 2 * at_row, 1.0, 0.0).astype(BF16)
    second = jnp.where(at_frame == 2 * at_row + 1, 1.0, 0.0).astype(BF16)

    def encode_block(b):
        rows, out_rows = slice(b * EDGE, (b + 1) * EDGE), slice(b * part, (b + 1) * part)

        def encode(i, _):
            columns = pl.ds(pl.multiple_of(i * tile, tile), tile)
            projected = lax.dot_general(attended[rows], out_w[columns], NT, preferred_element_type=F32)
            encoded = (audio[rows, columns].astype(F32) + projected).astype(BF16)
            pooled[out_rows, columns] = jnp.dot(first, encoded, preferred_element_type=F32).astype(BF16)
            pooled[out_rows, pl.ds(pl.multiple_of(width + i * tile, tile), tile)] = jnp.dot(
                second, encoded, preferred_element_type=F32
            ).astype(BF16)
            return 0

        lax.fori_loop(0, half, encode, 0)

    def to_partner(event, source, target):
        return pltpu.make_async_remote_copy(
            src_ref=source,
            dst_ref=target,
            send_sem=swap_send.at[event],
            recv_sem=swap_recv.at[event],
            device_id={"grp": x, "seq": s},
            device_id_type=MESH,
        )

    cut = part // 2
    spreads = [
        to_partner(event, pooled.at[pl.ds(start, rows)], partner.at[pl.ds(start, rows)])
        for event, (start, rows) in enumerate(((0, part), (part, cut), (part + cut, part - cut)))
    ]

    def shard_columns(k):
        return pl.ds(pl.multiple_of((g, y)[k] * columns_here, 128), columns_here)

    def give_back(h, k):
        rows = pl.ds(h * part, part)
        return to_partner(3 + 2 * h + k, produced.at[k, rows], thinker.at[rows, shard_columns(k)])

    backs = [[give_back(h, k) for k in range(2)] for h in range(2)]

    def project(h):
        rows = slice(h * part, (h + 1) * part)
        for k in range(2):

            def one(i, _, k=k):
                columns = pl.ds(pl.multiple_of(i * tile, tile), tile)
                batch = jnp.concatenate([pooled[rows], partner[rows]], axis=0)
                found = jnp.dot(batch, adapter_w[k, :, columns], preferred_element_type=F32).astype(BF16)
                start = pl.multiple_of((g, y)[k] * columns_here + i * tile, tile)
                thinker[rows, pl.ds(start, tile)] = found[:part]
                produced[k, rows, columns] = found[part:]
                return 0

            lax.fori_loop(0, columns_here // tile, one, 0)
            backs[h][k].start()

    def normalise(h):
        for back in backs[h]:
            back.wait_recv()

        def rms_rows(i, _):
            rows = pl.ds(pl.multiple_of(h * part + i * 32, 32), 32)
            widened = thinker[rows].astype(F32)
            squares = jnp.mean(widened * widened, axis=-1, keepdims=True)
            expert_in[rows] = (widened * lax.rsqrt(squares + RMS_EPSILON) * moe_gain[...]).astype(BF16)
            return 0

        lax.fori_loop(0, part // 32, rms_rows, 0)

    encode_block(0)
    spreads[0].start()
    steps(16)
    encode_block(1)
    spreads[1].start()
    steps(17)
    own_adapter.wait()
    steps(18)
    for one in sum(items[len(QKV_PLAN) + 1 :], []):
        one.end()
    spreads[0].wait_recv()
    project(0)
    spreads[2].start()
    normalise(0)

    def second_project():
        spreads[1].wait_recv()
        spreads[2].wait_recv()
        project(1)

    def second_normalise():
        normalise(1)

    for copy in table_copies:
        copy.wait()

    def finish():
        for weight in sum(items, []):
            weight.drain()
        for copy in spreads + sum(backs, []):
            copy.wait_send()

        @pl.when(has_right)
        def _():
            ids_right.wait_send()
            halo_right.wait_send()

        @pl.when(has_left)
        def _():
            ids_left.wait_send()
            halo_left.wait_send()

    return finish, second_project, second_normalise


def expert_kernel(
    seqs,
    expert_in,
    thinker,
    tables,
    gate_hbm,
    up_hbm,
    down_hbm,
    result,
    gate_w,
    up_w,
    down_w,
    tokens_all,
    hidden,
    mine,
    theirs,
    to_other,
    incoming,
    outgoing,
    load_sem,
    tok_send,
    tok_recv,
    half_send,
    half_recv,
    sum_send,
    sum_recv,
    share_of,
    prepare=None,
):
    g, s = lax.axis_index("grp"), lax.axis_index("seq")
    planes = seqs // 2
    z, c = s // 2, lax.rem(s, 2)
    other = 1 - c
    rows, width = expert_in.shape
    ff = gate_w.shape[1]
    loads = [
        pltpu.make_async_copy(source, target, load_sem.at[i])
        for i, (source, target) in enumerate(((gate_hbm, gate_w), (up_hbm, up_w), (down_hbm, down_w)))
    ]

    def start_loads():
        for load in loads:
            load.start()

    if prepare is None:
        start_loads()
        greet(g, s, 1, seqs, False)
    else:
        settle, second_project, second_normalise = prepare(start_loads)

    part = rows // 2

    def span(h):
        return pl.ds(pl.multiple_of(h * part, part), part)

    def move(source, target, send, recv, plane, core):
        return pltpu.make_async_remote_copy(
            src_ref=source,
            dst_ref=target,
            send_sem=send,
            recv_sem=recv,
            device_id={"grp": g, "seq": plane * 2 + core},
            device_id_type=MESH,
        )

    def token_copy(side, origin, h, plane, own=False):
        slot = tokens_all.at[origin, c, span(h)]
        source = expert_in.at[span(h)] if own else slot
        return move(source, slot, tok_send.at[side, origin, h], tok_recv.at[0, origin, h], plane, c)

    def other_copy(origin, h, own=False):
        slot = tokens_all.at[origin, c, span(h)]
        source = expert_in.at[span(h)] if own else slot
        return move(source, slot, tok_send.at[2, origin, h], tok_recv.at[1, origin, h], z, other)

    def half_copy(origin, h):
        return move(
            to_other.at[origin, span(h)],
            theirs.at[origin, span(h)],
            half_send.at[origin, h],
            half_recv.at[origin, h],
            z,
            other,
        )

    def sum_copy(side, target, h, plane):
        return move(
            outgoing.at[side, target, span(h)],
            incoming.at[side, target, span(h)],
            sum_send.at[side, target, h],
            sum_recv.at[side, target, h],
            plane,
            c,
        )

    has_above, has_below = z < planes - 1, z > 0

    @pl.when(has_above)
    def _():
        token_copy(0, z, 0, z + 1, True).start()

    @pl.when(has_below)
    def _():
        token_copy(1, z, 0, z - 1, True).start()

    other_copy(z, 0, True).start()
    tokens_all[z, c, 0:part] = expert_in[0:part]
    for load in loads:
        load.wait()
    for k in range(seqs):
        share_of[k] = jnp.broadcast_to(tables[k, pl.ds(s, 1)], (128, rows)).T
    rise_tile = 384 if ff % 384 == 0 else 128
    fall_tile = 512 if width % 512 == 0 else 128

    def experts(origin, h):
        other_copy(origin, h).wait_recv()

        def rise(i, _):
            columns = pl.ds(pl.multiple_of(i * rise_tile, rise_tile), rise_tile)
            batch = tokens_all[origin, :, span(h)].reshape(2 * part, width)
            gate = jnp.dot(batch, gate_w[:, columns], preferred_element_type=F32)
            up = jnp.dot(batch, up_w[:, columns], preferred_element_type=F32)
            hidden[:, columns] = (gate / (1.0 + jnp.exp(-gate)) * up).astype(BF16)
            return 0

        lax.fori_loop(0, ff // rise_tile, rise, 0)
        share = jnp.concatenate([share_of[origin * 2 + k, span(h), 0:1] for k in range(2)], axis=0)

        def fall(i, _):
            columns = pl.ds(pl.multiple_of(i * fall_tile, fall_tile), fall_tile)
            produced = jnp.dot(hidden[...], down_w[:, columns], preferred_element_type=F32)
            weighted = (produced.astype(BF16).astype(F32) * share).astype(BF16)
            mine[origin, span(h), columns] = jnp.where(c == 0, weighted[:part], weighted[part:])
            to_other[origin, span(h), columns] = jnp.where(c == 0, weighted[part:], weighted[:part])
            return 0

        lax.fori_loop(0, width // fall_tile, fall, 0)
        half_copy(origin, h).start()

    def take(side, origin, h):
        token_copy(side, origin, h, z).wait_recv()

        @pl.when(jnp.where(side == 0, has_above, has_below))
        def _():
            token_copy(side, origin, h, z + 1 - 2 * side).start()

        other_copy(origin, h).start()

    def send_sum(side, origin, h, starts):
        half_copy(origin, h).wait_recv()
        total = mine[origin, span(h)].astype(F32) + theirs[origin, span(h)].astype(F32)
        if starts:
            outgoing[side, origin, span(h)] = total.astype(BF16)
        else:
            sum_copy(side, origin, h, z).wait_recv()
            came = incoming[side, origin, span(h)].astype(F32)
            outgoing[side, origin, span(h)] = (total + came).astype(BF16)
        sum_copy(side, origin, h, z + 2 * side - 1).start()

    def arrival(side, t):
        reach = jnp.where(side == 0, z, planes - 1 - z)
        first = t <= reach
        distance = jnp.where(first, t, 2 * reach + 1 - t)
        valid = (t >= 1) & (t <= 2 * reach)
        return z + (2 * side - 1) * distance, jnp.where(first, 0, 1), valid, t == 2 * reach

    ends = (z == planes - 1, z == 0)
    experts(z, 0)
    if prepare is not None:
        second_project()

    def slot(t, _):
        for side in range(2):
            origin, h, valid, last = arrival(side, t)

            @pl.when(valid)
            def _(side=side, origin=origin, h=h):
                take(side, origin, h)

            @pl.when(last & (has_above, has_below)[side])
            def _(side=side):
                token_copy(side, z, 1, z + 1 - 2 * side, True).start()

        for side in range(2):
            passed = jnp.where(side == 0, planes - 1 - z, z)
            origin, h, valid, _ = arrival(side, t - 2 * passed - 1)

            @pl.when(valid & jnp.logical_not(ends[side]))
            def _(side=side, origin=origin, h=h):
                send_sum(side, origin, h, False)

        @pl.when(t == 1)
        def _():
            if prepare is not None:
                second_normalise()
            for side in range(2):

                @pl.when(ends[1 - side])
                def _(side=side):
                    token_copy(side, z, 1, z + 1 - 2 * side, True).start()

            other_copy(z, 1, True).start()
            tokens_all[z, c, part:] = expert_in[part:]

        def compute(j, _):
            side = jnp.where(z >= planes // 2, j, 1 - j)
            origin, h, valid, _ = arrival(side, t)
            own = j == 2
            now = t == jnp.where(ends[0] | ends[1], 1, 2 * planes - 3)

            @pl.when(jnp.where(own, now, valid))
            def _():
                experts(jnp.where(own, z, origin), jnp.where(own, 1, h))

            @pl.when(jnp.logical_not(own) & valid & jnp.where(side == 0, ends[0], ends[1]))
            def _():
                send_sum(side, origin, h, True)

            return 0

        lax.fori_loop(0, 3, compute, 0)
        return 0

    lax.fori_loop(1, 2 * planes, slot, 0)

    @pl.when(z == 0)
    def _():
        incoming[1, z] = jnp.zeros((rows, width), BF16)

    @pl.when(z == planes - 1)
    def _():
        incoming[0, z] = jnp.zeros((rows, width), BF16)

    for h in range(2):
        half_copy(z, h).wait_recv()

        @pl.when(has_below)
        def _(h=h):
            sum_copy(1, z, h, z).wait_recv()

        @pl.when(has_above)
        def _(h=h):
            sum_copy(0, z, h, z).wait_recv()

        def finish(i, _, h=h):
            here = pl.ds(pl.multiple_of(h * part + i * 32, 32), 32)
            total = thinker[here].astype(F32) + mine[z, here].astype(F32) + theirs[z, here].astype(F32)
            total = total + incoming[0, z, here].astype(F32) + incoming[1, z, here].astype(F32)
            result[here] = total.astype(BF16)
            return 0

        lax.fori_loop(0, part // 32, finish, 0)

    def drain(origin, _):
        for h in range(2):
            other_copy(origin, h).wait_send()
            half_copy(origin, h).wait_send()

            @pl.when((origin <= z) & has_above)
            def _(h=h):
                token_copy(0, origin, h, z).wait_send()

            @pl.when((origin >= z) & has_below)
            def _(h=h):
                token_copy(1, origin, h, z).wait_send()

            @pl.when(origin > z)
            def _(h=h):
                sum_copy(1, origin, h, z).wait_send()

            @pl.when(origin < z)
            def _(h=h):
                sum_copy(0, origin, h, z).wait_send()

        return 0

    lax.fori_loop(0, planes, drain, 0)
    if prepare is not None:
        settle()


def body(
    groups,
    seqs,
    audio,
    block_ids,
    norm_gain,
    qkv_weight,
    out_weight,
    adapter_weight,
    moe_gain,
    gate_weight,
    up_weight,
    down_weight,
    routes,
    route_weights,
):
    frames, width = audio.shape[1:]
    tokens, features = routes.shape[1], moe_gain.shape[0]
    blocks = frames // EDGE
    vmem = pl.BlockSpec(memory_space=pltpu.VMEM)
    anywhere = pl.BlockSpec(memory_space=pl.ANY)
    dma = pltpu.SemaphoreType.DMA
    events = max(13, groups - 1)
    planes = seqs // 2
    ff = gate_weight.shape[2]
    block = (planes, tokens, features)
    expert_scratch = [
        pltpu.VMEM((features, ff), BF16),
        pltpu.VMEM((features, ff), BF16),
        pltpu.VMEM((ff, features), BF16),
        pltpu.VMEM((planes, 2, tokens, features), BF16),
        pltpu.VMEM((tokens, ff), BF16),
        pltpu.VMEM(block, BF16),
        pltpu.VMEM(block, BF16),
        pltpu.VMEM(block, BF16),
        pltpu.VMEM((2,) + block, BF16),
        pltpu.VMEM((2,) + block, BF16),
        dma((3,)),
        dma((3, planes, 2)),
        dma((2, planes, 2)),
        dma((planes, 2)),
        dma((planes, 2)),
        dma((2, planes, 2)),
        dma((2, planes, 2)),
        pltpu.VMEM((seqs, tokens, 128), F32),
    ]
    expert_weights = (gate_weight[0], up_weight[0], down_weight[0])
    if groups == 4 and seqs == 8:
        gathers = sum(sum(1 for share in pair if share) for plan in (QKV_PLAN, OUT_PLAN) for pair in plan)
        result = pl.pallas_call(
            functools.partial(fused_kernel, groups, seqs),
            out_shape=jax.ShapeDtypeStruct((tokens, features), BF16),
            in_specs=[anywhere] * 12,
            out_specs=vmem,
            scratch_shapes=[
                pltpu.VMEM((tokens, features), BF16),
                pltpu.VMEM((tokens, features), BF16),
                pltpu.VMEM((seqs, seqs, tokens), F32),
                pltpu.VMEM((frames, width), BF16),
                pltpu.VMEM(block_ids.shape, jnp.int32),
                pltpu.VMEM(norm_gain.shape, F32),
                pltpu.VMEM(moe_gain.shape, F32),
                pltpu.VMEM(routes.shape[:0:-1], jnp.int32),
                pltpu.VMEM(routes.shape[:0:-1], F32),
                dma((6,)),
                pltpu.VMEM((3 * width, width), BF16),
                pltpu.VMEM((width, width), BF16),
                pltpu.VMEM((2,) + adapter_weight.shape, BF16),
                pltpu.VMEM((frames + 2 * EDGE, width), BF16),
                pltpu.VMEM((frames, width), BF16),
                pltpu.VMEM((frames + 2 * EDGE, 2 * width), BF16),
                pltpu.VMEM((2, HALO, width), BF16),
                pltpu.VMEM((blocks + 2, 8, EDGE), jnp.int32),
                pltpu.VMEM((seqs, tokens), F32),
                pltpu.VMEM((frames, width), BF16),
                pltpu.VMEM((tokens, 2 * width), BF16),
                pltpu.VMEM((tokens, 2 * width), BF16),
                pltpu.VMEM((2, tokens, adapter_weight.shape[1]), BF16),
                dma,
                dma((gathers,)),
                dma((gathers, events)),
                dma((gathers, events)),
                dma((ADAPTER_PARTS, 4)),
                dma((ADAPTER_PARTS, 4)),
                dma((7,)),
                dma((7,)),
                dma((4,)),
                dma((4,)),
                dma((seqs - 1,)),
                dma((seqs - 1,)),
            ]
            + expert_scratch,
            compiler_params=pltpu.CompilerParams(
                collective_id=2, has_side_effects=True, vmem_limit_bytes=VMEM_LIMIT
            ),
            name="fused",
        )(
            audio,
            block_ids,
            norm_gain,
            moe_gain,
            routes[0].T,
            route_weights[0].T,
            qkv_weight.T,
            out_weight.T,
            adapter_weight,
            *expert_weights,
        )
        return result[None]
    thinker, expert_in, tables = pl.pallas_call(
        functools.partial(encoder_kernel, groups, seqs),
        out_shape=(
            jax.ShapeDtypeStruct((tokens, features), BF16),
            jax.ShapeDtypeStruct((tokens, features), BF16),
            jax.ShapeDtypeStruct((seqs, seqs, tokens), F32),
        ),
        in_specs=[vmem] * 6 + [anywhere] * 3,
        out_specs=(vmem,) * 3,
        scratch_shapes=[
            pltpu.VMEM((3 * width, width), BF16),
            pltpu.VMEM((width, width), BF16),
            pltpu.VMEM((2 * width, features), BF16),
            pltpu.VMEM((frames, width), BF16),
            pltpu.VMEM((frames, width), BF16),
            pltpu.VMEM((frames + 2 * EDGE, 2 * width), BF16),
            pltpu.VMEM((blocks + 2, 8, EDGE), jnp.int32),
            pltpu.VMEM((seqs, tokens), F32),
            pltpu.VMEM((frames, width), BF16),
            pltpu.VMEM((frames // 2, width), BF16),
            pltpu.VMEM((frames // 2, width), BF16),
            dma((5,)),
            dma((5, events)),
            dma((5, events)),
            dma((4,)),
            dma((4,)),
            dma((seqs - 1,)),
            dma((seqs - 1,)),
        ],
        compiler_params=pltpu.CompilerParams(
            collective_id=0, has_side_effects=True, vmem_limit_bytes=VMEM_LIMIT
        ),
        name="encoder",
    )(
        audio,
        block_ids,
        norm_gain,
        moe_gain,
        routes[0].T,
        route_weights[0].T,
        qkv_weight.T,
        out_weight.T,
        adapter_weight,
    )
    result = pl.pallas_call(
        functools.partial(expert_kernel, seqs),
        out_shape=jax.ShapeDtypeStruct((tokens, features), BF16),
        in_specs=[vmem] * 3 + [anywhere] * 3,
        out_specs=vmem,
        scratch_shapes=expert_scratch,
        compiler_params=pltpu.CompilerParams(
            collective_id=1, has_side_effects=True, vmem_limit_bytes=VMEM_LIMIT
        ),
        name="experts",
    )(expert_in, thinker, tables, *expert_weights)
    return result[None]


def solution(mesh):
    placed = (
        P("grp", "seq", None),
        P("grp", "seq"),
        P(),
        P(None, "grp"),
        P(None, "grp"),
        P(None, "grp"),
        P(),
        P("seq", None, None),
        P("seq", None, None),
        P("seq", None, None),
        P("grp", "seq", None),
        P("grp", "seq", None),
    )
    return jax.shard_map(
        functools.partial(body, mesh.shape["grp"], mesh.shape["seq"]),
        mesh=mesh,
        in_specs=placed,
        out_specs=P("grp", "seq", None),
        check_vma=False,
    )
```

```python
import functools

import jax
import jax.numpy as jnp
from jax import lax
from jax.experimental import pallas as pl
from jax.experimental.pallas import tpu as pltpu
from jax.sharding import PartitionSpec as P

HEAD = 64
EDGE = 128
HALO = 112
PIECES = 2
QKV_PLAN = ((5, 0), (4, 0), (0, 6))
OUT_PLAN = ((3, 2),)
ADAPTER_PARTS = 4
STEPS = (
    (("begin", 0), ),
    (("begin", 1), ),
    (("forward", 0), ("begin", 2), ),
    (("forward", 1), ("share", 0), ("forward", 2), ("begin", 3), ("begin", 4), ("share", 1), ("relay", 0), ("share", 2), ("relay", 1), ("end", 0), ("end", 1), ("end", 2), ),
    (("forward", 3), ("begin", 5), ),
    (),
    (("forward", 4), ("begin", 6), ),
    (),
    (("share", 3), ),
    (),
    (),
    (("forward", 5), ("begin", 7), ("relay", 4), ),
    (),
    (("relay", 3), ("forward", 6), ),
    (),
    (),
    (("forward", 7), ("relay", 5), ),
    (),
    (("relay", 6), ("relay", 7), ),
)
LN_EPSILON = 1e-05
RMS_EPSILON = 1e-06
MASKED = -1e30
VMEM_LIMIT = 66_000_000
MESH = pl.DeviceIdType.MESH
BF16 = jnp.bfloat16
F32 = jnp.float32
NT = (((1,), (1,)), ((), ()))


def greet(g, s, groups, seqs, across):
    barrier = pltpu.get_barrier_semaphore()
    if across:
        for k in range(1, groups):
            pl.semaphore_signal(
                barrier, inc=1, device_id={"grp": lax.rem(g + k, groups), "seq": s}, device_id_type=MESH
            )
    for k in range(1, seqs):
        pl.semaphore_signal(
            barrier, inc=1, device_id={"grp": g, "seq": lax.rem(s + k, seqs)}, device_id_type=MESH
        )
    pl.semaphore_wait(barrier, seqs - 1 + (groups - 1 if across else 0))


def fill_table(routes, route_weights, table):
    experts = lax.broadcasted_iota(jnp.int32, table.shape, 0)
    given = route_weights[...]
    shares = given / jnp.sum(given, axis=0, keepdims=True)
    chosen = routes[...]
    table[...] = sum(
        jnp.where(experts == chosen[k : k + 1], shares[k : k + 1], 0.0) for k in range(chosen.shape[0])
    )


class Gather:
    def __init__(self, g, s, groups, seqs, shard, whole, rows, by_lanes, deep, own_sem, send_sem, recv_sem):
        self.g, self.s, self.groups = g, s, groups
        self.shard, self.whole, self.by_lanes = shard, whole, by_lanes
        self.own_sem, self.send_sem, self.recv_sem = own_sem, send_sem, recv_sem
        self.first, self.rows = rows
        self.routed = groups == 4
        self.deep = deep and self.routed and seqs % 4 == 0
        core, plane = lax.rem(s, 2), lax.rem(s // 2, 2)
        self.other = s + 1 - 2 * core
        self.paired = s + 2 - 4 * plane
        if self.deep:
            self.size = self.rows // 4
            self.start = self.first + (plane * 2 + core) * self.size
            self.paired_start = self.first + ((1 - plane) * 2 + core) * self.size
        else:
            self.size = self.rows // 2
            self.start = self.first + core * self.size
        self.cut = (self.size // 2 + 15) // 16 * 16
        self.copies = {}

    def part(self, group, first, count):
        if self.by_lanes:
            columns = self.shard.shape[1]
            start = pl.multiple_of(group * columns, 128)
            return self.whole.at[pl.ds(pl.multiple_of(first, 16), count), pl.ds(start, columns)]
        return self.whole.at[pl.ds(pl.multiple_of(group * self.shard.shape[0] + first, 16), count)]

    def source(self, first, count):
        return self.shard.at[pl.ds(pl.multiple_of(first, 16), count)]

    def send(self, event, source, target, grp, seq):
        copy = pltpu.make_async_remote_copy(
            src_ref=source,
            dst_ref=target,
            send_sem=self.send_sem.at[event],
            recv_sem=self.recv_sem.at[event],
            device_id={"grp": grp, "seq": seq},
            device_id_type=MESH,
        )
        copy.start()
        self.copies[event] = copy

    def pass_on(self, event, part, grp, seq):
        self.send(event, part, part, grp, seq)

    def got(self, *events):
        for event in events:
            self.copies[event].wait_recv()

    def xor(self, k):
        if k == 1:
            return self.g + 1 - 2 * lax.rem(self.g, 2)
        if k == 2:
            return lax.rem(self.g + 2, 4)
        return 3 - self.g

    def begin(self):
        if self.routed:
            for event, k in ((0, 1), (1, 2)):
                self.send(
                    event,
                    self.source(self.start, self.size),
                    self.part(self.g, self.start, self.size),
                    self.xor(k),
                    self.s,
                )
        else:
            for k in range(1, self.groups):
                self.send(
                    k - 1,
                    self.source(self.first, self.rows),
                    self.part(self.g, self.first, self.rows),
                    lax.rem(self.g + k, self.groups),
                    self.s,
                )
        self.own = pltpu.make_async_copy(
            self.source(self.first, self.rows), self.part(self.g, self.first, self.rows), self.own_sem
        )
        self.own.start()

    def forward(self):
        if not self.routed:
            return
        x, y = self.xor(1), self.xor(2)
        self.got(0, 1)
        self.pass_on(2, self.part(y, self.start, self.cut), x, self.s)
        self.pass_on(3, self.part(x, self.start + self.cut, self.size - self.cut), y, self.s)
        for event, k in ((0, x), (1, y)):
            near = self.part(k, self.start, self.size)
            if self.deep:
                self.pass_on(7 + event, near, self.g, self.paired)
            self.pass_on(4 + event, near, self.g, self.other)

    def share(self):
        if not self.routed:
            return
        self.got(2, 3)
        far = self.part(self.xor(3), self.start, self.size)
        if self.deep:
            self.pass_on(9, far, self.g, self.paired)
        self.pass_on(6, far, self.g, self.other)

    def relay(self):
        if not self.deep:
            return
        for event, k in ((0, 1), (1, 2), (2, 3)):
            self.got(7 + event)
            self.pass_on(10 + event, self.part(self.xor(k), self.paired_start, self.size), self.g, self.other)

    def end(self):
        self.own.wait()
        if self.deep:
            self.got(4, 5, 6, 10, 11, 12)
        elif self.routed:
            self.got(4, 5, 6)
        else:
            self.got(*range(self.groups - 1))

    def drain(self):
        for copy in self.copies.values():
            copy.wait_send()


class PairShare:
    def __init__(self, g, s, shard, whole, first, rows, send_sem, recv_sem):
        self.g, self.s, self.shard, self.whole = g, s, shard, whole
        self.send_sem, self.recv_sem = send_sem, recv_sem
        core, plane = lax.rem(s, 2), lax.rem(s // 2, 2)
        self.other, self.paired = s + 1 - 2 * core, s + 2 - 4 * plane
        self.size = rows // 4
        self.here = self.span(first + (plane * 2 + core) * self.size)
        self.there = self.span(first + ((1 - plane) * 2 + core) * self.size)
        self.copies = {}

    def span(self, first):
        return pl.ds(pl.multiple_of(first, 16), self.size)

    def send(self, event, source, rows, grp, seq):
        copy = pltpu.make_async_remote_copy(
            src_ref=source.at[rows],
            dst_ref=self.whole.at[rows],
            send_sem=self.send_sem.at[event],
            recv_sem=self.recv_sem.at[event],
            device_id={"grp": grp, "seq": seq},
            device_id_type=MESH,
        )
        copy.start()
        self.copies[event] = copy

    def begin(self):
        self.send(0, self.shard, self.here, lax.rem(self.g + 2, 4), self.s)

    def forward(self):
        self.copies[0].wait_recv()
        self.send(1, self.whole, self.here, self.g, self.paired)
        self.send(2, self.whole, self.here, self.g, self.other)

    def share(self):
        pass

    def relay(self):
        self.copies[1].wait_recv()
        self.send(3, self.whole, self.there, self.g, self.other)

    def end(self):
        self.copies[2].wait_recv()
        self.copies[3].wait_recv()

    def drain(self):
        for copy in self.copies.values():
            copy.wait_send()


def encoder_kernel(
    groups,
    seqs,
    audio_block,
    ids,
    gain,
    moe_gain,
    routes,
    route_weights,
    qkv_shard,
    out_shard,
    adapter_shard,
    thinker,
    expert_in,
    tables,
    qkv_w,
    out_w,
    adapter_w,
    normed,
    query,
    pairs,
    ids_ext,
    table,
    attended,
    even,
    odd,
    own_sem,
    weight_send,
    weight_recv,
    edge_send,
    edge_recv,
    tab_send,
    tab_recv,
):
    g, s = lax.axis_index("grp"), lax.axis_index("seq")
    audio = audio_block.at[0]
    frames, width = audio.shape
    heads_pairs = width // 128
    blocks = frames // EDGE
    fill_table(routes, route_weights, table)
    for b in range(blocks):
        ids_ext[b + 1] = jnp.broadcast_to(ids[0:1, b * EDGE : (b + 1) * EDGE], (8, EDGE))
    greet(g, s, groups, seqs, True)

    def gather(i, shard, whole, rows, by_lanes, deep):
        return Gather(
            g, s, groups, seqs, shard, whole, rows, by_lanes, deep, own_sem.at[i], weight_send.at[i], weight_recv.at[i]
        )

    def split(rows, at):
        return (0, at), (at, rows - at)

    qkv_rows, ad_rows = qkv_shard.shape[0], adapter_shard.shape[0]
    qkv_deep, qkv_plain = split(qkv_rows, (qkv_rows // 2 + 63) // 64 * 64)
    ad_deep, ad_plain = split(ad_rows, ad_rows // 2)
    qkv_a = gather(0, qkv_shard, qkv_w, qkv_deep, False, True)
    qkv_b = gather(1, qkv_shard, qkv_w, qkv_plain, False, False)
    out = gather(2, out_shard, out_w, (0, out_shard.shape[0]), False, False)
    ad_a = gather(3, adapter_shard, adapter_w, ad_deep, True, True)
    ad_b = gather(4, adapter_shard, adapter_w, ad_plain, True, False)
    qkv_a.begin()
    qkv_b.begin()

    table_copies = []
    for k in range(1, seqs):
        copy = pltpu.make_async_remote_copy(
            src_ref=table,
            dst_ref=tables.at[s],
            send_sem=tab_send.at[k - 1],
            recv_sem=tab_recv.at[k - 1],
            device_id={"grp": g, "seq": lax.rem(s + k, seqs)},
            device_id_type=MESH,
        )
        copy.start()
        table_copies.append(copy)
    tables[s] = table[...]

    def edge(event, source, target, step):
        return pltpu.make_async_remote_copy(
            src_ref=source,
            dst_ref=target,
            send_sem=edge_send.at[event],
            recv_sem=edge_recv.at[event],
            device_id={"grp": g, "seq": lax.rem(s + step + seqs, seqs)},
            device_id_type=MESH,
        )

    ids_right = edge(0, ids_ext.at[blocks], ids_ext.at[0], 1)
    ids_left = edge(1, ids_ext.at[1], ids_ext.at[blocks + 1], -1)
    pairs_right = edge(2, pairs.at[pl.ds(frames, EDGE)], pairs.at[pl.ds(0, EDGE)], 1)
    pairs_left = edge(3, pairs.at[pl.ds(EDGE, EDGE)], pairs.at[pl.ds(frames + EDGE, EDGE)], -1)
    has_left, has_right = s > 0, s < seqs - 1

    @pl.when(has_right)
    def _():
        ids_right.start()

    @pl.when(has_left)
    def _():
        ids_left.start()

    @pl.when(s == 0)
    def _():
        ids_ext[0] = jnp.full(ids_ext.shape[1:], -1, jnp.int32)
        pairs[0:EDGE] = jnp.zeros((EDGE, pairs.shape[1]), BF16)

    @pl.when(s == seqs - 1)
    def _():
        ids_ext[blocks + 1] = jnp.full(ids_ext.shape[1:], -1, jnp.int32)
        pairs[frames + EDGE :] = jnp.zeros((EDGE, pairs.shape[1]), BF16)

    def norm_rows(i, _):
        rows = pl.ds(pl.multiple_of(i * 64, 64), 64)
        signal = audio[rows].astype(F32)
        centred = signal - jnp.mean(signal, axis=-1, keepdims=True)
        variance = jnp.mean(centred * centred, axis=-1, keepdims=True)
        normed[rows] = (centred * lax.rsqrt(variance + LN_EPSILON) * gain[...]).astype(BF16)
        return 0

    lax.fori_loop(0, frames // 64, norm_rows, 0)

    qkv_a.forward()
    qkv_b.forward()
    out.begin()
    ad_a.begin()
    qkv_a.share()
    qkv_b.share()
    qkv_a.relay()
    qkv_a.end()
    qkv_b.end()

    tile = 256

    def project_pairs(i, _):
        source = pl.ds(pl.multiple_of(width + i * tile, tile), tile)
        columns = pl.ds(pl.multiple_of(i * tile, tile), tile)
        pairs[EDGE : EDGE + frames, columns] = lax.dot_general(
            normed[...], qkv_w[source], NT, preferred_element_type=F32
        ).astype(BF16)
        return 0

    lax.fori_loop(0, 2 * width // tile, project_pairs, 0)

    @pl.when(has_right)
    def _():
        pairs_right.start()

    @pl.when(has_left)
    def _():
        pairs_left.start()

    out.forward()
    ad_b.begin()

    def project_query(i, _):
        columns = pl.ds(pl.multiple_of(i * tile, tile), tile)
        query[:, columns] = lax.dot_general(
            normed[...], qkv_w[columns], NT, preferred_element_type=F32
        ).astype(BF16)
        return 0

    lax.fori_loop(0, width // tile, project_query, 0)
    out.share()
    ad_a.forward()

    @pl.when(has_left)
    def _():
        ids_right.wait_recv()
        pairs_right.wait_recv()

    @pl.when(has_right)
    def _():
        ids_left.wait_recv()
        pairs_left.wait_recv()

    low = lax.broadcasted_iota(jnp.int32, (EDGE, 128), 1) < HEAD
    span = 3 * EDGE
    for b in range(blocks):
        rows = slice(b * EDGE, (b + 1) * EDGE)
        keys = slice(b * EDGE, b * EDGE + span)
        key_ids = jnp.concatenate([ids_ext[b + j][0:1] for j in range(3)], axis=1)
        frame_ids = jnp.broadcast_to(ids_ext[b + 1][0:1], (EDGE, EDGE)).T[:, 0:1]
        same = frame_ids == key_ids
        allowed = jnp.concatenate([same, same], axis=0)

        def attend(p, _, rows=rows, keys=keys, allowed=allowed):
            columns = pl.ds(pl.multiple_of(p * 128, 128), 128)
            both = query[rows, columns]
            nothing = jnp.zeros_like(both)
            stacked = jnp.concatenate(
                [jnp.where(low, both, nothing), jnp.where(low, nothing, both)], axis=0
            )
            scores = lax.dot_general(
                stacked, pairs[keys, columns], NT, preferred_element_type=F32
            ) * HEAD ** (-0.5)
            scores = jnp.where(allowed, scores, MASKED)
            highest = jnp.max(scores, axis=-1, keepdims=True)
            exponent = jnp.exp(scores - highest)
            total = jnp.sum(exponent, axis=-1, keepdims=True)
            value_columns = pl.ds(pl.multiple_of(width + p * 128, 128), 128)
            mixed = jnp.dot(
                (exponent / total).astype(BF16), pairs[keys, value_columns], preferred_element_type=F32
            )
            attended[rows, columns] = jnp.where(low, mixed[:EDGE], mixed[EDGE:]).astype(BF16)
            return 0

        lax.fori_loop(0, heads_pairs, attend, 0)

    out.end()
    tokens = frames // 2
    at_row = lax.broadcasted_iota(jnp.int32, (tokens, frames), 0)
    at_frame = lax.broadcasted_iota(jnp.int32, (tokens, frames), 1)
    first = jnp.where(at_frame == 2 * at_row, 1.0, 0.0).astype(BF16)
    second = jnp.where(at_frame == 2 * at_row + 1, 1.0, 0.0).astype(BF16)

    def encode(i, _):
        columns = pl.ds(pl.multiple_of(i * tile, tile), tile)
        projected = lax.dot_general(attended[...], out_w[columns], NT, preferred_element_type=F32)
        encoded = (audio[:, columns].astype(F32) + projected).astype(BF16)
        even[:, columns] = jnp.dot(first, encoded, preferred_element_type=F32).astype(BF16)
        odd[:, columns] = jnp.dot(second, encoded, preferred_element_type=F32).astype(BF16)
        return 0

    lax.fori_loop(0, width // tile, encode, 0)
    ad_b.forward()
    ad_a.share()
    ad_a.relay()
    ad_b.share()
    ad_a.end()
    ad_b.end()

    def adapt(i, _):
        columns = pl.ds(pl.multiple_of(i * tile, tile), tile)
        thinker[:, columns] = (
            jnp.dot(even[...], adapter_w[0:width, columns], preferred_element_type=F32)
            + jnp.dot(odd[...], adapter_w[width:, columns], preferred_element_type=F32)
        ).astype(BF16)
        return 0

    lax.fori_loop(0, thinker.shape[1] // tile, adapt, 0)

    def rms_rows(i, _):
        rows = pl.ds(pl.multiple_of(i * 32, 32), 32)
        widened = thinker[rows].astype(F32)
        squares = jnp.mean(widened * widened, axis=-1, keepdims=True)
        expert_in[rows] = (widened * lax.rsqrt(squares + RMS_EPSILON) * moe_gain[...]).astype(BF16)
        return 0

    lax.fori_loop(0, tokens // 32, rms_rows, 0)

    for copy in table_copies:
        copy.wait()
    for weight in (qkv_a, qkv_b, out, ad_a, ad_b):
        weight.drain()

    @pl.when(has_right)
    def _():
        ids_right.wait_send()
        pairs_right.wait_send()

    @pl.when(has_left)
    def _():
        ids_left.wait_send()
        pairs_left.wait_send()


def fused_kernel(
    groups,
    seqs,
    audio_block,
    ids,
    gain,
    moe_gain,
    routes,
    route_weights,
    qkv_shard,
    out_shard,
    adapter_shard,
    gate_hbm,
    up_hbm,
    down_hbm,
    result,
    thinker,
    expert_in,
    tables,
    *scratch,
):
    def prepare(start_loads):
        return encode_tokens(
            start_loads,
            groups,
            seqs,
            audio_block,
            ids,
            gain,
            moe_gain,
            routes,
            route_weights,
            qkv_shard,
            out_shard,
            adapter_shard,
            thinker,
            expert_in,
            tables,
            *scratch[:32],
        )

    expert_kernel(
        seqs, expert_in, thinker, tables, gate_hbm, up_hbm, down_hbm, result, *scratch[32:], prepare=prepare
    )


def encode_tokens(
    start_loads,
    groups,
    seqs,
    audio_hbm,
    ids_hbm,
    gain_hbm,
    moe_gain_hbm,
    routes_hbm,
    route_weights_hbm,
    qkv_shard,
    out_shard,
    adapter_shard,
    thinker,
    expert_in,
    tables,
    audio,
    ids,
    gain,
    moe_gain,
    routes,
    route_weights,
    input_sem,
    qkv_w,
    out_w,
    adapter_w,
    normed,
    query,
    pairs,
    halo,
    ids_ext,
    table,
    attended,
    pooled,
    partner,
    produced,
    adapter_sem,
    own_sem,
    weight_send,
    weight_recv,
    pair_send,
    pair_recv,
    swap_send,
    swap_recv,
    edge_send,
    edge_recv,
    tab_send,
    tab_recv,
):
    g, s = lax.axis_index("grp"), lax.axis_index("seq")
    frames, width = audio.shape
    blocks = frames // EDGE
    inputs = [
        pltpu.make_async_copy(source, target, input_sem.at[i])
        for i, (source, target) in enumerate(
            (
                (audio_hbm.at[0], audio),
                (ids_hbm, ids),
                (gain_hbm, gain),
                (moe_gain_hbm, moe_gain),
                (routes_hbm, routes),
                (route_weights_hbm, route_weights),
            )
        )
    ]
    for load in inputs:
        load.start()
    greet(g, s, groups, seqs, True)

    def gather(i, shard, whole, first, rows, deep, by_lanes=False):
        return Gather(
            g, s, groups, seqs, shard, whole, (first, rows), by_lanes, deep,
            own_sem.at[i], weight_send.at[i], weight_recv.at[i],
        )

    items, count = [], 0
    for shard, whole, by_lanes, plan in (
        (qkv_shard, qkv_w, False, QKV_PLAN),
        (out_shard, out_w, False, OUT_PLAN),
    ):
        units, first = sum(sum(pair) for pair in plan), 0
        for pair in plan:
            item = []
            for deep, share in ((True, pair[0]), (False, pair[1])):
                if share:
                    rows = shard.shape[0] * share // units
                    item.append(gather(count, shard, whole, first, rows, deep, by_lanes))
                    first, count = first + rows, count + 1
            items.append(item)
    stripe = adapter_shard.shape[0] // ADAPTER_PARTS
    for k in range(ADAPTER_PARTS):
        items.append(
            [PairShare(g, s, adapter_shard, adapter_w.at[1], k * stripe, stripe, pair_send.at[k], pair_recv.at[k])]
        )
    own_adapter = pltpu.make_async_copy(adapter_shard, adapter_w.at[0], adapter_sem)

    def steps(point):
        for what, k in STEPS[point]:
            for one in items[k]:
                getattr(one, what)()

    steps(0)

    def edge(event, source, target, step):
        return pltpu.make_async_remote_copy(
            src_ref=source,
            dst_ref=target,
            send_sem=edge_send.at[event],
            recv_sem=edge_recv.at[event],
            device_id={"grp": g, "seq": lax.rem(s + step + seqs, seqs)},
            device_id_type=MESH,
        )

    ids_right = edge(0, ids_ext.at[blocks], ids_ext.at[0], 1)
    ids_left = edge(1, ids_ext.at[1], ids_ext.at[blocks + 1], -1)
    halo_right = edge(2, audio_hbm.at[0, pl.ds(frames - HALO, HALO)], halo.at[0], 1)
    halo_left = edge(3, audio_hbm.at[0, pl.ds(0, HALO)], halo.at[1], -1)
    has_left, has_right = s > 0, s < seqs - 1

    @pl.when(has_right)
    def _():
        halo_right.start()

    @pl.when(has_left)
    def _():
        halo_left.start()

    steps(1)
    for load in inputs:
        load.wait()
    for b in range(blocks):
        ids_ext[b + 1] = jnp.broadcast_to(ids[0:1, b * EDGE : (b + 1) * EDGE], (8, EDGE))

    @pl.when(has_right)
    def _():
        ids_right.start()

    @pl.when(has_left)
    def _():
        ids_left.start()

    fill_table(routes, route_weights, table)
    table_copies = []
    for k in range(1, seqs):
        copy = pltpu.make_async_remote_copy(
            src_ref=table,
            dst_ref=tables.at[s],
            send_sem=tab_send.at[k - 1],
            recv_sem=tab_recv.at[k - 1],
            device_id={"grp": g, "seq": lax.rem(s + k, seqs)},
            device_id_type=MESH,
        )
        copy.start()
        table_copies.append(copy)
    tables[s] = table[...]
    own_adapter.start()
    start_loads()

    @pl.when(s == 0)
    def _():
        ids_ext[0] = jnp.full(ids_ext.shape[1:], -1, jnp.int32)
        halo[0] = jnp.zeros(halo.shape[1:], BF16)

    @pl.when(s == seqs - 1)
    def _():
        ids_ext[blocks + 1] = jnp.full(ids_ext.shape[1:], -1, jnp.int32)
        halo[1] = jnp.zeros(halo.shape[1:], BF16)

    def layer_norm(signal):
        signal = signal.astype(F32)
        centred = signal - jnp.mean(signal, axis=-1, keepdims=True)
        variance = jnp.mean(centred * centred, axis=-1, keepdims=True)
        return (centred * lax.rsqrt(variance + LN_EPSILON) * gain[...]).astype(BF16)

    def norm_rows(i, _):
        rows = pl.multiple_of(i * 64, 64)
        normed[pl.ds(EDGE + rows, 64)] = layer_norm(audio[pl.ds(rows, 64)])
        return 0

    lax.fori_loop(0, frames // 64, norm_rows, 0)
    spare = jnp.zeros((EDGE - HALO, width), BF16)
    normed[0 : EDGE - HALO] = spare
    normed[frames + EDGE + HALO :] = spare
    steps(2)

    @pl.when(has_left)
    def _():
        ids_right.wait_recv()
        halo_right.wait_recv()

    @pl.when(has_right)
    def _():
        ids_left.wait_recv()
        halo_left.wait_recv()

    def norm_halo(i, _):
        rows = pl.multiple_of(i * 16, 16)
        normed[pl.ds(EDGE - HALO + rows, 16)] = layer_norm(halo[0, pl.ds(rows, 16)])
        normed[pl.ds(EDGE + frames + rows, 16)] = layer_norm(halo[1, pl.ds(rows, 16)])
        return 0

    lax.fori_loop(0, HALO // 16, norm_halo, 0)
    steps(3)
    tile = 256

    def project_pairs(i, _):
        source = pl.ds(pl.multiple_of(width + i * tile, tile), tile)
        columns = pl.ds(pl.multiple_of(i * tile, tile), tile)
        pairs[:, columns] = lax.dot_general(
            normed[...], qkv_w[source], NT, preferred_element_type=F32
        ).astype(BF16)
        return 0

    half = width // tile
    lax.fori_loop(0, half, project_pairs, 0)
    steps(4)
    lax.fori_loop(half, 2 * half, project_pairs, 0)
    steps(5)

    def project_query(i, _):
        columns = pl.ds(pl.multiple_of(i * tile, tile), tile)
        query[:, columns] = lax.dot_general(
            normed[EDGE : EDGE + frames], qkv_w[columns], NT, preferred_element_type=F32
        ).astype(BF16) * BF16(HEAD ** (-0.5))
        return 0

    lax.fori_loop(0, half, project_query, 0)
    steps(6)
    low = lax.broadcasted_iota(jnp.int32, (EDGE, 128), 1) < HEAD
    span = 3 * EDGE
    for b in range(blocks):
        rows = slice(b * EDGE, (b + 1) * EDGE)
        keys = slice(b * EDGE, b * EDGE + span)
        key_ids = jnp.concatenate([ids_ext[b + j][0:1] for j in range(3)], axis=1)
        frame_ids = jnp.broadcast_to(ids_ext[b + 1][0:1], (EDGE, EDGE)).T[:, 0:1]
        same = frame_ids == key_ids
        allowed = jnp.concatenate([same, same], axis=0)

        def attend(p, _, rows=rows, keys=keys, allowed=allowed):
            columns = pl.ds(pl.multiple_of(p * 128, 128), 128)
            both = query[rows, columns]
            nothing = jnp.zeros_like(both)
            stacked = jnp.concatenate(
                [jnp.where(low, both, nothing), jnp.where(low, nothing, both)], axis=0
            )
            scores = lax.dot_general(stacked, pairs[keys, columns], NT, preferred_element_type=F32)
            scores = jnp.where(allowed, scores, MASKED)
            highest = jnp.max(scores, axis=-1, keepdims=True)
            exponent = jnp.exp(scores - highest)
            total = jnp.sum(exponent, axis=-1, keepdims=True)
            value_columns = pl.ds(pl.multiple_of(width + p * 128, 128), 128)
            mixed = jnp.dot(
                exponent.astype(BF16), pairs[keys, value_columns], preferred_element_type=F32
            ) / total
            attended[rows, columns] = jnp.where(low, mixed[:EDGE], mixed[EDGE:]).astype(BF16)
            return 0

        heads_pairs = width // 128
        cuts = [heads_pairs * k // 4 for k in range(5)]
        for k in range(4):
            lax.fori_loop(cuts[k], cuts[k + 1], attend, 0)
            steps(7 + 4 * b + k)

    for one in items[len(QKV_PLAN)]:
        one.end()
    steps(15)
    tokens = frames // 2
    part = tokens // 2
    x, y = g + 1 - 2 * lax.rem(g, 2), lax.rem(g + 2, 4)
    columns_here = adapter_shard.shape[1]
    at_row = lax.broadcasted_iota(jnp.int32, (part, EDGE), 0)
    at_frame = lax.broadcasted_iota(jnp.int32, (part, EDGE), 1)
    first = jnp.where(at_frame == 2 * at_row, 1.0, 0.0).astype(BF16)
    second = jnp.where(at_frame == 2 * at_row + 1, 1.0, 0.0).astype(BF16)

    def encode_block(b):
        rows, out_rows = slice(b * EDGE, (b + 1) * EDGE), slice(b * part, (b + 1) * part)

        def encode(i, _):
            columns = pl.ds(pl.multiple_of(i * tile, tile), tile)
            projected = lax.dot_general(attended[rows], out_w[columns], NT, preferred_element_type=F32)
            encoded = (audio[rows, columns].astype(F32) + projected).astype(BF16)
            pooled[out_rows, columns] = jnp.dot(first, encoded, preferred_element_type=F32).astype(BF16)
            pooled[out_rows, pl.ds(pl.multiple_of(width + i * tile, tile), tile)] = jnp.dot(
                second, encoded, preferred_element_type=F32
            ).astype(BF16)
            return 0

        lax.fori_loop(0, half, encode, 0)

    def to_partner(event, source, target):
        return pltpu.make_async_remote_copy(
            src_ref=source,
            dst_ref=target,
            send_sem=swap_send.at[event],
            recv_sem=swap_recv.at[event],
            device_id={"grp": x, "seq": s},
            device_id_type=MESH,
        )

    piece = part // PIECES
    batches = [(0, part)] + [(part + k * piece, piece) for k in range(PIECES)]
    spreads = [
        to_partner(event, pooled.at[pl.ds(start, rows)], partner.at[pl.ds(start, rows)])
        for event, (start, rows) in enumerate(batches)
    ]

    def shard_columns(k):
        return pl.ds(pl.multiple_of((g, y)[k] * columns_here, 128), columns_here)

    def give_back(b, k):
        rows = pl.ds(*batches[b])
        return to_partner(len(batches) + 2 * b + k, produced.at[k, rows], thinker.at[rows, shard_columns(k)])

    backs = [[give_back(b, k) for k in range(2)] for b in range(len(batches))]

    def project(b):
        count = batches[b][1]
        rows = slice(batches[b][0], batches[b][0] + count)
        spreads[b].wait_recv()
        for k in range(2):

            def one(i, _, k=k):
                columns = pl.ds(pl.multiple_of(i * tile, tile), tile)
                batch = jnp.concatenate([pooled[rows], partner[rows]], axis=0)
                found = jnp.dot(batch, adapter_w[k, :, columns], preferred_element_type=F32).astype(BF16)
                start = pl.multiple_of((g, y)[k] * columns_here + i * tile, tile)
                thinker[rows, pl.ds(start, tile)] = found[:count]
                produced[k, rows, columns] = found[count:]
                return 0

            lax.fori_loop(0, columns_here // tile, one, 0)
            backs[b][k].start()

    def normalise(b):
        for back in backs[b]:
            back.wait_recv()

        def rms_rows(i, _):
            rows = pl.ds(pl.multiple_of(batches[b][0] + i * 32, 32), 32)
            widened = thinker[rows].astype(F32)
            squares = jnp.mean(widened * widened, axis=-1, keepdims=True)
            expert_in[rows] = (widened * lax.rsqrt(squares + RMS_EPSILON) * moe_gain[...]).astype(BF16)
            return 0

        lax.fori_loop(0, batches[b][1] // 32, rms_rows, 0)

    encode_block(0)
    spreads[0].start()
    steps(16)
    encode_block(1)
    spreads[1].start()
    steps(17)
    own_adapter.wait()
    steps(18)
    for one in sum(items[len(QKV_PLAN) + 1 :], []):
        one.end()
    project(0)
    project(1)
    spreads[2].start()
    normalise(0)

    for copy in table_copies:
        copy.wait()

    def finish():
        for weight in sum(items, []):
            weight.drain()
        for copy in spreads + sum(backs, []):
            copy.wait_send()

        @pl.when(has_right)
        def _():
            ids_right.wait_send()
            halo_right.wait_send()

        @pl.when(has_left)
        def _():
            ids_left.wait_send()
            halo_left.wait_send()

    return finish, project, normalise


def expert_kernel(
    seqs,
    expert_in,
    thinker,
    tables,
    gate_hbm,
    up_hbm,
    down_hbm,
    result,
    gate_w,
    up_w,
    down_w,
    tokens_all,
    hidden,
    mine,
    theirs,
    to_other,
    incoming,
    outgoing,
    load_sem,
    tok_send,
    tok_recv,
    half_send,
    half_recv,
    sum_send,
    sum_recv,
    share_of,
    prepare=None,
):
    g, s = lax.axis_index("grp"), lax.axis_index("seq")
    planes = seqs // 2
    z, c = s // 2, lax.rem(s, 2)
    other = 1 - c
    rows, width = expert_in.shape
    ff = gate_w.shape[1]
    loads = [
        pltpu.make_async_copy(source, target, load_sem.at[i])
        for i, (source, target) in enumerate(((gate_hbm, gate_w), (up_hbm, up_w), (down_hbm, down_w)))
    ]

    def start_loads():
        for load in loads:
            load.start()

    if prepare is None:
        start_loads()
        greet(g, s, 1, seqs, False)
    else:
        settle, project, normalise = prepare(start_loads)

    part = rows // 2

    piece = part // PIECES

    def span(h):
        return pl.ds(pl.multiple_of(h * part, part), part)

    def strip(h, k):
        return pl.ds(pl.multiple_of(h * part + k * piece, piece), piece)

    def move(source, target, send, recv, plane, core):
        return pltpu.make_async_remote_copy(
            src_ref=source,
            dst_ref=target,
            send_sem=send,
            recv_sem=recv,
            device_id={"grp": g, "seq": plane * 2 + core},
            device_id_type=MESH,
        )

    def token_copy(side, origin, h, k, plane, own=False):
        slot = tokens_all.at[origin, c, strip(h, k)]
        source = expert_in.at[strip(h, k)] if own else slot
        event = h * PIECES + k
        return move(source, slot, tok_send.at[side, origin, event], tok_recv.at[0, origin, event], plane, c)

    def other_copy(origin, h, k, own=False):
        slot = tokens_all.at[origin, c, strip(h, k)]
        source = expert_in.at[strip(h, k)] if own else slot
        event = h * PIECES + k
        return move(source, slot, tok_send.at[2, origin, event], tok_recv.at[1, origin, event], z, other)

    def own_tokens(side, h, *pieces):
        for k in pieces or range(PIECES):
            token_copy(side, z, h, k, z + 1 - 2 * side, True).start()

    def own_other(h, *pieces):
        for k in pieces or range(PIECES):
            other_copy(z, h, k, True).start()

    def second_half(k):
        if prepare is not None:
            normalise(1 + k)
        for side in range(2):

            @pl.when((z == planes - 1, z == 0)[1 - side])
            def _(side=side):
                own_tokens(side, 1, k)

        own_other(1, k)
        here = slice(part + k * piece, part + (k + 1) * piece)
        tokens_all[z, c, here] = expert_in[here]

    def half_copy(origin, h):
        return move(
            to_other.at[origin, span(h)],
            theirs.at[origin, span(h)],
            half_send.at[origin, h],
            half_recv.at[origin, h],
            z,
            other,
        )

    def sum_copy(side, target, h, k, plane):
        return move(
            outgoing.at[side, target, strip(h, k)],
            incoming.at[side, target, strip(h, k)],
            sum_send.at[side, target, h * PIECES + k],
            sum_recv.at[side, target, h * PIECES + k],
            plane,
            c,
        )

    has_above, has_below = z < planes - 1, z > 0

    @pl.when(has_above)
    def _():
        own_tokens(0, 0)

    @pl.when(has_below)
    def _():
        own_tokens(1, 0)

    own_other(0)
    tokens_all[z, c, 0:part] = expert_in[0:part]
    second_half(0)
    for load in loads:
        load.wait()
    for k in range(seqs):
        share_of[k] = jnp.broadcast_to(tables[k, pl.ds(s, 1)], (128, rows)).T
    rise_tile = 384 if ff % 384 == 0 else 128
    fall_tile = 512 if width % 512 == 0 else 128

    def experts(origin, h):
        for k in range(PIECES):
            other_copy(origin, h, k).wait_recv()

        def rise(i, _):
            columns = pl.ds(pl.multiple_of(i * rise_tile, rise_tile), rise_tile)
            batch = tokens_all[origin, :, span(h)].reshape(2 * part, width)
            gate = jnp.dot(batch, gate_w[:, columns], preferred_element_type=F32)
            up = jnp.dot(batch, up_w[:, columns], preferred_element_type=F32)
            hidden[:, columns] = (gate / (1.0 + jnp.exp(-gate)) * up).astype(BF16)
            return 0

        lax.fori_loop(0, ff // rise_tile, rise, 0)
        share = jnp.concatenate([share_of[origin * 2 + k, span(h), 0:1] for k in range(2)], axis=0)

        def fall(i, _):
            columns = pl.ds(pl.multiple_of(i * fall_tile, fall_tile), fall_tile)
            produced = jnp.dot(hidden[...], down_w[:, columns], preferred_element_type=F32)
            weighted = (produced.astype(BF16).astype(F32) * share).astype(BF16)
            mine[origin, span(h), columns] = jnp.where(c == 0, weighted[:part], weighted[part:])
            to_other[origin, span(h), columns] = jnp.where(c == 0, weighted[part:], weighted[:part])
            return 0

        lax.fori_loop(0, width // fall_tile, fall, 0)
        half_copy(origin, h).start()

    def take(side, origin, h):
        for k in range(PIECES):
            token_copy(side, origin, h, k, z).wait_recv()

            @pl.when(jnp.where(side == 0, has_above, has_below))
            def _(k=k):
                token_copy(side, origin, h, k, z + 1 - 2 * side).start()

            other_copy(origin, h, k).start()

    def send_sum(side, origin, h, starts):
        half_copy(origin, h).wait_recv()
        for k in range(PIECES):
            here = strip(h, k)
            total = mine[origin, here].astype(F32) + theirs[origin, here].astype(F32)

            @pl.when(starts)
            def _(here=here, total=total):
                outgoing[side, origin, here] = total.astype(BF16)

            @pl.when(jnp.logical_not(starts))
            def _(here=here, total=total, k=k):
                sum_copy(side, origin, h, k, z).wait_recv()
                came = incoming[side, origin, here].astype(F32)
                outgoing[side, origin, here] = (total + came).astype(BF16)

            sum_copy(side, origin, h, k, z + 2 * side - 1).start()

    def arrival(side, t):
        reach = jnp.where(side == 0, z, planes - 1 - z)
        first = t <= reach
        distance = jnp.where(first, t, 2 * reach + 1 - t)
        valid = (t >= 1) & (t <= 2 * reach)
        return z + (2 * side - 1) * distance, jnp.where(first, 0, 1), valid, t == 2 * reach

    ends = (z == planes - 1, z == 0)
    experts(z, 0)
    if prepare is not None:
        project(2)

    def slot(t, _):
        for side in range(2):
            origin, h, valid, last = arrival(side, t)

            @pl.when(valid)
            def _(side=side, origin=origin, h=h):
                take(side, origin, h)

            @pl.when(last & (has_above, has_below)[side])
            def _(side=side):
                own_tokens(side, 1)

        for side in range(2):
            passed = jnp.where(side == 0, planes - 1 - z, z)
            origin, h, valid, _ = arrival(side, t - 2 * passed - 1)

            @pl.when(valid)
            def _(side=side, origin=origin, h=h):
                send_sum(side, origin, h, ends[side])

        @pl.when(t == 1)
        def _():
            for k in range(1, PIECES):
                second_half(k)

        def compute(j, _):
            side = jnp.where(z >= planes // 2, j, 1 - j)
            origin, h, valid, _ = arrival(side, t)
            own = j == 2
            now = t == jnp.where(ends[0] | ends[1], 1, 2 * planes - 3)

            @pl.when(jnp.where(own, now, valid))
            def _():
                experts(jnp.where(own, z, origin), jnp.where(own, 1, h))

            return 0

        lax.fori_loop(0, 3, compute, 0)
        return 0

    lax.fori_loop(1, 2 * planes, slot, 0)

    @pl.when(z == 0)
    def _():
        incoming[1, z] = jnp.zeros((rows, width), BF16)

    @pl.when(z == planes - 1)
    def _():
        incoming[0, z] = jnp.zeros((rows, width), BF16)

    for h in range(2):
        half_copy(z, h).wait_recv()

        @pl.when(has_below)
        def _(h=h):
            for k in range(PIECES):
                sum_copy(1, z, h, k, z).wait_recv()

        @pl.when(has_above)
        def _(h=h):
            for k in range(PIECES):
                sum_copy(0, z, h, k, z).wait_recv()

        def finish(i, _, h=h):
            here = pl.ds(pl.multiple_of(h * part + i * 32, 32), 32)
            total = thinker[here].astype(F32) + mine[z, here].astype(F32) + theirs[z, here].astype(F32)
            total = total + incoming[0, z, here].astype(F32) + incoming[1, z, here].astype(F32)
            result[here] = total.astype(BF16)
            return 0

        lax.fori_loop(0, part // 32, finish, 0)

    def drain(origin, _):
        for h in range(2):
            half_copy(origin, h).wait_send()
            for k in range(PIECES):
                other_copy(origin, h, k).wait_send()

                @pl.when((origin <= z) & has_above)
                def _(h=h, k=k):
                    token_copy(0, origin, h, k, z).wait_send()

                @pl.when((origin >= z) & has_below)
                def _(h=h, k=k):
                    token_copy(1, origin, h, k, z).wait_send()

                @pl.when(origin > z)
                def _(h=h, k=k):
                    sum_copy(1, origin, h, k, z).wait_send()

                @pl.when(origin < z)
                def _(h=h, k=k):
                    sum_copy(0, origin, h, k, z).wait_send()

        return 0

    lax.fori_loop(0, planes, drain, 0)
    if prepare is not None:
        settle()


def body(
    groups,
    seqs,
    audio,
    block_ids,
    norm_gain,
    qkv_weight,
    out_weight,
    adapter_weight,
    moe_gain,
    gate_weight,
    up_weight,
    down_weight,
    routes,
    route_weights,
):
    frames, width = audio.shape[1:]
    tokens, features = routes.shape[1], moe_gain.shape[0]
    blocks = frames // EDGE
    vmem = pl.BlockSpec(memory_space=pltpu.VMEM)
    anywhere = pl.BlockSpec(memory_space=pl.ANY)
    dma = pltpu.SemaphoreType.DMA
    events = max(13, groups - 1)
    planes = seqs // 2
    ff = gate_weight.shape[2]
    block = (planes, tokens, features)
    expert_scratch = [
        pltpu.VMEM((features, ff), BF16),
        pltpu.VMEM((features, ff), BF16),
        pltpu.VMEM((ff, features), BF16),
        pltpu.VMEM((planes, 2, tokens, features), BF16),
        pltpu.VMEM((tokens, ff), BF16),
        pltpu.VMEM(block, BF16),
        pltpu.VMEM(block, BF16),
        pltpu.VMEM(block, BF16),
        pltpu.VMEM((2,) + block, BF16),
        pltpu.VMEM((2,) + block, BF16),
        dma((3,)),
        dma((3, planes, 2 * PIECES)),
        dma((2, planes, 2 * PIECES)),
        dma((planes, 2)),
        dma((planes, 2)),
        dma((2, planes, 2 * PIECES)),
        dma((2, planes, 2 * PIECES)),
        pltpu.VMEM((seqs, tokens, 128), F32),
    ]
    expert_weights = (gate_weight[0], up_weight[0], down_weight[0])
    if groups == 4 and seqs == 8:
        gathers = sum(sum(1 for share in pair if share) for plan in (QKV_PLAN, OUT_PLAN) for pair in plan)
        result = pl.pallas_call(
            functools.partial(fused_kernel, groups, seqs),
            out_shape=jax.ShapeDtypeStruct((tokens, features), BF16),
            in_specs=[anywhere] * 12,
            out_specs=vmem,
            scratch_shapes=[
                pltpu.VMEM((tokens, features), BF16),
                pltpu.VMEM((tokens, features), BF16),
                pltpu.VMEM((seqs, seqs, tokens), F32),
                pltpu.VMEM((frames, width), BF16),
                pltpu.VMEM(block_ids.shape, jnp.int32),
                pltpu.VMEM(norm_gain.shape, F32),
                pltpu.VMEM(moe_gain.shape, F32),
                pltpu.VMEM(routes.shape[:0:-1], jnp.int32),
                pltpu.VMEM(routes.shape[:0:-1], F32),
                dma((6,)),
                pltpu.VMEM((3 * width, width), BF16),
                pltpu.VMEM((width, width), BF16),
                pltpu.VMEM((2,) + adapter_weight.shape, BF16),
                pltpu.VMEM((frames + 2 * EDGE, width), BF16),
                pltpu.VMEM((frames, width), BF16),
                pltpu.VMEM((frames + 2 * EDGE, 2 * width), BF16),
                pltpu.VMEM((2, HALO, width), BF16),
                pltpu.VMEM((blocks + 2, 8, EDGE), jnp.int32),
                pltpu.VMEM((seqs, tokens), F32),
                pltpu.VMEM((frames, width), BF16),
                pltpu.VMEM((tokens, 2 * width), BF16),
                pltpu.VMEM((tokens, 2 * width), BF16),
                pltpu.VMEM((2, tokens, adapter_weight.shape[1]), BF16),
                dma,
                dma((gathers,)),
                dma((gathers, events)),
                dma((gathers, events)),
                dma((ADAPTER_PARTS, 4)),
                dma((ADAPTER_PARTS, 4)),
                dma((3 * (1 + PIECES),)),
                dma((3 * (1 + PIECES),)),
                dma((4,)),
                dma((4,)),
                dma((seqs - 1,)),
                dma((seqs - 1,)),
            ]
            + expert_scratch,
            compiler_params=pltpu.CompilerParams(
                collective_id=2, has_side_effects=True, vmem_limit_bytes=VMEM_LIMIT
            ),
            name="fused",
        )(
            audio,
            block_ids,
            norm_gain,
            moe_gain,
            routes[0].T,
            route_weights[0].T,
            qkv_weight.T,
            out_weight.T,
            adapter_weight,
            *expert_weights,
        )
        return result[None]
    thinker, expert_in, tables = pl.pallas_call(
        functools.partial(encoder_kernel, groups, seqs),
        out_shape=(
            jax.ShapeDtypeStruct((tokens, features), BF16),
            jax.ShapeDtypeStruct((tokens, features), BF16),
            jax.ShapeDtypeStruct((seqs, seqs, tokens), F32),
        ),
        in_specs=[vmem] * 6 + [anywhere] * 3,
        out_specs=(vmem,) * 3,
        scratch_shapes=[
            pltpu.VMEM((3 * width, width), BF16),
            pltpu.VMEM((width, width), BF16),
            pltpu.VMEM((2 * width, features), BF16),
            pltpu.VMEM((frames, width), BF16),
            pltpu.VMEM((frames, width), BF16),
            pltpu.VMEM((frames + 2 * EDGE, 2 * width), BF16),
            pltpu.VMEM((blocks + 2, 8, EDGE), jnp.int32),
            pltpu.VMEM((seqs, tokens), F32),
            pltpu.VMEM((frames, width), BF16),
            pltpu.VMEM((frames // 2, width), BF16),
            pltpu.VMEM((frames // 2, width), BF16),
            dma((5,)),
            dma((5, events)),
            dma((5, events)),
            dma((4,)),
            dma((4,)),
            dma((seqs - 1,)),
            dma((seqs - 1,)),
        ],
        compiler_params=pltpu.CompilerParams(
            collective_id=0, has_side_effects=True, vmem_limit_bytes=VMEM_LIMIT
        ),
        name="encoder",
    )(
        audio,
        block_ids,
        norm_gain,
        moe_gain,
        routes[0].T,
        route_weights[0].T,
        qkv_weight.T,
        out_weight.T,
        adapter_weight,
    )
    result = pl.pallas_call(
        functools.partial(expert_kernel, seqs),
        out_shape=jax.ShapeDtypeStruct((tokens, features), BF16),
        in_specs=[vmem] * 3 + [anywhere] * 3,
        out_specs=vmem,
        scratch_shapes=expert_scratch,
        compiler_params=pltpu.CompilerParams(
            collective_id=1, has_side_effects=True, vmem_limit_bytes=VMEM_LIMIT
        ),
        name="experts",
    )(expert_in, thinker, tables, *expert_weights)
    return result[None]


def solution(mesh):
    placed = (
        P("grp", "seq", None),
        P("grp", "seq"),
        P(),
        P(None, "grp"),
        P(None, "grp"),
        P(None, "grp"),
        P(),
        P("seq", None, None),
        P("seq", None, None),
        P("seq", None, None),
        P("grp", "seq", None),
        P("grp", "seq", None),
    )
    return jax.shard_map(
        functools.partial(body, mesh.shape["grp"], mesh.shape["seq"]),
        mesh=mesh,
        in_specs=placed,
        out_specs=P("grp", "seq", None),
        check_vma=False,
    )
```

```python
import functools

import jax
import jax.numpy as jnp
from jax import lax
from jax.experimental import pallas as pl
from jax.experimental.pallas import tpu as pltpu
from jax.sharding import PartitionSpec as P

HEAD = 64
EDGE = 128
HALO = 112
PIECES = 2
QKV_PLAN = ((3, 0), (3, 0), (3, 0), (0, 6))
OUT_PLAN = ((3, 2),)
ADAPTER_PARTS = 5
STEPS = (
    (("begin", 0), ("begin", 1), ("begin", 2), ),
    (),
    (("begin", 3), ("forward", 0), ),
    (("forward", 1), ("forward", 2), ("forward", 3), ("share", 0), ("share", 1), ("begin", 4), ("relay", 0), ("share", 2), ("share", 3), ("relay", 3), ("relay", 1), ("relay", 2), ("begin", 5), ("end", 0), ("end", 1), ("end", 2), ("end", 3), ),
    (("forward", 4), ("begin", 8), ("begin", 9), ),
    (),
    (),
    (("begin", 7), ("begin", 6), ("share", 4), ),
    (("forward", 5), ),
    (),
    (),
    (("forward", 8), ("relay", 4), ),
    (),
    (("forward", 9), ),
    (),
    (),
    (("forward", 7), ),
    (),
    (("forward", 6), ("relay", 8), ("relay", 7), ("relay", 9), ("relay", 6), ("relay", 5), ),
)
LN_EPSILON = 1e-05
RMS_EPSILON = 1e-06
MASKED = -1e30
VMEM_LIMIT = 66_000_000
MESH = pl.DeviceIdType.MESH
BF16 = jnp.bfloat16
F32 = jnp.float32
NT = (((1,), (1,)), ((), ()))


def greet(g, s, groups, seqs, across):
    barrier = pltpu.get_barrier_semaphore()
    if across:
        for k in range(1, groups):
            pl.semaphore_signal(
                barrier, inc=1, device_id={"grp": lax.rem(g + k, groups), "seq": s}, device_id_type=MESH
            )
    for k in range(1, seqs):
        pl.semaphore_signal(
            barrier, inc=1, device_id={"grp": g, "seq": lax.rem(s + k, seqs)}, device_id_type=MESH
        )
    pl.semaphore_wait(barrier, seqs - 1 + (groups - 1 if across else 0))


def fill_table(routes, route_weights, table):
    experts = lax.broadcasted_iota(jnp.int32, table.shape, 0)
    given = route_weights[...]
    shares = given / jnp.sum(given, axis=0, keepdims=True)
    chosen = routes[...]
    table[...] = sum(
        jnp.where(experts == chosen[k : k + 1], shares[k : k + 1], 0.0) for k in range(chosen.shape[0])
    )


class Gather:
    def __init__(self, g, s, groups, seqs, shard, whole, rows, by_lanes, deep, own_sem, send_sem, recv_sem):
        self.g, self.s, self.groups = g, s, groups
        self.shard, self.whole, self.by_lanes = shard, whole, by_lanes
        self.own_sem, self.send_sem, self.recv_sem = own_sem, send_sem, recv_sem
        self.first, self.rows = rows
        self.routed = groups == 4
        self.deep = deep and self.routed and seqs % 4 == 0
        core, plane = lax.rem(s, 2), lax.rem(s // 2, 2)
        self.other = s + 1 - 2 * core
        self.paired = s + 2 - 4 * plane
        if self.deep:
            self.size = self.rows // 4
            self.start = self.first + (plane * 2 + core) * self.size
            self.paired_start = self.first + ((1 - plane) * 2 + core) * self.size
        else:
            self.size = self.rows // 2
            self.start = self.first + core * self.size
        self.cut = (self.size // 2 + 15) // 16 * 16
        self.copies = {}

    def part(self, group, first, count):
        if self.by_lanes:
            columns = self.shard.shape[1]
            start = pl.multiple_of(group * columns, 128)
            return self.whole.at[pl.ds(pl.multiple_of(first, 16), count), pl.ds(start, columns)]
        return self.whole.at[pl.ds(pl.multiple_of(group * self.shard.shape[0] + first, 16), count)]

    def source(self, first, count):
        return self.shard.at[pl.ds(pl.multiple_of(first, 16), count)]

    def send(self, event, source, target, grp, seq):
        copy = pltpu.make_async_remote_copy(
            src_ref=source,
            dst_ref=target,
            send_sem=self.send_sem.at[event],
            recv_sem=self.recv_sem.at[event],
            device_id={"grp": grp, "seq": seq},
            device_id_type=MESH,
        )
        copy.start()
        self.copies[event] = copy

    def pass_on(self, event, part, grp, seq):
        self.send(event, part, part, grp, seq)

    def got(self, *events):
        for event in events:
            self.copies[event].wait_recv()

    def xor(self, k):
        if k == 1:
            return self.g + 1 - 2 * lax.rem(self.g, 2)
        if k == 2:
            return lax.rem(self.g + 2, 4)
        return 3 - self.g

    def begin(self):
        if self.routed:
            for event, k in ((0, 1), (1, 2)):
                self.send(
                    event,
                    self.source(self.start, self.size),
                    self.part(self.g, self.start, self.size),
                    self.xor(k),
                    self.s,
                )
        else:
            for k in range(1, self.groups):
                self.send(
                    k - 1,
                    self.source(self.first, self.rows),
                    self.part(self.g, self.first, self.rows),
                    lax.rem(self.g + k, self.groups),
                    self.s,
                )
        self.own = pltpu.make_async_copy(
            self.source(self.first, self.rows), self.part(self.g, self.first, self.rows), self.own_sem
        )
        self.own.start()

    def forward(self):
        if not self.routed:
            return
        x, y = self.xor(1), self.xor(2)
        self.got(0, 1)
        self.pass_on(2, self.part(y, self.start, self.cut), x, self.s)
        self.pass_on(3, self.part(x, self.start + self.cut, self.size - self.cut), y, self.s)
        for event, k in ((0, x), (1, y)):
            near = self.part(k, self.start, self.size)
            if self.deep:
                self.pass_on(7 + event, near, self.g, self.paired)
            self.pass_on(4 + event, near, self.g, self.other)

    def share(self):
        if not self.routed:
            return
        self.got(2, 3)
        far = self.part(self.xor(3), self.start, self.size)
        if self.deep:
            self.pass_on(9, far, self.g, self.paired)
        self.pass_on(6, far, self.g, self.other)

    def relay(self):
        if not self.deep:
            return
        for event, k in ((0, 1), (1, 2), (2, 3)):
            self.got(7 + event)
            self.pass_on(10 + event, self.part(self.xor(k), self.paired_start, self.size), self.g, self.other)

    def end(self):
        self.own.wait()
        if self.deep:
            self.got(4, 5, 6, 10, 11, 12)
        elif self.routed:
            self.got(4, 5, 6)
        else:
            self.got(*range(self.groups - 1))

    def drain(self):
        for copy in self.copies.values():
            copy.wait_send()


class PairShare:
    def __init__(self, g, s, shard, whole, first, rows, send_sem, recv_sem):
        self.g, self.s, self.shard, self.whole = g, s, shard, whole
        self.send_sem, self.recv_sem = send_sem, recv_sem
        core, plane = lax.rem(s, 2), lax.rem(s // 2, 2)
        self.other, self.paired = s + 1 - 2 * core, s + 2 - 4 * plane
        self.size = rows // 4
        self.here = self.span(first + (plane * 2 + core) * self.size)
        self.there = self.span(first + ((1 - plane) * 2 + core) * self.size)
        self.copies = {}

    def span(self, first):
        return pl.ds(pl.multiple_of(first, 16), self.size)

    def send(self, event, source, rows, grp, seq):
        copy = pltpu.make_async_remote_copy(
            src_ref=source.at[rows],
            dst_ref=self.whole.at[rows],
            send_sem=self.send_sem.at[event],
            recv_sem=self.recv_sem.at[event],
            device_id={"grp": grp, "seq": seq},
            device_id_type=MESH,
        )
        copy.start()
        self.copies[event] = copy

    def begin(self):
        self.send(0, self.shard, self.here, lax.rem(self.g + 2, 4), self.s)

    def forward(self):
        self.copies[0].wait_recv()
        self.send(1, self.whole, self.here, self.g, self.paired)
        self.send(2, self.whole, self.here, self.g, self.other)

    def share(self):
        pass

    def relay(self):
        self.copies[1].wait_recv()
        self.send(3, self.whole, self.there, self.g, self.other)

    def end(self):
        self.copies[2].wait_recv()
        self.copies[3].wait_recv()

    def drain(self):
        for copy in self.copies.values():
            copy.wait_send()


def encoder_kernel(
    groups,
    seqs,
    audio_block,
    ids,
    gain,
    moe_gain,
    routes,
    route_weights,
    qkv_shard,
    out_shard,
    adapter_shard,
    thinker,
    expert_in,
    tables,
    qkv_w,
    out_w,
    adapter_w,
    normed,
    query,
    pairs,
    ids_ext,
    table,
    attended,
    even,
    odd,
    own_sem,
    weight_send,
    weight_recv,
    edge_send,
    edge_recv,
    tab_send,
    tab_recv,
):
    g, s = lax.axis_index("grp"), lax.axis_index("seq")
    audio = audio_block.at[0]
    frames, width = audio.shape
    heads_pairs = width // 128
    blocks = frames // EDGE
    fill_table(routes, route_weights, table)
    for b in range(blocks):
        ids_ext[b + 1] = jnp.broadcast_to(ids[0:1, b * EDGE : (b + 1) * EDGE], (8, EDGE))
    greet(g, s, groups, seqs, True)

    def gather(i, shard, whole, rows, by_lanes, deep):
        return Gather(
            g, s, groups, seqs, shard, whole, rows, by_lanes, deep, own_sem.at[i], weight_send.at[i], weight_recv.at[i]
        )

    def split(rows, at):
        return (0, at), (at, rows - at)

    qkv_rows, ad_rows = qkv_shard.shape[0], adapter_shard.shape[0]
    qkv_deep, qkv_plain = split(qkv_rows, (qkv_rows // 2 + 63) // 64 * 64)
    ad_deep, ad_plain = split(ad_rows, ad_rows // 2)
    qkv_a = gather(0, qkv_shard, qkv_w, qkv_deep, False, True)
    qkv_b = gather(1, qkv_shard, qkv_w, qkv_plain, False, False)
    out = gather(2, out_shard, out_w, (0, out_shard.shape[0]), False, False)
    ad_a = gather(3, adapter_shard, adapter_w, ad_deep, True, True)
    ad_b = gather(4, adapter_shard, adapter_w, ad_plain, True, False)
    qkv_a.begin()
    qkv_b.begin()

    table_copies = []
    for k in range(1, seqs):
        copy = pltpu.make_async_remote_copy(
            src_ref=table,
            dst_ref=tables.at[s],
            send_sem=tab_send.at[k - 1],
            recv_sem=tab_recv.at[k - 1],
            device_id={"grp": g, "seq": lax.rem(s + k, seqs)},
            device_id_type=MESH,
        )
        copy.start()
        table_copies.append(copy)
    tables[s] = table[...]

    def edge(event, source, target, step):
        return pltpu.make_async_remote_copy(
            src_ref=source,
            dst_ref=target,
            send_sem=edge_send.at[event],
            recv_sem=edge_recv.at[event],
            device_id={"grp": g, "seq": lax.rem(s + step + seqs, seqs)},
            device_id_type=MESH,
        )

    ids_right = edge(0, ids_ext.at[blocks], ids_ext.at[0], 1)
    ids_left = edge(1, ids_ext.at[1], ids_ext.at[blocks + 1], -1)
    pairs_right = edge(2, pairs.at[pl.ds(frames, EDGE)], pairs.at[pl.ds(0, EDGE)], 1)
    pairs_left = edge(3, pairs.at[pl.ds(EDGE, EDGE)], pairs.at[pl.ds(frames + EDGE, EDGE)], -1)
    has_left, has_right = s > 0, s < seqs - 1

    @pl.when(has_right)
    def _():
        ids_right.start()

    @pl.when(has_left)
    def _():
        ids_left.start()

    @pl.when(s == 0)
    def _():
        ids_ext[0] = jnp.full(ids_ext.shape[1:], -1, jnp.int32)
        pairs[0:EDGE] = jnp.zeros((EDGE, pairs.shape[1]), BF16)

    @pl.when(s == seqs - 1)
    def _():
        ids_ext[blocks + 1] = jnp.full(ids_ext.shape[1:], -1, jnp.int32)
        pairs[frames + EDGE :] = jnp.zeros((EDGE, pairs.shape[1]), BF16)

    def norm_rows(i, _):
        rows = pl.ds(pl.multiple_of(i * 64, 64), 64)
        signal = audio[rows].astype(F32)
        centred = signal - jnp.mean(signal, axis=-1, keepdims=True)
        variance = jnp.mean(centred * centred, axis=-1, keepdims=True)
        normed[rows] = (centred * lax.rsqrt(variance + LN_EPSILON) * gain[...]).astype(BF16)
        return 0

    lax.fori_loop(0, frames // 64, norm_rows, 0)

    qkv_a.forward()
    qkv_b.forward()
    out.begin()
    ad_a.begin()
    qkv_a.share()
    qkv_b.share()
    qkv_a.relay()
    qkv_a.end()
    qkv_b.end()

    tile = 256

    def project_pairs(i, _):
        source = pl.ds(pl.multiple_of(width + i * tile, tile), tile)
        columns = pl.ds(pl.multiple_of(i * tile, tile), tile)
        pairs[EDGE : EDGE + frames, columns] = lax.dot_general(
            normed[...], qkv_w[source], NT, preferred_element_type=F32
        ).astype(BF16)
        return 0

    lax.fori_loop(0, 2 * width // tile, project_pairs, 0)

    @pl.when(has_right)
    def _():
        pairs_right.start()

    @pl.when(has_left)
    def _():
        pairs_left.start()

    out.forward()
    ad_b.begin()

    def project_query(i, _):
        columns = pl.ds(pl.multiple_of(i * tile, tile), tile)
        query[:, columns] = lax.dot_general(
            normed[...], qkv_w[columns], NT, preferred_element_type=F32
        ).astype(BF16)
        return 0

    lax.fori_loop(0, width // tile, project_query, 0)
    out.share()
    ad_a.forward()

    @pl.when(has_left)
    def _():
        ids_right.wait_recv()
        pairs_right.wait_recv()

    @pl.when(has_right)
    def _():
        ids_left.wait_recv()
        pairs_left.wait_recv()

    low = lax.broadcasted_iota(jnp.int32, (EDGE, 128), 1) < HEAD
    span = 3 * EDGE
    for b in range(blocks):
        rows = slice(b * EDGE, (b + 1) * EDGE)
        keys = slice(b * EDGE, b * EDGE + span)
        key_ids = jnp.concatenate([ids_ext[b + j][0:1] for j in range(3)], axis=1)
        frame_ids = jnp.broadcast_to(ids_ext[b + 1][0:1], (EDGE, EDGE)).T[:, 0:1]
        same = frame_ids == key_ids
        allowed = jnp.concatenate([same, same], axis=0)

        def attend(p, _, rows=rows, keys=keys, allowed=allowed):
            columns = pl.ds(pl.multiple_of(p * 128, 128), 128)
            both = query[rows, columns]
            nothing = jnp.zeros_like(both)
            stacked = jnp.concatenate(
                [jnp.where(low, both, nothing), jnp.where(low, nothing, both)], axis=0
            )
            scores = lax.dot_general(
                stacked, pairs[keys, columns], NT, preferred_element_type=F32
            ) * HEAD ** (-0.5)
            scores = jnp.where(allowed, scores, MASKED)
            highest = jnp.max(scores, axis=-1, keepdims=True)
            exponent = jnp.exp(scores - highest)
            total = jnp.sum(exponent, axis=-1, keepdims=True)
            value_columns = pl.ds(pl.multiple_of(width + p * 128, 128), 128)
            mixed = jnp.dot(
                (exponent / total).astype(BF16), pairs[keys, value_columns], preferred_element_type=F32
            )
            attended[rows, columns] = jnp.where(low, mixed[:EDGE], mixed[EDGE:]).astype(BF16)
            return 0

        lax.fori_loop(0, heads_pairs, attend, 0)

    out.end()
    tokens = frames // 2
    at_row = lax.broadcasted_iota(jnp.int32, (tokens, frames), 0)
    at_frame = lax.broadcasted_iota(jnp.int32, (tokens, frames), 1)
    first = jnp.where(at_frame == 2 * at_row, 1.0, 0.0).astype(BF16)
    second = jnp.where(at_frame == 2 * at_row + 1, 1.0, 0.0).astype(BF16)

    def encode(i, _):
        columns = pl.ds(pl.multiple_of(i * tile, tile), tile)
        projected = lax.dot_general(attended[...], out_w[columns], NT, preferred_element_type=F32)
        encoded = (audio[:, columns].astype(F32) + projected).astype(BF16)
        even[:, columns] = jnp.dot(first, encoded, preferred_element_type=F32).astype(BF16)
        odd[:, columns] = jnp.dot(second, encoded, preferred_element_type=F32).astype(BF16)
        return 0

    lax.fori_loop(0, width // tile, encode, 0)
    ad_b.forward()
    ad_a.share()
    ad_a.relay()
    ad_b.share()
    ad_a.end()
    ad_b.end()

    def adapt(i, _):
        columns = pl.ds(pl.multiple_of(i * tile, tile), tile)
        thinker[:, columns] = (
            jnp.dot(even[...], adapter_w[0:width, columns], preferred_element_type=F32)
            + jnp.dot(odd[...], adapter_w[width:, columns], preferred_element_type=F32)
        ).astype(BF16)
        return 0

    lax.fori_loop(0, thinker.shape[1] // tile, adapt, 0)

    def rms_rows(i, _):
        rows = pl.ds(pl.multiple_of(i * 32, 32), 32)
        widened = thinker[rows].astype(F32)
        squares = jnp.mean(widened * widened, axis=-1, keepdims=True)
        expert_in[rows] = (widened * lax.rsqrt(squares + RMS_EPSILON) * moe_gain[...]).astype(BF16)
        return 0

    lax.fori_loop(0, tokens // 32, rms_rows, 0)

    for copy in table_copies:
        copy.wait()
    for weight in (qkv_a, qkv_b, out, ad_a, ad_b):
        weight.drain()

    @pl.when(has_right)
    def _():
        ids_right.wait_send()
        pairs_right.wait_send()

    @pl.when(has_left)
    def _():
        ids_left.wait_send()
        pairs_left.wait_send()


def fused_kernel(
    groups,
    seqs,
    audio_block,
    ids,
    gain,
    moe_gain,
    routes,
    route_weights,
    qkv_shard,
    out_shard,
    adapter_shard,
    gate_hbm,
    up_hbm,
    down_hbm,
    result,
    thinker,
    expert_in,
    tables,
    *scratch,
):
    def prepare(start_loads):
        return encode_tokens(
            start_loads,
            groups,
            seqs,
            audio_block,
            ids,
            gain,
            moe_gain,
            routes,
            route_weights,
            qkv_shard,
            out_shard,
            adapter_shard,
            thinker,
            expert_in,
            tables,
            *scratch[:32],
        )

    expert_kernel(
        seqs, expert_in, thinker, tables, gate_hbm, up_hbm, down_hbm, result, *scratch[32:], prepare=prepare
    )


def encode_tokens(
    start_loads,
    groups,
    seqs,
    audio_hbm,
    ids_hbm,
    gain_hbm,
    moe_gain_hbm,
    routes_hbm,
    route_weights_hbm,
    qkv_shard,
    out_shard,
    adapter_shard,
    thinker,
    expert_in,
    tables,
    audio,
    ids,
    gain,
    moe_gain,
    routes,
    route_weights,
    input_sem,
    qkv_w,
    out_w,
    adapter_w,
    normed,
    query,
    pairs,
    halo,
    ids_ext,
    table,
    attended,
    pooled,
    partner,
    produced,
    adapter_sem,
    own_sem,
    weight_send,
    weight_recv,
    pair_send,
    pair_recv,
    swap_send,
    swap_recv,
    edge_send,
    edge_recv,
    tab_send,
    tab_recv,
):
    g, s = lax.axis_index("grp"), lax.axis_index("seq")
    frames, width = audio.shape
    blocks = frames // EDGE
    inputs = [
        pltpu.make_async_copy(source, target, input_sem.at[i])
        for i, (source, target) in enumerate(
            (
                (audio_hbm.at[0], audio),
                (ids_hbm, ids),
                (gain_hbm, gain),
                (moe_gain_hbm, moe_gain),
                (routes_hbm, routes),
                (route_weights_hbm, route_weights),
            )
        )
    ]
    for load in inputs:
        load.start()
    greet(g, s, groups, seqs, True)

    def gather(i, shard, whole, first, rows, deep, by_lanes=False):
        return Gather(
            g, s, groups, seqs, shard, whole, (first, rows), by_lanes, deep,
            own_sem.at[i], weight_send.at[i], weight_recv.at[i],
        )

    items, count = [], 0
    for shard, whole, by_lanes, plan in (
        (qkv_shard, qkv_w, False, QKV_PLAN),
        (out_shard, out_w, False, OUT_PLAN),
    ):
        units, first = sum(sum(pair) for pair in plan), 0
        for pair in plan:
            item = []
            for deep, share in ((True, pair[0]), (False, pair[1])):
                if share:
                    rows = shard.shape[0] * share // units
                    item.append(gather(count, shard, whole, first, rows, deep, by_lanes))
                    first, count = first + rows, count + 1
            items.append(item)
    stripe = adapter_shard.shape[0] // ADAPTER_PARTS
    for k in range(ADAPTER_PARTS):
        items.append(
            [PairShare(g, s, adapter_shard, adapter_w.at[1], k * stripe, stripe, pair_send.at[k], pair_recv.at[k])]
        )
    own_adapter = pltpu.make_async_copy(adapter_shard, adapter_w.at[0], adapter_sem)

    def steps(point):
        for what, k in STEPS[point]:
            for one in items[k]:
                getattr(one, what)()

    steps(0)

    def edge(event, source, target, step):
        return pltpu.make_async_remote_copy(
            src_ref=source,
            dst_ref=target,
            send_sem=edge_send.at[event],
            recv_sem=edge_recv.at[event],
            device_id={"grp": g, "seq": lax.rem(s + step + seqs, seqs)},
            device_id_type=MESH,
        )

    ids_right = edge(0, ids_ext.at[blocks], ids_ext.at[0], 1)
    ids_left = edge(1, ids_ext.at[1], ids_ext.at[blocks + 1], -1)
    halo_right = edge(2, audio_hbm.at[0, pl.ds(frames - HALO, HALO)], halo.at[0], 1)
    halo_left = edge(3, audio_hbm.at[0, pl.ds(0, HALO)], halo.at[1], -1)
    has_left, has_right = s > 0, s < seqs - 1

    @pl.when(has_right)
    def _():
        halo_right.start()

    @pl.when(has_left)
    def _():
        halo_left.start()

    steps(1)
    for load in inputs:
        load.wait()
    for b in range(blocks):
        ids_ext[b + 1] = jnp.broadcast_to(ids[0:1, b * EDGE : (b + 1) * EDGE], (8, EDGE))

    @pl.when(has_right)
    def _():
        ids_right.start()

    @pl.when(has_left)
    def _():
        ids_left.start()

    fill_table(routes, route_weights, table)
    table_copies = []
    for k in range(1, seqs):
        copy = pltpu.make_async_remote_copy(
            src_ref=table,
            dst_ref=tables.at[s],
            send_sem=tab_send.at[k - 1],
            recv_sem=tab_recv.at[k - 1],
            device_id={"grp": g, "seq": lax.rem(s + k, seqs)},
            device_id_type=MESH,
        )
        copy.start()
        table_copies.append(copy)
    tables[s] = table[...]
    own_adapter.start()
    start_loads()

    @pl.when(s == 0)
    def _():
        ids_ext[0] = jnp.full(ids_ext.shape[1:], -1, jnp.int32)
        halo[0] = jnp.zeros(halo.shape[1:], BF16)

    @pl.when(s == seqs - 1)
    def _():
        ids_ext[blocks + 1] = jnp.full(ids_ext.shape[1:], -1, jnp.int32)
        halo[1] = jnp.zeros(halo.shape[1:], BF16)

    def layer_norm(signal):
        signal = signal.astype(F32)
        centred = signal - jnp.mean(signal, axis=-1, keepdims=True)
        variance = jnp.mean(centred * centred, axis=-1, keepdims=True)
        return (centred * lax.rsqrt(variance + LN_EPSILON) * gain[...]).astype(BF16)

    def norm_rows(i, _):
        rows = pl.multiple_of(i * 64, 64)
        normed[pl.ds(EDGE + rows, 64)] = layer_norm(audio[pl.ds(rows, 64)])
        return 0

    lax.fori_loop(0, frames // 64, norm_rows, 0)
    spare = jnp.zeros((EDGE - HALO, width), BF16)
    normed[0 : EDGE - HALO] = spare
    normed[frames + EDGE + HALO :] = spare
    steps(2)

    @pl.when(has_left)
    def _():
        ids_right.wait_recv()
        halo_right.wait_recv()

    @pl.when(has_right)
    def _():
        ids_left.wait_recv()
        halo_left.wait_recv()

    def norm_halo(i, _):
        rows = pl.multiple_of(i * 16, 16)
        normed[pl.ds(EDGE - HALO + rows, 16)] = layer_norm(halo[0, pl.ds(rows, 16)])
        normed[pl.ds(EDGE + frames + rows, 16)] = layer_norm(halo[1, pl.ds(rows, 16)])
        return 0

    lax.fori_loop(0, HALO // 16, norm_halo, 0)
    steps(3)
    tile = 256

    def project_pairs(i, _):
        source = pl.ds(pl.multiple_of(width + i * tile, tile), tile)
        columns = pl.ds(pl.multiple_of(i * tile, tile), tile)
        pairs[:, columns] = lax.dot_general(
            normed[...], qkv_w[source], NT, preferred_element_type=F32
        ).astype(BF16)
        return 0

    half = width // tile
    lax.fori_loop(0, half, project_pairs, 0)
    steps(4)
    lax.fori_loop(half, 2 * half, project_pairs, 0)
    steps(5)

    def project_query(i, _):
        columns = pl.ds(pl.multiple_of(i * tile, tile), tile)
        query[:, columns] = lax.dot_general(
            normed[EDGE : EDGE + frames], qkv_w[columns], NT, preferred_element_type=F32
        ).astype(BF16) * BF16(HEAD ** (-0.5))
        return 0

    lax.fori_loop(0, half, project_query, 0)
    steps(6)
    low = lax.broadcasted_iota(jnp.int32, (EDGE, 128), 1) < HEAD
    span = 3 * EDGE
    for b in range(blocks):
        rows = slice(b * EDGE, (b + 1) * EDGE)
        keys = slice(b * EDGE, b * EDGE + span)
        key_ids = jnp.concatenate([ids_ext[b + j][0:1] for j in range(3)], axis=1)
        frame_ids = jnp.broadcast_to(ids_ext[b + 1][0:1], (EDGE, EDGE)).T[:, 0:1]
        same = frame_ids == key_ids
        allowed = jnp.concatenate([same, same], axis=0)

        def attend(p, _, rows=rows, keys=keys, allowed=allowed):
            columns = pl.ds(pl.multiple_of(p * 128, 128), 128)
            both = query[rows, columns]
            nothing = jnp.zeros_like(both)
            stacked = jnp.concatenate(
                [jnp.where(low, both, nothing), jnp.where(low, nothing, both)], axis=0
            )
            scores = lax.dot_general(stacked, pairs[keys, columns], NT, preferred_element_type=F32)
            scores = jnp.where(allowed, scores, MASKED)
            highest = jnp.max(scores, axis=-1, keepdims=True)
            exponent = jnp.exp(scores - highest)
            total = jnp.sum(exponent, axis=-1, keepdims=True)
            value_columns = pl.ds(pl.multiple_of(width + p * 128, 128), 128)
            mixed = jnp.dot(
                exponent.astype(BF16), pairs[keys, value_columns], preferred_element_type=F32
            ) / total
            attended[rows, columns] = jnp.where(low, mixed[:EDGE], mixed[EDGE:]).astype(BF16)
            return 0

        heads_pairs = width // 128
        cuts = [heads_pairs * k // 4 for k in range(5)]
        for k in range(4):
            lax.fori_loop(cuts[k], cuts[k + 1], attend, 0)
            steps(7 + 4 * b + k)

    for one in items[len(QKV_PLAN)]:
        one.end()
    steps(15)
    tokens = frames // 2
    part = tokens // 2
    x, y = g + 1 - 2 * lax.rem(g, 2), lax.rem(g + 2, 4)
    columns_here = adapter_shard.shape[1]
    at_row = lax.broadcasted_iota(jnp.int32, (part, EDGE), 0)
    at_frame = lax.broadcasted_iota(jnp.int32, (part, EDGE), 1)
    first = jnp.where(at_frame == 2 * at_row, 1.0, 0.0).astype(BF16)
    second = jnp.where(at_frame == 2 * at_row + 1, 1.0, 0.0).astype(BF16)

    def encode_block(b):
        rows, out_rows = slice(b * EDGE, (b + 1) * EDGE), slice(b * part, (b + 1) * part)

        def encode(i, _):
            columns = pl.ds(pl.multiple_of(i * tile, tile), tile)
            projected = lax.dot_general(attended[rows], out_w[columns], NT, preferred_element_type=F32)
            encoded = (audio[rows, columns].astype(F32) + projected).astype(BF16)
            pooled[out_rows, columns] = jnp.dot(first, encoded, preferred_element_type=F32).astype(BF16)
            pooled[out_rows, pl.ds(pl.multiple_of(width + i * tile, tile), tile)] = jnp.dot(
                second, encoded, preferred_element_type=F32
            ).astype(BF16)
            return 0

        lax.fori_loop(0, half, encode, 0)

    def to_partner(event, source, target):
        return pltpu.make_async_remote_copy(
            src_ref=source,
            dst_ref=target,
            send_sem=swap_send.at[event],
            recv_sem=swap_recv.at[event],
            device_id={"grp": x, "seq": s},
            device_id_type=MESH,
        )

    piece = part // PIECES
    batches = [(0, part)] + [(part + k * piece, piece) for k in range(PIECES)]
    spreads = [
        to_partner(event, pooled.at[pl.ds(start, rows)], partner.at[pl.ds(start, rows)])
        for event, (start, rows) in enumerate(batches)
    ]

    def shard_columns(k):
        return pl.ds(pl.multiple_of((g, y)[k] * columns_here, 128), columns_here)

    def give_back(b, k):
        rows = pl.ds(*batches[b])
        return to_partner(len(batches) + 2 * b + k, produced.at[k, rows], thinker.at[rows, shard_columns(k)])

    backs = [[give_back(b, k) for k in range(2)] for b in range(len(batches))]

    def project(b):
        count = batches[b][1]
        rows = slice(batches[b][0], batches[b][0] + count)
        spreads[b].wait_recv()
        for k in range(2):

            def one(i, _, k=k):
                columns = pl.ds(pl.multiple_of(i * tile, tile), tile)
                batch = jnp.concatenate([pooled[rows], partner[rows]], axis=0)
                found = jnp.dot(batch, adapter_w[k, :, columns], preferred_element_type=F32).astype(BF16)
                start = pl.multiple_of((g, y)[k] * columns_here + i * tile, tile)
                thinker[rows, pl.ds(start, tile)] = found[:count]
                produced[k, rows, columns] = found[count:]
                return 0

            lax.fori_loop(0, columns_here // tile, one, 0)
            backs[b][k].start()

    def normalise(b):
        for back in backs[b]:
            back.wait_recv()

        def rms_rows(i, _):
            rows = pl.ds(pl.multiple_of(batches[b][0] + i * 32, 32), 32)
            widened = thinker[rows].astype(F32)
            squares = jnp.mean(widened * widened, axis=-1, keepdims=True)
            expert_in[rows] = (widened * lax.rsqrt(squares + RMS_EPSILON) * moe_gain[...]).astype(BF16)
            return 0

        lax.fori_loop(0, batches[b][1] // 32, rms_rows, 0)

    encode_block(0)
    spreads[0].start()
    steps(16)
    encode_block(1)
    spreads[1].start()
    steps(17)
    own_adapter.wait()
    steps(18)
    for one in sum(items[len(QKV_PLAN) + 1 :], []):
        one.end()
    for copy in table_copies:
        copy.wait()
    project(0)
    project(1)
    spreads[2].start()
    normalise(0)


    def finish():
        for weight in sum(items, []):
            weight.drain()
        for copy in spreads + sum(backs, []):
            copy.wait_send()

        @pl.when(has_right)
        def _():
            ids_right.wait_send()
            halo_right.wait_send()

        @pl.when(has_left)
        def _():
            ids_left.wait_send()
            halo_left.wait_send()

    return finish, project, normalise


def expert_kernel(
    seqs,
    expert_in,
    thinker,
    tables,
    gate_hbm,
    up_hbm,
    down_hbm,
    result,
    gate_w,
    up_w,
    down_w,
    tokens_all,
    hidden,
    mine,
    theirs,
    to_other,
    incoming,
    outgoing,
    load_sem,
    tok_send,
    tok_recv,
    half_send,
    half_recv,
    sum_send,
    sum_recv,
    share_of,
    done,
    done_sem,
    prepare=None,
):
    g, s = lax.axis_index("grp"), lax.axis_index("seq")
    planes = seqs // 2
    z, c = s // 2, lax.rem(s, 2)
    other = 1 - c
    rows, width = expert_in.shape
    ff = gate_w.shape[1]
    loads = [
        pltpu.make_async_copy(source, target, load_sem.at[i])
        for i, (source, target) in enumerate(((gate_hbm, gate_w), (up_hbm, up_w), (down_hbm, down_w)))
    ]

    def start_loads():
        for load in loads:
            load.start()

    if prepare is None:
        start_loads()
        greet(g, s, 1, seqs, False)
    else:
        settle, project, normalise = prepare(start_loads)

    part = rows // 2

    piece = part // PIECES

    def span(h):
        return pl.ds(pl.multiple_of(h * part, part), part)

    def strip(h, k):
        return pl.ds(pl.multiple_of(h * part + k * piece, piece), piece)

    def move(source, target, send, recv, plane, core):
        return pltpu.make_async_remote_copy(
            src_ref=source,
            dst_ref=target,
            send_sem=send,
            recv_sem=recv,
            device_id={"grp": g, "seq": plane * 2 + core},
            device_id_type=MESH,
        )

    def token_copy(side, origin, h, k, plane, own=False):
        slot = tokens_all.at[origin, c, strip(h, k)]
        source = expert_in.at[strip(h, k)] if own else slot
        event = h * PIECES + k
        return move(source, slot, tok_send.at[side, origin, event], tok_recv.at[0, origin, event], plane, c)

    def other_copy(origin, h, k, own=False):
        slot = tokens_all.at[origin, c, strip(h, k)]
        source = expert_in.at[strip(h, k)] if own else slot
        event = h * PIECES + k
        return move(source, slot, tok_send.at[2, origin, event], tok_recv.at[1, origin, event], z, other)

    def own_tokens(side, h, *pieces):
        for k in pieces or range(PIECES):
            token_copy(side, z, h, k, z + 1 - 2 * side, True).start()

    def own_other(h, *pieces):
        for k in pieces or range(PIECES):
            other_copy(z, h, k, True).start()

    def second_half(k):
        if prepare is not None:
            normalise(1 + k)
        for side in range(2):

            @pl.when((z == planes - 1, z == 0)[1 - side])
            def _(side=side):
                own_tokens(side, 1, k)

        own_other(1, k)
        here = slice(part + k * piece, part + (k + 1) * piece)
        tokens_all[z, c, here] = expert_in[here]

    def half_copy(origin, h):
        return move(
            to_other.at[origin, span(h)],
            theirs.at[origin, span(h)],
            half_send.at[origin, h],
            half_recv.at[origin, h],
            z,
            other,
        )

    def sum_copy(side, target, h, k, plane):
        return move(
            outgoing.at[side, target, strip(h, k)],
            incoming.at[side, target, strip(h, k)],
            sum_send.at[side, target, h * PIECES + k],
            sum_recv.at[side, target, h * PIECES + k],
            plane,
            c,
        )

    has_above, has_below = z < planes - 1, z > 0

    @pl.when(has_above)
    def _():
        own_tokens(0, 0)

    @pl.when(has_below)
    def _():
        own_tokens(1, 0)

    own_other(0)
    tokens_all[z, c, 0:part] = expert_in[0:part]
    second_half(0)
    for load in loads:
        load.wait()
    for k in range(seqs):
        share_of[k] = jnp.broadcast_to(tables[k, pl.ds(s, 1)], (128, rows)).T
    rise_tile = 384 if ff % 384 == 0 else 128
    fall_tile = 512 if width % 512 == 0 else 128

    def experts(origin, h):
        for k in range(PIECES):
            other_copy(origin, h, k).wait_recv()

        def rise(i, _):
            columns = pl.ds(pl.multiple_of(i * rise_tile, rise_tile), rise_tile)
            batch = tokens_all[origin, :, span(h)].reshape(2 * part, width)
            gate = jnp.dot(batch, gate_w[:, columns], preferred_element_type=F32)
            up = jnp.dot(batch, up_w[:, columns], preferred_element_type=F32)
            hidden[:, columns] = (gate / (1.0 + jnp.exp(-gate)) * up).astype(BF16)
            return 0

        lax.fori_loop(0, ff // rise_tile, rise, 0)
        share = jnp.concatenate([share_of[origin * 2 + k, span(h), 0:1] for k in range(2)], axis=0)

        def fall(i, _):
            columns = pl.ds(pl.multiple_of(i * fall_tile, fall_tile), fall_tile)
            produced = jnp.dot(hidden[...], down_w[:, columns], preferred_element_type=F32)
            weighted = (produced.astype(BF16).astype(F32) * share).astype(BF16)
            mine[origin, span(h), columns] = jnp.where(c == 0, weighted[:part], weighted[part:])
            to_other[origin, span(h), columns] = jnp.where(c == 0, weighted[part:], weighted[:part])
            return 0

        lax.fori_loop(0, width // fall_tile, fall, 0)
        half_copy(origin, h).start()

    def take(side, origin, h):
        for k in range(PIECES):
            token_copy(side, origin, h, k, z).wait_recv()

            @pl.when(jnp.where(side == 0, has_above, has_below))
            def _(k=k):
                token_copy(side, origin, h, k, z + 1 - 2 * side).start()

            other_copy(origin, h, k).start()

    def send_sum(side, origin, h, starts):
        half_copy(origin, h).wait_recv()
        for k in range(PIECES):
            here = strip(h, k)
            total = mine[origin, here].astype(F32) + theirs[origin, here].astype(F32)

            @pl.when(starts)
            def _(here=here, total=total):
                outgoing[side, origin, here] = total.astype(BF16)

            @pl.when(jnp.logical_not(starts))
            def _(here=here, total=total, k=k):
                sum_copy(side, origin, h, k, z).wait_recv()
                came = incoming[side, origin, here].astype(F32)
                outgoing[side, origin, here] = (total + came).astype(BF16)

            sum_copy(side, origin, h, k, z + 2 * side - 1).start()

    def arrival(side, t):
        reach = jnp.where(side == 0, z, planes - 1 - z)
        first = t <= reach
        distance = jnp.where(first, t, 2 * reach + 1 - t)
        valid = (t >= 1) & (t <= 2 * reach)
        return z + (2 * side - 1) * distance, jnp.where(first, 0, 1), valid, t == 2 * reach

    ends = (z == planes - 1, z == 0)
    experts(z, 0)
    if prepare is not None:
        project(2)

    def slot(t, _):
        for side in range(2):
            origin, h, valid, last = arrival(side, t)

            @pl.when(valid)
            def _(side=side, origin=origin, h=h):
                take(side, origin, h)

            @pl.when(last & (has_above, has_below)[side])
            def _(side=side):
                own_tokens(side, 1)

        for side in range(2):
            passed = jnp.where(side == 0, planes - 1 - z, z)
            origin, h, valid, _ = arrival(side, t - 2 * passed - 1)

            @pl.when(valid)
            def _(side=side, origin=origin, h=h):
                send_sum(side, origin, h, ends[side])

        @pl.when(t == 1)
        def _():
            for k in range(1, PIECES):
                second_half(k)

        def compute(j, _):
            side = jnp.where(z >= planes // 2, j, 1 - j)
            origin, h, valid, _ = arrival(side, t)
            own = j == 2
            now = t == jnp.where(ends[0] | ends[1], 1, 2 * planes - 3)

            @pl.when(jnp.where(own, now, valid))
            def _():
                experts(jnp.where(own, z, origin), jnp.where(own, 1, h))

            return 0

        lax.fori_loop(0, 3, compute, 0)
        return 0

    lax.fori_loop(1, 2 * planes, slot, 0)

    @pl.when(z == 0)
    def _():
        incoming[1, z] = jnp.zeros((rows, width), BF16)

    @pl.when(z == planes - 1)
    def _():
        incoming[0, z] = jnp.zeros((rows, width), BF16)

    outs = [
        pltpu.make_async_copy(
            done.at[pl.ds(h * part, part)], result.at[pl.ds(h * part, part)], done_sem.at[h]
        )
        for h in range(2)
    ]
    for h in range(2):
        half_copy(z, h).wait_recv()

        @pl.when(has_below)
        def _(h=h):
            for k in range(PIECES):
                sum_copy(1, z, h, k, z).wait_recv()

        @pl.when(has_above)
        def _(h=h):
            for k in range(PIECES):
                sum_copy(0, z, h, k, z).wait_recv()

        def finish(i, _, h=h):
            here = pl.ds(pl.multiple_of(h * part + i * 32, 32), 32)
            total = thinker[here].astype(F32) + mine[z, here].astype(F32) + theirs[z, here].astype(F32)
            total = total + incoming[0, z, here].astype(F32) + incoming[1, z, here].astype(F32)
            done[here] = total.astype(BF16)
            return 0

        lax.fori_loop(0, part // 32, finish, 0)
        outs[h].start()

    def drain(origin, _):
        for h in range(2):
            half_copy(origin, h).wait_send()
            for k in range(PIECES):
                other_copy(origin, h, k).wait_send()

                @pl.when((origin <= z) & has_above)
                def _(h=h, k=k):
                    token_copy(0, origin, h, k, z).wait_send()

                @pl.when((origin >= z) & has_below)
                def _(h=h, k=k):
                    token_copy(1, origin, h, k, z).wait_send()

                @pl.when(origin > z)
                def _(h=h, k=k):
                    sum_copy(1, origin, h, k, z).wait_send()

                @pl.when(origin < z)
                def _(h=h, k=k):
                    sum_copy(0, origin, h, k, z).wait_send()

        return 0

    lax.fori_loop(0, planes, drain, 0)
    if prepare is not None:
        settle()
    for out in outs:
        out.wait()


def body(
    groups,
    seqs,
    audio,
    block_ids,
    norm_gain,
    qkv_weight,
    out_weight,
    adapter_weight,
    moe_gain,
    gate_weight,
    up_weight,
    down_weight,
    routes,
    route_weights,
):
    frames, width = audio.shape[1:]
    tokens, features = routes.shape[1], moe_gain.shape[0]
    blocks = frames // EDGE
    vmem = pl.BlockSpec(memory_space=pltpu.VMEM)
    anywhere = pl.BlockSpec(memory_space=pl.ANY)
    dma = pltpu.SemaphoreType.DMA
    events = max(13, groups - 1)
    planes = seqs // 2
    ff = gate_weight.shape[2]
    block = (planes, tokens, features)
    expert_scratch = [
        pltpu.VMEM((features, ff), BF16),
        pltpu.VMEM((features, ff), BF16),
        pltpu.VMEM((ff, features), BF16),
        pltpu.VMEM((planes, 2, tokens, features), BF16),
        pltpu.VMEM((tokens, ff), BF16),
        pltpu.VMEM(block, BF16),
        pltpu.VMEM(block, BF16),
        pltpu.VMEM(block, BF16),
        pltpu.VMEM((2,) + block, BF16),
        pltpu.VMEM((2,) + block, BF16),
        dma((3,)),
        dma((3, planes, 2 * PIECES)),
        dma((2, planes, 2 * PIECES)),
        dma((planes, 2)),
        dma((planes, 2)),
        dma((2, planes, 2 * PIECES)),
        dma((2, planes, 2 * PIECES)),
        pltpu.VMEM((seqs, tokens, 128), F32),
        pltpu.VMEM((tokens, features), BF16),
        dma((2,)),
    ]
    expert_weights = (gate_weight[0], up_weight[0], down_weight[0])
    if groups == 4 and seqs == 8:
        gathers = sum(sum(1 for share in pair if share) for plan in (QKV_PLAN, OUT_PLAN) for pair in plan)
        result = pl.pallas_call(
            functools.partial(fused_kernel, groups, seqs),
            out_shape=jax.ShapeDtypeStruct((tokens, features), BF16),
            in_specs=[anywhere] * 12,
            out_specs=anywhere,
            scratch_shapes=[
                pltpu.VMEM((tokens, features), BF16),
                pltpu.VMEM((tokens, features), BF16),
                pltpu.VMEM((seqs, seqs, tokens), F32),
                pltpu.VMEM((frames, width), BF16),
                pltpu.VMEM(block_ids.shape, jnp.int32),
                pltpu.VMEM(norm_gain.shape, F32),
                pltpu.VMEM(moe_gain.shape, F32),
                pltpu.VMEM(routes.shape[:0:-1], jnp.int32),
                pltpu.VMEM(routes.shape[:0:-1], F32),
                dma((6,)),
                pltpu.VMEM((3 * width, width), BF16),
                pltpu.VMEM((width, width), BF16),
                pltpu.VMEM((2,) + adapter_weight.shape, BF16),
                pltpu.VMEM((frames + 2 * EDGE, width), BF16),
                pltpu.VMEM((frames, width), BF16),
                pltpu.VMEM((frames + 2 * EDGE, 2 * width), BF16),
                pltpu.VMEM((2, HALO, width), BF16),
                pltpu.VMEM((blocks + 2, 8, EDGE), jnp.int32),
                pltpu.VMEM((seqs, tokens), F32),
                pltpu.VMEM((frames, width), BF16),
                pltpu.VMEM((tokens, 2 * width), BF16),
                pltpu.VMEM((tokens, 2 * width), BF16),
                pltpu.VMEM((2, tokens, adapter_weight.shape[1]), BF16),
                dma,
                dma((gathers,)),
                dma((gathers, events)),
                dma((gathers, events)),
                dma((ADAPTER_PARTS, 4)),
                dma((ADAPTER_PARTS, 4)),
                dma((3 * (1 + PIECES),)),
                dma((3 * (1 + PIECES),)),
                dma((4,)),
                dma((4,)),
                dma((seqs - 1,)),
                dma((seqs - 1,)),
            ]
            + expert_scratch,
            compiler_params=pltpu.CompilerParams(
                collective_id=2, has_side_effects=True, vmem_limit_bytes=VMEM_LIMIT
            ),
            name="fused",
        )(
            audio,
            block_ids,
            norm_gain,
            moe_gain,
            routes[0].T,
            route_weights[0].T,
            qkv_weight.T,
            out_weight.T,
            adapter_weight,
            *expert_weights,
        )
        return result[None]
    thinker, expert_in, tables = pl.pallas_call(
        functools.partial(encoder_kernel, groups, seqs),
        out_shape=(
            jax.ShapeDtypeStruct((tokens, features), BF16),
            jax.ShapeDtypeStruct((tokens, features), BF16),
            jax.ShapeDtypeStruct((seqs, seqs, tokens), F32),
        ),
        in_specs=[vmem] * 6 + [anywhere] * 3,
        out_specs=(vmem,) * 3,
        scratch_shapes=[
            pltpu.VMEM((3 * width, width), BF16),
            pltpu.VMEM((width, width), BF16),
            pltpu.VMEM((2 * width, features), BF16),
            pltpu.VMEM((frames, width), BF16),
            pltpu.VMEM((frames, width), BF16),
            pltpu.VMEM((frames + 2 * EDGE, 2 * width), BF16),
            pltpu.VMEM((blocks + 2, 8, EDGE), jnp.int32),
            pltpu.VMEM((seqs, tokens), F32),
            pltpu.VMEM((frames, width), BF16),
            pltpu.VMEM((frames // 2, width), BF16),
            pltpu.VMEM((frames // 2, width), BF16),
            dma((5,)),
            dma((5, events)),
            dma((5, events)),
            dma((4,)),
            dma((4,)),
            dma((seqs - 1,)),
            dma((seqs - 1,)),
        ],
        compiler_params=pltpu.CompilerParams(
            collective_id=0, has_side_effects=True, vmem_limit_bytes=VMEM_LIMIT
        ),
        name="encoder",
    )(
        audio,
        block_ids,
        norm_gain,
        moe_gain,
        routes[0].T,
        route_weights[0].T,
        qkv_weight.T,
        out_weight.T,
        adapter_weight,
    )
    result = pl.pallas_call(
        functools.partial(expert_kernel, seqs),
        out_shape=jax.ShapeDtypeStruct((tokens, features), BF16),
        in_specs=[vmem] * 3 + [anywhere] * 3,
        out_specs=anywhere,
        scratch_shapes=expert_scratch,
        compiler_params=pltpu.CompilerParams(
            collective_id=1, has_side_effects=True, vmem_limit_bytes=VMEM_LIMIT
        ),
        name="experts",
    )(expert_in, thinker, tables, *expert_weights)
    return result[None]


def solution(mesh):
    placed = (
        P("grp", "seq", None),
        P("grp", "seq"),
        P(),
        P(None, "grp"),
        P(None, "grp"),
        P(None, "grp"),
        P(),
        P("seq", None, None),
        P("seq", None, None),
        P("seq", None, None),
        P("grp", "seq", None),
        P("grp", "seq", None),
    )
    return jax.shard_map(
        functools.partial(body, mesh.shape["grp"], mesh.shape["seq"]),
        mesh=mesh,
        in_specs=placed,
        out_specs=P("grp", "seq", None),
        check_vma=False,
    )
```

```python
import functools

import jax
import jax.numpy as jnp
from jax import lax
from jax.experimental import pallas as pl
from jax.experimental.pallas import tpu as pltpu
from jax.sharding import PartitionSpec as P

HEAD = 64
EDGE = 128
HALO = 112
PIECES = 2
QKV_PLAN = ((2, 0), (4, 0), (3, 0), (0, 6))
OUT_PLAN = ((2, 3),)
ADAPTER_PARTS = 5
STEPS = (
    (("begin", 0), ("begin", 1), ),
    (("forward", 0), ),
    (("begin", 2), ("begin", 3), ("share", 0), ("forward", 1), ),
    (("forward", 2), ("forward", 3), ("share", 1), ("share", 2), ("begin", 4), ("relay", 1), ("relay", 0), ("share", 3), ("relay", 2), ("relay", 3), ("begin", 5), ("end", 0), ("end", 1), ("end", 2), ("end", 3), ),
    (),
    (("forward", 4), ),
    (("begin", 9), ),
    (),
    (),
    (("share", 4), ("begin", 6), ("begin", 8), ("forward", 5), ),
    (),
    (),
    (("forward", 9), ("relay", 4), ),
    (),
    (("begin", 7), ),
    (("relay", 5), ("forward", 6), ),
    (("forward", 8), ),
    (),
    (("relay", 9), ("relay", 6), ("forward", 7), ("relay", 8), ("relay", 7), ),
)
LN_EPSILON = 1e-05
RMS_EPSILON = 1e-06
MASKED = -1e30
VMEM_LIMIT = 66_000_000
MESH = pl.DeviceIdType.MESH
BF16 = jnp.bfloat16
F32 = jnp.float32
NT = (((1,), (1,)), ((), ()))


def greet(g, s, groups, seqs, across):
    barrier = pltpu.get_barrier_semaphore()
    if across:
        for k in range(1, groups):
            pl.semaphore_signal(
                barrier, inc=1, device_id={"grp": lax.rem(g + k, groups), "seq": s}, device_id_type=MESH
            )
    for k in range(1, seqs):
        pl.semaphore_signal(
            barrier, inc=1, device_id={"grp": g, "seq": lax.rem(s + k, seqs)}, device_id_type=MESH
        )
    pl.semaphore_wait(barrier, seqs - 1 + (groups - 1 if across else 0))


def fill_table(routes, route_weights, table):
    experts = lax.broadcasted_iota(jnp.int32, table.shape, 0)
    given = route_weights[...]
    shares = given / jnp.sum(given, axis=0, keepdims=True)
    chosen = routes[...]
    table[...] = sum(
        jnp.where(experts == chosen[k : k + 1], shares[k : k + 1], 0.0) for k in range(chosen.shape[0])
    )


class Gather:
    def __init__(self, g, s, groups, seqs, shard, whole, rows, by_lanes, deep, own_sem, send_sem, recv_sem):
        self.g, self.s, self.groups = g, s, groups
        self.shard, self.whole, self.by_lanes = shard, whole, by_lanes
        self.own_sem, self.send_sem, self.recv_sem = own_sem, send_sem, recv_sem
        self.first, self.rows = rows
        self.routed = groups == 4
        self.deep = deep and self.routed and seqs % 4 == 0
        core, plane = lax.rem(s, 2), lax.rem(s // 2, 2)
        self.other = s + 1 - 2 * core
        self.paired = s + 2 - 4 * plane
        if self.deep:
            self.size = self.rows // 4
            self.start = self.first + (plane * 2 + core) * self.size
            self.paired_start = self.first + ((1 - plane) * 2 + core) * self.size
        else:
            self.size = self.rows // 2
            self.start = self.first + core * self.size
        self.cut = (self.size // 2 + 15) // 16 * 16
        self.copies = {}

    def part(self, group, first, count):
        if self.by_lanes:
            columns = self.shard.shape[1]
            start = pl.multiple_of(group * columns, 128)
            return self.whole.at[pl.ds(pl.multiple_of(first, 16), count), pl.ds(start, columns)]
        return self.whole.at[pl.ds(pl.multiple_of(group * self.shard.shape[0] + first, 16), count)]

    def source(self, first, count):
        return self.shard.at[pl.ds(pl.multiple_of(first, 16), count)]

    def send(self, event, source, target, grp, seq):
        copy = pltpu.make_async_remote_copy(
            src_ref=source,
            dst_ref=target,
            send_sem=self.send_sem.at[event],
            recv_sem=self.recv_sem.at[event],
            device_id={"grp": grp, "seq": seq},
            device_id_type=MESH,
        )
        copy.start()
        self.copies[event] = copy

    def pass_on(self, event, part, grp, seq):
        self.send(event, part, part, grp, seq)

    def got(self, *events):
        for event in events:
            self.copies[event].wait_recv()

    def xor(self, k):
        if k == 1:
            return self.g + 1 - 2 * lax.rem(self.g, 2)
        if k == 2:
            return lax.rem(self.g + 2, 4)
        return 3 - self.g

    def begin(self):
        if self.routed:
            for event, k in ((0, 1), (1, 2)):
                self.send(
                    event,
                    self.source(self.start, self.size),
                    self.part(self.g, self.start, self.size),
                    self.xor(k),
                    self.s,
                )
        else:
            for k in range(1, self.groups):
                self.send(
                    k - 1,
                    self.source(self.first, self.rows),
                    self.part(self.g, self.first, self.rows),
                    lax.rem(self.g + k, self.groups),
                    self.s,
                )
        self.own = pltpu.make_async_copy(
            self.source(self.first, self.rows), self.part(self.g, self.first, self.rows), self.own_sem
        )
        self.own.start()

    def forward(self):
        if not self.routed:
            return
        x, y = self.xor(1), self.xor(2)
        self.got(0, 1)
        self.pass_on(2, self.part(y, self.start, self.cut), x, self.s)
        self.pass_on(3, self.part(x, self.start + self.cut, self.size - self.cut), y, self.s)
        for event, k in ((0, x), (1, y)):
            near = self.part(k, self.start, self.size)
            if self.deep:
                self.pass_on(7 + event, near, self.g, self.paired)
            self.pass_on(4 + event, near, self.g, self.other)

    def share(self):
        if not self.routed:
            return
        self.got(2, 3)
        far = self.part(self.xor(3), self.start, self.size)
        if self.deep:
            self.pass_on(9, far, self.g, self.paired)
        self.pass_on(6, far, self.g, self.other)

    def relay(self):
        if not self.deep:
            return
        for event, k in ((0, 1), (1, 2), (2, 3)):
            self.got(7 + event)
            self.pass_on(10 + event, self.part(self.xor(k), self.paired_start, self.size), self.g, self.other)

    def end(self):
        self.own.wait()
        if self.deep:
            self.got(4, 5, 6, 10, 11, 12)
        elif self.routed:
            self.got(4, 5, 6)
        else:
            self.got(*range(self.groups - 1))

    def drain(self):
        for copy in self.copies.values():
            copy.wait_send()


class PairShare:
    def __init__(self, g, s, shard, whole, first, rows, send_sem, recv_sem):
        self.g, self.s, self.shard, self.whole = g, s, shard, whole
        self.send_sem, self.recv_sem = send_sem, recv_sem
        core, plane = lax.rem(s, 2), lax.rem(s // 2, 2)
        self.other, self.paired = s + 1 - 2 * core, s + 2 - 4 * plane
        self.size = rows // 4
        self.here = self.span(first + (plane * 2 + core) * self.size)
        self.there = self.span(first + ((1 - plane) * 2 + core) * self.size)
        self.copies = {}

    def span(self, first):
        return pl.ds(pl.multiple_of(first, 16), self.size)

    def send(self, event, source, rows, grp, seq):
        copy = pltpu.make_async_remote_copy(
            src_ref=source.at[rows],
            dst_ref=self.whole.at[rows],
            send_sem=self.send_sem.at[event],
            recv_sem=self.recv_sem.at[event],
            device_id={"grp": grp, "seq": seq},
            device_id_type=MESH,
        )
        copy.start()
        self.copies[event] = copy

    def begin(self):
        self.send(0, self.shard, self.here, lax.rem(self.g + 2, 4), self.s)

    def forward(self):
        self.copies[0].wait_recv()
        self.send(1, self.whole, self.here, self.g, self.paired)
        self.send(2, self.whole, self.here, self.g, self.other)

    def share(self):
        pass

    def relay(self):
        self.copies[1].wait_recv()
        self.send(3, self.whole, self.there, self.g, self.other)

    def end(self):
        self.copies[2].wait_recv()
        self.copies[3].wait_recv()

    def drain(self):
        for copy in self.copies.values():
            copy.wait_send()


def encoder_kernel(
    groups,
    seqs,
    audio_block,
    ids,
    gain,
    moe_gain,
    routes,
    route_weights,
    qkv_shard,
    out_shard,
    adapter_shard,
    thinker,
    expert_in,
    tables,
    qkv_w,
    out_w,
    adapter_w,
    normed,
    query,
    pairs,
    ids_ext,
    table,
    attended,
    even,
    odd,
    own_sem,
    weight_send,
    weight_recv,
    edge_send,
    edge_recv,
    tab_send,
    tab_recv,
):
    g, s = lax.axis_index("grp"), lax.axis_index("seq")
    audio = audio_block.at[0]
    frames, width = audio.shape
    heads_pairs = width // 128
    blocks = frames // EDGE
    fill_table(routes, route_weights, table)
    for b in range(blocks):
        ids_ext[b + 1] = jnp.broadcast_to(ids[0:1, b * EDGE : (b + 1) * EDGE], (8, EDGE))
    greet(g, s, groups, seqs, True)

    def gather(i, shard, whole, rows, by_lanes, deep):
        return Gather(
            g, s, groups, seqs, shard, whole, rows, by_lanes, deep, own_sem.at[i], weight_send.at[i], weight_recv.at[i]
        )

    def split(rows, at):
        return (0, at), (at, rows - at)

    qkv_rows, ad_rows = qkv_shard.shape[0], adapter_shard.shape[0]
    qkv_deep, qkv_plain = split(qkv_rows, (qkv_rows // 2 + 63) // 64 * 64)
    ad_deep, ad_plain = split(ad_rows, ad_rows // 2)
    qkv_a = gather(0, qkv_shard, qkv_w, qkv_deep, False, True)
    qkv_b = gather(1, qkv_shard, qkv_w, qkv_plain, False, False)
    out = gather(2, out_shard, out_w, (0, out_shard.shape[0]), False, False)
    ad_a = gather(3, adapter_shard, adapter_w, ad_deep, True, True)
    ad_b = gather(4, adapter_shard, adapter_w, ad_plain, True, False)
    qkv_a.begin()
    qkv_b.begin()

    table_copies = []
    for k in range(1, seqs):
        copy = pltpu.make_async_remote_copy(
            src_ref=table,
            dst_ref=tables.at[s],
            send_sem=tab_send.at[k - 1],
            recv_sem=tab_recv.at[k - 1],
            device_id={"grp": g, "seq": lax.rem(s + k, seqs)},
            device_id_type=MESH,
        )
        copy.start()
        table_copies.append(copy)
    tables[s] = table[...]

    def edge(event, source, target, step):
        return pltpu.make_async_remote_copy(
            src_ref=source,
            dst_ref=target,
            send_sem=edge_send.at[event],
            recv_sem=edge_recv.at[event],
            device_id={"grp": g, "seq": lax.rem(s + step + seqs, seqs)},
            device_id_type=MESH,
        )

    ids_right = edge(0, ids_ext.at[blocks], ids_ext.at[0], 1)
    ids_left = edge(1, ids_ext.at[1], ids_ext.at[blocks + 1], -1)
    pairs_right = edge(2, pairs.at[pl.ds(frames, EDGE)], pairs.at[pl.ds(0, EDGE)], 1)
    pairs_left = edge(3, pairs.at[pl.ds(EDGE, EDGE)], pairs.at[pl.ds(frames + EDGE, EDGE)], -1)
    has_left, has_right = s > 0, s < seqs - 1

    @pl.when(has_right)
    def _():
        ids_right.start()

    @pl.when(has_left)
    def _():
        ids_left.start()

    @pl.when(s == 0)
    def _():
        ids_ext[0] = jnp.full(ids_ext.shape[1:], -1, jnp.int32)
        pairs[0:EDGE] = jnp.zeros((EDGE, pairs.shape[1]), BF16)

    @pl.when(s == seqs - 1)
    def _():
        ids_ext[blocks + 1] = jnp.full(ids_ext.shape[1:], -1, jnp.int32)
        pairs[frames + EDGE :] = jnp.zeros((EDGE, pairs.shape[1]), BF16)

    def norm_rows(i, _):
        rows = pl.ds(pl.multiple_of(i * 64, 64), 64)
        signal = audio[rows].astype(F32)
        centred = signal - jnp.mean(signal, axis=-1, keepdims=True)
        variance = jnp.mean(centred * centred, axis=-1, keepdims=True)
        normed[rows] = (centred * lax.rsqrt(variance + LN_EPSILON) * gain[...]).astype(BF16)
        return 0

    lax.fori_loop(0, frames // 64, norm_rows, 0)

    qkv_a.forward()
    qkv_b.forward()
    out.begin()
    ad_a.begin()
    qkv_a.share()
    qkv_b.share()
    qkv_a.relay()
    qkv_a.end()
    qkv_b.end()

    tile = 256

    def project_pairs(i, _):
        source = pl.ds(pl.multiple_of(width + i * tile, tile), tile)
        columns = pl.ds(pl.multiple_of(i * tile, tile), tile)
        pairs[EDGE : EDGE + frames, columns] = lax.dot_general(
            normed[...], qkv_w[source], NT, preferred_element_type=F32
        ).astype(BF16)
        return 0

    lax.fori_loop(0, 2 * width // tile, project_pairs, 0)

    @pl.when(has_right)
    def _():
        pairs_right.start()

    @pl.when(has_left)
    def _():
        pairs_left.start()

    out.forward()
    ad_b.begin()

    def project_query(i, _):
        columns = pl.ds(pl.multiple_of(i * tile, tile), tile)
        query[:, columns] = lax.dot_general(
            normed[...], qkv_w[columns], NT, preferred_element_type=F32
        ).astype(BF16)
        return 0

    lax.fori_loop(0, width // tile, project_query, 0)
    out.share()
    ad_a.forward()

    @pl.when(has_left)
    def _():
        ids_right.wait_recv()
        pairs_right.wait_recv()

    @pl.when(has_right)
    def _():
        ids_left.wait_recv()
        pairs_left.wait_recv()

    low = lax.broadcasted_iota(jnp.int32, (EDGE, 128), 1) < HEAD
    span = 3 * EDGE
    for b in range(blocks):
        rows = slice(b * EDGE, (b + 1) * EDGE)
        keys = slice(b * EDGE, b * EDGE + span)
        key_ids = jnp.concatenate([ids_ext[b + j][0:1] for j in range(3)], axis=1)
        frame_ids = jnp.broadcast_to(ids_ext[b + 1][0:1], (EDGE, EDGE)).T[:, 0:1]
        same = frame_ids == key_ids
        allowed = jnp.concatenate([same, same], axis=0)

        def attend(p, _, rows=rows, keys=keys, allowed=allowed):
            columns = pl.ds(pl.multiple_of(p * 128, 128), 128)
            both = query[rows, columns]
            nothing = jnp.zeros_like(both)
            stacked = jnp.concatenate(
                [jnp.where(low, both, nothing), jnp.where(low, nothing, both)], axis=0
            )
            scores = lax.dot_general(
                stacked, pairs[keys, columns], NT, preferred_element_type=F32
            ) * HEAD ** (-0.5)
            scores = jnp.where(allowed, scores, MASKED)
            highest = jnp.max(scores, axis=-1, keepdims=True)
            exponent = jnp.exp(scores - highest)
            total = jnp.sum(exponent, axis=-1, keepdims=True)
            value_columns = pl.ds(pl.multiple_of(width + p * 128, 128), 128)
            mixed = jnp.dot(
                (exponent / total).astype(BF16), pairs[keys, value_columns], preferred_element_type=F32
            )
            attended[rows, columns] = jnp.where(low, mixed[:EDGE], mixed[EDGE:]).astype(BF16)
            return 0

        lax.fori_loop(0, heads_pairs, attend, 0)

    out.end()
    tokens = frames // 2
    at_row = lax.broadcasted_iota(jnp.int32, (tokens, frames), 0)
    at_frame = lax.broadcasted_iota(jnp.int32, (tokens, frames), 1)
    first = jnp.where(at_frame == 2 * at_row, 1.0, 0.0).astype(BF16)
    second = jnp.where(at_frame == 2 * at_row + 1, 1.0, 0.0).astype(BF16)

    def encode(i, _):
        columns = pl.ds(pl.multiple_of(i * tile, tile), tile)
        projected = lax.dot_general(attended[...], out_w[columns], NT, preferred_element_type=F32)
        encoded = (audio[:, columns].astype(F32) + projected).astype(BF16)
        even[:, columns] = jnp.dot(first, encoded, preferred_element_type=F32).astype(BF16)
        odd[:, columns] = jnp.dot(second, encoded, preferred_element_type=F32).astype(BF16)
        return 0

    lax.fori_loop(0, width // tile, encode, 0)
    ad_b.forward()
    ad_a.share()
    ad_a.relay()
    ad_b.share()
    ad_a.end()
    ad_b.end()

    def adapt(i, _):
        columns = pl.ds(pl.multiple_of(i * tile, tile), tile)
        thinker[:, columns] = (
            jnp.dot(even[...], adapter_w[0:width, columns], preferred_element_type=F32)
            + jnp.dot(odd[...], adapter_w[width:, columns], preferred_element_type=F32)
        ).astype(BF16)
        return 0

    lax.fori_loop(0, thinker.shape[1] // tile, adapt, 0)

    def rms_rows(i, _):
        rows = pl.ds(pl.multiple_of(i * 32, 32), 32)
        widened = thinker[rows].astype(F32)
        squares = jnp.mean(widened * widened, axis=-1, keepdims=True)
        expert_in[rows] = (widened * lax.rsqrt(squares + RMS_EPSILON) * moe_gain[...]).astype(BF16)
        return 0

    lax.fori_loop(0, tokens // 32, rms_rows, 0)

    for copy in table_copies:
        copy.wait()
    for weight in (qkv_a, qkv_b, out, ad_a, ad_b):
        weight.drain()

    @pl.when(has_right)
    def _():
        ids_right.wait_send()
        pairs_right.wait_send()

    @pl.when(has_left)
    def _():
        ids_left.wait_send()
        pairs_left.wait_send()


def fused_kernel(
    groups,
    seqs,
    audio_block,
    ids,
    gain,
    moe_gain,
    routes,
    route_weights,
    qkv_shard,
    out_shard,
    adapter_shard,
    gate_hbm,
    up_hbm,
    down_hbm,
    result,
    thinker,
    expert_in,
    tables,
    *scratch,
):
    def prepare(start_loads):
        return encode_tokens(
            start_loads,
            groups,
            seqs,
            audio_block,
            ids,
            gain,
            moe_gain,
            routes,
            route_weights,
            qkv_shard,
            out_shard,
            adapter_shard,
            thinker,
            expert_in,
            tables,
            *scratch[:32],
        )

    expert_kernel(
        seqs, expert_in, thinker, tables, gate_hbm, up_hbm, down_hbm, result, *scratch[32:], prepare=prepare
    )


def encode_tokens(
    start_loads,
    groups,
    seqs,
    audio_hbm,
    ids_hbm,
    gain_hbm,
    moe_gain_hbm,
    routes_hbm,
    route_weights_hbm,
    qkv_shard,
    out_shard,
    adapter_shard,
    thinker,
    expert_in,
    tables,
    audio,
    ids,
    gain,
    moe_gain,
    routes,
    route_weights,
    input_sem,
    qkv_w,
    out_w,
    adapter_w,
    normed,
    query,
    pairs,
    halo,
    ids_ext,
    table,
    attended,
    pooled,
    partner,
    produced,
    adapter_sem,
    own_sem,
    weight_send,
    weight_recv,
    pair_send,
    pair_recv,
    swap_send,
    swap_recv,
    edge_send,
    edge_recv,
    tab_send,
    tab_recv,
):
    g, s = lax.axis_index("grp"), lax.axis_index("seq")
    frames, width = audio.shape
    blocks = frames // EDGE
    inputs = [
        pltpu.make_async_copy(source, target, input_sem.at[i])
        for i, (source, target) in enumerate(
            (
                (audio_hbm.at[0], audio),
                (ids_hbm, ids),
                (gain_hbm, gain),
                (moe_gain_hbm, moe_gain),
                (routes_hbm, routes),
                (route_weights_hbm, route_weights),
            )
        )
    ]
    for load in inputs:
        load.start()
    greet(g, s, groups, seqs, True)

    def gather(i, shard, whole, first, rows, deep, by_lanes=False):
        return Gather(
            g, s, groups, seqs, shard, whole, (first, rows), by_lanes, deep,
            own_sem.at[i], weight_send.at[i], weight_recv.at[i],
        )

    items, count = [], 0
    for shard, whole, by_lanes, plan in (
        (qkv_shard, qkv_w, False, QKV_PLAN),
        (out_shard, out_w, False, OUT_PLAN),
    ):
        units, first = sum(sum(pair) for pair in plan), 0
        for pair in plan:
            item = []
            for deep, share in ((True, pair[0]), (False, pair[1])):
                if share:
                    rows = shard.shape[0] * share // units
                    item.append(gather(count, shard, whole, first, rows, deep, by_lanes))
                    first, count = first + rows, count + 1
            items.append(item)
    stripe = adapter_shard.shape[0] // ADAPTER_PARTS
    for k in range(ADAPTER_PARTS):
        items.append(
            [PairShare(g, s, adapter_shard, adapter_w.at[1], k * stripe, stripe, pair_send.at[k], pair_recv.at[k])]
        )
    own_adapter = pltpu.make_async_copy(adapter_shard, adapter_w.at[0], adapter_sem)

    def steps(point):
        for what, k in STEPS[point]:
            for one in items[k]:
                getattr(one, what)()

    steps(0)

    def edge(event, source, target, step):
        return pltpu.make_async_remote_copy(
            src_ref=source,
            dst_ref=target,
            send_sem=edge_send.at[event],
            recv_sem=edge_recv.at[event],
            device_id={"grp": g, "seq": lax.rem(s + step + seqs, seqs)},
            device_id_type=MESH,
        )

    ids_right = edge(0, ids_ext.at[blocks], ids_ext.at[0], 1)
    ids_left = edge(1, ids_ext.at[1], ids_ext.at[blocks + 1], -1)
    halo_right = edge(2, audio_hbm.at[0, pl.ds(frames - HALO, HALO)], halo.at[0], 1)
    halo_left = edge(3, audio_hbm.at[0, pl.ds(0, HALO)], halo.at[1], -1)
    has_left, has_right = s > 0, s < seqs - 1

    @pl.when(has_right)
    def _():
        halo_right.start()

    @pl.when(has_left)
    def _():
        halo_left.start()

    steps(1)
    for load in inputs:
        load.wait()
    for b in range(blocks):
        ids_ext[b + 1] = jnp.broadcast_to(ids[0:1, b * EDGE : (b + 1) * EDGE], (8, EDGE))

    @pl.when(has_right)
    def _():
        ids_right.start()

    @pl.when(has_left)
    def _():
        ids_left.start()

    fill_table(routes, route_weights, table)
    table_copies = []
    for k in range(1, seqs):
        copy = pltpu.make_async_remote_copy(
            src_ref=table,
            dst_ref=tables.at[s],
            send_sem=tab_send.at[k - 1],
            recv_sem=tab_recv.at[k - 1],
            device_id={"grp": g, "seq": lax.rem(s + k, seqs)},
            device_id_type=MESH,
        )
        copy.start()
        table_copies.append(copy)
    tables[s] = table[...]
    own_adapter.start()
    start_loads()

    @pl.when(s == 0)
    def _():
        ids_ext[0] = jnp.full(ids_ext.shape[1:], -1, jnp.int32)
        halo[0] = jnp.zeros(halo.shape[1:], BF16)

    @pl.when(s == seqs - 1)
    def _():
        ids_ext[blocks + 1] = jnp.full(ids_ext.shape[1:], -1, jnp.int32)
        halo[1] = jnp.zeros(halo.shape[1:], BF16)

    def layer_norm(signal):
        signal = signal.astype(F32)
        centred = signal - jnp.mean(signal, axis=-1, keepdims=True)
        variance = jnp.mean(centred * centred, axis=-1, keepdims=True)
        return (centred * lax.rsqrt(variance + LN_EPSILON) * gain[...]).astype(BF16)

    def norm_rows(i, _):
        rows = pl.multiple_of(i * 64, 64)
        normed[pl.ds(EDGE + rows, 64)] = layer_norm(audio[pl.ds(rows, 64)])
        return 0

    lax.fori_loop(0, frames // 64, norm_rows, 0)
    spare = jnp.zeros((EDGE - HALO, width), BF16)
    normed[0 : EDGE - HALO] = spare
    normed[frames + EDGE + HALO :] = spare
    steps(2)

    @pl.when(has_left)
    def _():
        ids_right.wait_recv()
        halo_right.wait_recv()

    @pl.when(has_right)
    def _():
        ids_left.wait_recv()
        halo_left.wait_recv()

    def norm_halo(i, _):
        rows = pl.multiple_of(i * 16, 16)
        normed[pl.ds(EDGE - HALO + rows, 16)] = layer_norm(halo[0, pl.ds(rows, 16)])
        normed[pl.ds(EDGE + frames + rows, 16)] = layer_norm(halo[1, pl.ds(rows, 16)])
        return 0

    lax.fori_loop(0, HALO // 16, norm_halo, 0)
    steps(3)
    tile = 256

    def project_pairs(i, _):
        source = pl.ds(pl.multiple_of(width + i * tile, tile), tile)
        columns = pl.ds(pl.multiple_of(i * tile, tile), tile)
        pairs[:, columns] = lax.dot_general(
            normed[...], qkv_w[source], NT, preferred_element_type=F32
        ).astype(BF16)
        return 0

    half = width // tile
    lax.fori_loop(0, half, project_pairs, 0)
    steps(4)
    lax.fori_loop(half, 2 * half, project_pairs, 0)
    steps(5)

    def project_query(i, _):
        columns = pl.ds(pl.multiple_of(i * tile, tile), tile)
        query[:, columns] = lax.dot_general(
            normed[EDGE : EDGE + frames], qkv_w[columns], NT, preferred_element_type=F32
        ).astype(BF16) * BF16(HEAD ** (-0.5))
        return 0

    lax.fori_loop(0, half, project_query, 0)
    steps(6)
    low = lax.broadcasted_iota(jnp.int32, (EDGE, 128), 1) < HEAD
    span = 3 * EDGE
    for b in range(blocks):
        rows = slice(b * EDGE, (b + 1) * EDGE)
        keys = slice(b * EDGE, b * EDGE + span)
        key_ids = jnp.concatenate([ids_ext[b + j][0:1] for j in range(3)], axis=1)
        frame_ids = jnp.broadcast_to(ids_ext[b + 1][0:1], (EDGE, EDGE)).T[:, 0:1]
        same = frame_ids == key_ids
        allowed = jnp.concatenate([same, same], axis=0)

        def attend(p, _, rows=rows, keys=keys, allowed=allowed):
            columns = pl.ds(pl.multiple_of(p * 128, 128), 128)
            both = query[rows, columns]
            nothing = jnp.zeros_like(both)
            stacked = jnp.concatenate(
                [jnp.where(low, both, nothing), jnp.where(low, nothing, both)], axis=0
            )
            scores = lax.dot_general(stacked, pairs[keys, columns], NT, preferred_element_type=F32)
            scores = jnp.where(allowed, scores, MASKED)
            highest = jnp.max(scores, axis=-1, keepdims=True)
            exponent = jnp.exp(scores - highest)
            total = jnp.sum(exponent, axis=-1, keepdims=True)
            value_columns = pl.ds(pl.multiple_of(width + p * 128, 128), 128)
            mixed = jnp.dot(
                exponent.astype(BF16), pairs[keys, value_columns], preferred_element_type=F32
            ) / total
            attended[rows, columns] = jnp.where(low, mixed[:EDGE], mixed[EDGE:]).astype(BF16)
            return 0

        heads_pairs = width // 128
        cuts = [heads_pairs * k // 4 for k in range(5)]
        for k in range(4):
            lax.fori_loop(cuts[k], cuts[k + 1], attend, 0)
            steps(7 + 4 * b + k)

    for one in items[len(QKV_PLAN)]:
        one.end()
    steps(15)
    tokens = frames // 2
    part = tokens // 2
    x, y = g + 1 - 2 * lax.rem(g, 2), lax.rem(g + 2, 4)
    columns_here = adapter_shard.shape[1]
    at_row = lax.broadcasted_iota(jnp.int32, (part, EDGE), 0)
    at_frame = lax.broadcasted_iota(jnp.int32, (part, EDGE), 1)
    first = jnp.where(at_frame == 2 * at_row, 1.0, 0.0).astype(BF16)
    second = jnp.where(at_frame == 2 * at_row + 1, 1.0, 0.0).astype(BF16)

    def encode_block(b, low_tile, high_tile):
        rows, out_rows = slice(b * EDGE, (b + 1) * EDGE), slice(b * part, (b + 1) * part)

        def encode(i, _):
            columns = pl.ds(pl.multiple_of(i * tile, tile), tile)
            projected = lax.dot_general(attended[rows], out_w[columns], NT, preferred_element_type=F32)
            encoded = (audio[rows, columns].astype(F32) + projected).astype(BF16)
            pooled[out_rows, columns] = jnp.dot(first, encoded, preferred_element_type=F32).astype(BF16)
            pooled[out_rows, pl.ds(pl.multiple_of(width + i * tile, tile), tile)] = jnp.dot(
                second, encoded, preferred_element_type=F32
            ).astype(BF16)
            return 0

        lax.fori_loop(low_tile, high_tile, encode, 0)

    def to_partner(event, source, target):
        return pltpu.make_async_remote_copy(
            src_ref=source,
            dst_ref=target,
            send_sem=swap_send.at[event],
            recv_sem=swap_recv.at[event],
            device_id={"grp": x, "seq": s},
            device_id_type=MESH,
        )

    piece = part // PIECES
    batches = [(0, part)] + [(part + k * piece, piece) for k in range(PIECES)]
    early = (half + 1) // 2 * tile
    spans = ((0, early), (width, early), (early, width - early), (width + early, width - early))
    spreads = []
    for b, (start, rows) in enumerate(batches):
        parts = spans if b == 0 else ((0, 2 * width),)
        copies = []
        for first_column, count in parts:
            where = (pl.ds(start, rows), pl.ds(first_column, count))
            copies.append(to_partner(len(copies) if b == 0 else len(spans) + b - 1, pooled.at[where], partner.at[where]))
        spreads.append(copies)
    events = len(spans) + len(batches) - 1

    def shard_columns(k):
        return pl.ds(pl.multiple_of((g, y)[k] * columns_here, 128), columns_here)

    def give_back(b, k):
        rows = pl.ds(*batches[b])
        return to_partner(events + 2 * b + k, produced.at[k, rows], thinker.at[rows, shard_columns(k)])

    backs = [[give_back(b, k) for k in range(2)] for b in range(len(batches))]

    def project(b):
        count = batches[b][1]
        rows = slice(batches[b][0], batches[b][0] + count)
        for copy in spreads[b]:
            copy.wait_recv()
        for k in range(2):
            if b == 0 and k == 1:
                for share in sum(items[len(QKV_PLAN) + 1 :], []):
                    share.end()

            def one(i, _, k=k):
                columns = pl.ds(pl.multiple_of(i * tile, tile), tile)
                batch = jnp.concatenate([pooled[rows], partner[rows]], axis=0)
                found = jnp.dot(batch, adapter_w[k, :, columns], preferred_element_type=F32).astype(BF16)
                start = pl.multiple_of((g, y)[k] * columns_here + i * tile, tile)
                thinker[rows, pl.ds(start, tile)] = found[:count]
                produced[k, rows, columns] = found[count:]
                return 0

            lax.fori_loop(0, columns_here // tile, one, 0)
            backs[b][k].start()

    def normalise(b):
        for back in backs[b]:
            back.wait_recv()

        def rms_rows(i, _):
            rows = pl.ds(pl.multiple_of(batches[b][0] + i * 32, 32), 32)
            widened = thinker[rows].astype(F32)
            squares = jnp.mean(widened * widened, axis=-1, keepdims=True)
            expert_in[rows] = (widened * lax.rsqrt(squares + RMS_EPSILON) * moe_gain[...]).astype(BF16)
            return 0

        lax.fori_loop(0, batches[b][1] // 32, rms_rows, 0)

    encode_block(0, 0, early // tile)
    for copy in spreads[0][:2]:
        copy.start()
    encode_block(0, early // tile, half)
    for copy in spreads[0][2:]:
        copy.start()
    steps(16)
    encode_block(1, 0, half)
    spreads[1][0].start()
    steps(17)
    own_adapter.wait()
    steps(18)
    for copy in table_copies:
        copy.wait()
    project(0)
    project(1)
    spreads[2][0].start()
    normalise(0)


    def finish():
        for weight in sum(items, []):
            weight.drain()
        for copy in sum(spreads, []) + sum(backs, []):
            copy.wait_send()

        @pl.when(has_right)
        def _():
            ids_right.wait_send()
            halo_right.wait_send()

        @pl.when(has_left)
        def _():
            ids_left.wait_send()
            halo_left.wait_send()

    return finish, project, normalise


def expert_kernel(
    seqs,
    expert_in,
    thinker,
    tables,
    gate_hbm,
    up_hbm,
    down_hbm,
    result,
    gate_w,
    up_w,
    down_w,
    tokens_all,
    hidden,
    mine,
    theirs,
    to_other,
    incoming,
    outgoing,
    load_sem,
    tok_send,
    tok_recv,
    half_send,
    half_recv,
    sum_send,
    sum_recv,
    share_of,
    done,
    done_sem,
    prepare=None,
):
    g, s = lax.axis_index("grp"), lax.axis_index("seq")
    planes = seqs // 2
    z, c = s // 2, lax.rem(s, 2)
    other = 1 - c
    rows, width = expert_in.shape
    ff = gate_w.shape[1]
    loads = [
        pltpu.make_async_copy(source, target, load_sem.at[i])
        for i, (source, target) in enumerate(((gate_hbm, gate_w), (up_hbm, up_w), (down_hbm, down_w)))
    ]

    def start_loads():
        for load in loads:
            load.start()

    if prepare is None:
        start_loads()
        greet(g, s, 1, seqs, False)
    else:
        settle, project, normalise = prepare(start_loads)

    part = rows // 2

    piece = part // PIECES

    def span(h):
        return pl.ds(pl.multiple_of(h * part, part), part)

    def strip(h, k):
        return pl.ds(pl.multiple_of(h * part + k * piece, piece), piece)

    def move(source, target, send, recv, plane, core):
        return pltpu.make_async_remote_copy(
            src_ref=source,
            dst_ref=target,
            send_sem=send,
            recv_sem=recv,
            device_id={"grp": g, "seq": plane * 2 + core},
            device_id_type=MESH,
        )

    def token_copy(side, origin, h, k, plane, own=False):
        slot = tokens_all.at[origin, c, strip(h, k)]
        source = expert_in.at[strip(h, k)] if own else slot
        event = h * PIECES + k
        return move(source, slot, tok_send.at[side, origin, event], tok_recv.at[0, origin, event], plane, c)

    def other_copy(origin, h, k, own=False):
        slot = tokens_all.at[origin, c, strip(h, k)]
        source = expert_in.at[strip(h, k)] if own else slot
        event = h * PIECES + k
        return move(source, slot, tok_send.at[2, origin, event], tok_recv.at[1, origin, event], z, other)

    def own_tokens(side, h, *pieces):
        for k in pieces or range(PIECES):
            token_copy(side, z, h, k, z + 1 - 2 * side, True).start()

    def own_other(h, *pieces):
        for k in pieces or range(PIECES):
            other_copy(z, h, k, True).start()

    def second_half(k):
        if prepare is not None:
            normalise(1 + k)
        for side in range(2):

            @pl.when((z == planes - 1, z == 0)[1 - side])
            def _(side=side):
                own_tokens(side, 1, k)

        own_other(1, k)
        here = slice(part + k * piece, part + (k + 1) * piece)
        tokens_all[z, c, here] = expert_in[here]

    def half_copy(origin, h):
        return move(
            to_other.at[origin, span(h)],
            theirs.at[origin, span(h)],
            half_send.at[origin, h],
            half_recv.at[origin, h],
            z,
            other,
        )

    def sum_copy(side, target, h, k, plane):
        return move(
            outgoing.at[side, target, strip(h, k)],
            incoming.at[side, target, strip(h, k)],
            sum_send.at[side, target, h * PIECES + k],
            sum_recv.at[side, target, h * PIECES + k],
            plane,
            c,
        )

    has_above, has_below = z < planes - 1, z > 0

    @pl.when(has_above)
    def _():
        own_tokens(0, 0)

    @pl.when(has_below)
    def _():
        own_tokens(1, 0)

    own_other(0)
    tokens_all[z, c, 0:part] = expert_in[0:part]
    second_half(0)
    for load in loads:
        load.wait()
    for k in range(seqs):
        share_of[k] = jnp.broadcast_to(tables[k, pl.ds(s, 1)], (128, rows)).T
    rise_tile = 384 if ff % 384 == 0 else 128
    fall_tile = 512 if width % 512 == 0 else 128

    def experts(origin, h):
        for k in range(PIECES):
            other_copy(origin, h, k).wait_recv()

        def rise(i, _):
            columns = pl.ds(pl.multiple_of(i * rise_tile, rise_tile), rise_tile)
            batch = tokens_all[origin, :, span(h)].reshape(2 * part, width)
            gate = jnp.dot(batch, gate_w[:, columns], preferred_element_type=F32)
            up = jnp.dot(batch, up_w[:, columns], preferred_element_type=F32)
            hidden[:, columns] = (gate / (1.0 + jnp.exp(-gate)) * up).astype(BF16)
            return 0

        lax.fori_loop(0, ff // rise_tile, rise, 0)
        share = jnp.concatenate([share_of[origin * 2 + k, span(h), 0:1] for k in range(2)], axis=0)

        def fall(i, _):
            columns = pl.ds(pl.multiple_of(i * fall_tile, fall_tile), fall_tile)
            produced = jnp.dot(hidden[...], down_w[:, columns], preferred_element_type=F32)
            weighted = (produced.astype(BF16).astype(F32) * share).astype(BF16)
            mine[origin, span(h), columns] = jnp.where(c == 0, weighted[:part], weighted[part:])
            to_other[origin, span(h), columns] = jnp.where(c == 0, weighted[part:], weighted[:part])
            return 0

        lax.fori_loop(0, width // fall_tile, fall, 0)
        half_copy(origin, h).start()

    def take(side, origin, h):
        for k in range(PIECES):
            token_copy(side, origin, h, k, z).wait_recv()

            @pl.when(jnp.where(side == 0, has_above, has_below))
            def _(k=k):
                token_copy(side, origin, h, k, z + 1 - 2 * side).start()

            other_copy(origin, h, k).start()

    def send_sum(side, origin, h, starts):
        half_copy(origin, h).wait_recv()
        for k in range(PIECES):
            here = strip(h, k)
            total = mine[origin, here].astype(F32) + theirs[origin, here].astype(F32)

            @pl.when(starts)
            def _(here=here, total=total):
                outgoing[side, origin, here] = total.astype(BF16)

            @pl.when(jnp.logical_not(starts))
            def _(here=here, total=total, k=k):
                sum_copy(side, origin, h, k, z).wait_recv()
                came = incoming[side, origin, here].astype(F32)
                outgoing[side, origin, here] = (total + came).astype(BF16)

            sum_copy(side, origin, h, k, z + 2 * side - 1).start()

    def arrival(side, t):
        reach = jnp.where(side == 0, z, planes - 1 - z)
        first = t <= reach
        distance = jnp.where(first, t, 2 * reach + 1 - t)
        valid = (t >= 1) & (t <= 2 * reach)
        return z + (2 * side - 1) * distance, jnp.where(first, 0, 1), valid, t == 2 * reach

    ends = (z == planes - 1, z == 0)
    experts(z, 0)
    if prepare is not None:
        project(2)

    def slot(t, _):
        for side in range(2):
            origin, h, valid, last = arrival(side, t)

            @pl.when(valid)
            def _(side=side, origin=origin, h=h):
                take(side, origin, h)

            @pl.when(last & (has_above, has_below)[side])
            def _(side=side):
                own_tokens(side, 1)

        for side in range(2):
            passed = jnp.where(side == 0, planes - 1 - z, z)
            origin, h, valid, _ = arrival(side, t - 2 * passed - 1)

            @pl.when(valid)
            def _(side=side, origin=origin, h=h):
                send_sum(side, origin, h, ends[side])

        @pl.when(t == 1)
        def _():
            for k in range(1, PIECES):
                second_half(k)

        def compute(j, _):
            side = jnp.where(z >= planes // 2, j, 1 - j)
            origin, h, valid, _ = arrival(side, t)
            own = j == 2
            now = t == jnp.where(ends[0] | ends[1], 1, 2 * planes - 3)

            @pl.when(jnp.where(own, now, valid))
            def _():
                experts(jnp.where(own, z, origin), jnp.where(own, 1, h))

            return 0

        lax.fori_loop(0, 3, compute, 0)
        return 0

    lax.fori_loop(1, 2 * planes, slot, 0)

    @pl.when(z == 0)
    def _():
        incoming[1, z] = jnp.zeros((rows, width), BF16)

    @pl.when(z == planes - 1)
    def _():
        incoming[0, z] = jnp.zeros((rows, width), BF16)

    outs = [
        pltpu.make_async_copy(
            done.at[pl.ds(h * part, part)], result.at[pl.ds(h * part, part)], done_sem.at[h]
        )
        for h in range(2)
    ]
    for h in range(2):
        half_copy(z, h).wait_recv()

        @pl.when(has_below)
        def _(h=h):
            for k in range(PIECES):
                sum_copy(1, z, h, k, z).wait_recv()

        @pl.when(has_above)
        def _(h=h):
            for k in range(PIECES):
                sum_copy(0, z, h, k, z).wait_recv()

        def finish(i, _, h=h):
            here = pl.ds(pl.multiple_of(h * part + i * 32, 32), 32)
            total = thinker[here].astype(F32) + mine[z, here].astype(F32) + theirs[z, here].astype(F32)
            total = total + incoming[0, z, here].astype(F32) + incoming[1, z, here].astype(F32)
            done[here] = total.astype(BF16)
            return 0

        lax.fori_loop(0, part // 32, finish, 0)
        outs[h].start()

    def drain(origin, _):
        for h in range(2):
            half_copy(origin, h).wait_send()
            for k in range(PIECES):
                other_copy(origin, h, k).wait_send()

                @pl.when((origin <= z) & has_above)
                def _(h=h, k=k):
                    token_copy(0, origin, h, k, z).wait_send()

                @pl.when((origin >= z) & has_below)
                def _(h=h, k=k):
                    token_copy(1, origin, h, k, z).wait_send()

                @pl.when(origin > z)
                def _(h=h, k=k):
                    sum_copy(1, origin, h, k, z).wait_send()

                @pl.when(origin < z)
                def _(h=h, k=k):
                    sum_copy(0, origin, h, k, z).wait_send()

        return 0

    lax.fori_loop(0, planes, drain, 0)
    if prepare is not None:
        settle()
    for out in outs:
        out.wait()


def body(
    groups,
    seqs,
    audio,
    block_ids,
    norm_gain,
    qkv_weight,
    out_weight,
    adapter_weight,
    moe_gain,
    gate_weight,
    up_weight,
    down_weight,
    routes,
    route_weights,
):
    frames, width = audio.shape[1:]
    tokens, features = routes.shape[1], moe_gain.shape[0]
    blocks = frames // EDGE
    vmem = pl.BlockSpec(memory_space=pltpu.VMEM)
    anywhere = pl.BlockSpec(memory_space=pl.ANY)
    dma = pltpu.SemaphoreType.DMA
    events = max(13, groups - 1)
    planes = seqs // 2
    ff = gate_weight.shape[2]
    block = (planes, tokens, features)
    expert_scratch = [
        pltpu.VMEM((features, ff), BF16),
        pltpu.VMEM((features, ff), BF16),
        pltpu.VMEM((ff, features), BF16),
        pltpu.VMEM((planes, 2, tokens, features), BF16),
        pltpu.VMEM((tokens, ff), BF16),
        pltpu.VMEM(block, BF16),
        pltpu.VMEM(block, BF16),
        pltpu.VMEM(block, BF16),
        pltpu.VMEM((2,) + block, BF16),
        pltpu.VMEM((2,) + block, BF16),
        dma((3,)),
        dma((3, planes, 2 * PIECES)),
        dma((2, planes, 2 * PIECES)),
        dma((planes, 2)),
        dma((planes, 2)),
        dma((2, planes, 2 * PIECES)),
        dma((2, planes, 2 * PIECES)),
        pltpu.VMEM((seqs, tokens, 128), F32),
        pltpu.VMEM((tokens, features), BF16),
        dma((2,)),
    ]
    expert_weights = (gate_weight[0], up_weight[0], down_weight[0])
    if groups == 4 and seqs == 8:
        gathers = sum(sum(1 for share in pair if share) for plan in (QKV_PLAN, OUT_PLAN) for pair in plan)
        result = pl.pallas_call(
            functools.partial(fused_kernel, groups, seqs),
            out_shape=jax.ShapeDtypeStruct((tokens, features), BF16),
            in_specs=[anywhere] * 12,
            out_specs=anywhere,
            scratch_shapes=[
                pltpu.VMEM((tokens, features), BF16),
                pltpu.VMEM((tokens, features), BF16),
                pltpu.VMEM((seqs, seqs, tokens), F32),
                pltpu.VMEM((frames, width), BF16),
                pltpu.VMEM(block_ids.shape, jnp.int32),
                pltpu.VMEM(norm_gain.shape, F32),
                pltpu.VMEM(moe_gain.shape, F32),
                pltpu.VMEM(routes.shape[:0:-1], jnp.int32),
                pltpu.VMEM(routes.shape[:0:-1], F32),
                dma((6,)),
                pltpu.VMEM((3 * width, width), BF16),
                pltpu.VMEM((width, width), BF16),
                pltpu.VMEM((2,) + adapter_weight.shape, BF16),
                pltpu.VMEM((frames + 2 * EDGE, width), BF16),
                pltpu.VMEM((frames, width), BF16),
                pltpu.VMEM((frames + 2 * EDGE, 2 * width), BF16),
                pltpu.VMEM((2, HALO, width), BF16),
                pltpu.VMEM((blocks + 2, 8, EDGE), jnp.int32),
                pltpu.VMEM((seqs, tokens), F32),
                pltpu.VMEM((frames, width), BF16),
                pltpu.VMEM((tokens, 2 * width), BF16),
                pltpu.VMEM((tokens, 2 * width), BF16),
                pltpu.VMEM((2, tokens, adapter_weight.shape[1]), BF16),
                dma,
                dma((gathers,)),
                dma((gathers, events)),
                dma((gathers, events)),
                dma((ADAPTER_PARTS, 4)),
                dma((ADAPTER_PARTS, 4)),
                dma((3 * (2 + PIECES),)),
                dma((3 * (2 + PIECES),)),
                dma((4,)),
                dma((4,)),
                dma((seqs - 1,)),
                dma((seqs - 1,)),
            ]
            + expert_scratch,
            compiler_params=pltpu.CompilerParams(
                collective_id=2, has_side_effects=True, vmem_limit_bytes=VMEM_LIMIT
            ),
            name="fused",
        )(
            audio,
            block_ids,
            norm_gain,
            moe_gain,
            routes[0].T,
            route_weights[0].T,
            qkv_weight.T,
            out_weight.T,
            adapter_weight,
            *expert_weights,
        )
        return result[None]
    thinker, expert_in, tables = pl.pallas_call(
        functools.partial(encoder_kernel, groups, seqs),
        out_shape=(
            jax.ShapeDtypeStruct((tokens, features), BF16),
            jax.ShapeDtypeStruct((tokens, features), BF16),
            jax.ShapeDtypeStruct((seqs, seqs, tokens), F32),
        ),
        in_specs=[vmem] * 6 + [anywhere] * 3,
        out_specs=(vmem,) * 3,
        scratch_shapes=[
            pltpu.VMEM((3 * width, width), BF16),
            pltpu.VMEM((width, width), BF16),
            pltpu.VMEM((2 * width, features), BF16),
            pltpu.VMEM((frames, width), BF16),
            pltpu.VMEM((frames, width), BF16),
            pltpu.VMEM((frames + 2 * EDGE, 2 * width), BF16),
            pltpu.VMEM((blocks + 2, 8, EDGE), jnp.int32),
            pltpu.VMEM((seqs, tokens), F32),
            pltpu.VMEM((frames, width), BF16),
            pltpu.VMEM((frames // 2, width), BF16),
            pltpu.VMEM((frames // 2, width), BF16),
            dma((5,)),
            dma((5, events)),
            dma((5, events)),
            dma((4,)),
            dma((4,)),
            dma((seqs - 1,)),
            dma((seqs - 1,)),
        ],
        compiler_params=pltpu.CompilerParams(
            collective_id=0, has_side_effects=True, vmem_limit_bytes=VMEM_LIMIT
        ),
        name="encoder",
    )(
        audio,
        block_ids,
        norm_gain,
        moe_gain,
        routes[0].T,
        route_weights[0].T,
        qkv_weight.T,
        out_weight.T,
        adapter_weight,
    )
    result = pl.pallas_call(
        functools.partial(expert_kernel, seqs),
        out_shape=jax.ShapeDtypeStruct((tokens, features), BF16),
        in_specs=[vmem] * 3 + [anywhere] * 3,
        out_specs=anywhere,
        scratch_shapes=expert_scratch,
        compiler_params=pltpu.CompilerParams(
            collective_id=1, has_side_effects=True, vmem_limit_bytes=VMEM_LIMIT
        ),
        name="experts",
    )(expert_in, thinker, tables, *expert_weights)
    return result[None]


def solution(mesh):
    placed = (
        P("grp", "seq", None),
        P("grp", "seq"),
        P(),
        P(None, "grp"),
        P(None, "grp"),
        P(None, "grp"),
        P(),
        P("seq", None, None),
        P("seq", None, None),
        P("seq", None, None),
        P("grp", "seq", None),
        P("grp", "seq", None),
    )
    return jax.shard_map(
        functools.partial(body, mesh.shape["grp"], mesh.shape["seq"]),
        mesh=mesh,
        in_specs=placed,
        out_specs=P("grp", "seq", None),
        check_vma=False,
    )
```

```python
import functools

import jax
import jax.numpy as jnp
from jax import lax
from jax.experimental import pallas as pl
from jax.experimental.pallas import tpu as pltpu
from jax.sharding import PartitionSpec as P

HEAD = 64
EDGE = 128
HALO = 112
PIECES = 2
QKV_PLAN = ((2, 0), (4, 0), (3, 0), (0, 6))
OUT_PLAN = ((2, 3),)
ADAPTER_PARTS = 5
STEPS = (
    (("begin", 0), ("begin", 1), ),
    (("forward", 0), ),
    (("begin", 2), ("begin", 3), ("share", 0), ("forward", 1), ),
    (("forward", 2), ("forward", 3), ("share", 1), ("share", 2), ("begin", 4), ("relay", 1), ("relay", 0), ("share", 3), ("relay", 2), ("relay", 3), ("begin", 5), ("end", 0), ("end", 1), ("end", 2), ("end", 3), ),
    (),
    (("forward", 4), ),
    (("begin", 9), ),
    (),
    (),
    (("share", 4), ("begin", 6), ("begin", 8), ("forward", 5), ),
    (),
    (),
    (("forward", 9), ("relay", 4), ),
    (),
    (("begin", 7), ),
    (("relay", 5), ("forward", 6), ),
    (("forward", 8), ),
    (),
    (("relay", 9), ("relay", 6), ("forward", 7), ("relay", 8), ("relay", 7), ),
)
LN_EPSILON = 1e-05
RMS_EPSILON = 1e-06
MASKED = -1e30
VMEM_LIMIT = 66_000_000
MESH = pl.DeviceIdType.MESH
BF16 = jnp.bfloat16
F32 = jnp.float32
NT = (((1,), (1,)), ((), ()))


def greet(g, s, groups, seqs, across):
    barrier = pltpu.get_barrier_semaphore()
    if across:
        for k in range(1, groups):
            pl.semaphore_signal(
                barrier, inc=1, device_id={"grp": lax.rem(g + k, groups), "seq": s}, device_id_type=MESH
            )
    for k in range(1, seqs):
        pl.semaphore_signal(
            barrier, inc=1, device_id={"grp": g, "seq": lax.rem(s + k, seqs)}, device_id_type=MESH
        )
    pl.semaphore_wait(barrier, seqs - 1 + (groups - 1 if across else 0))


def fill_table(routes, route_weights, table):
    experts = lax.broadcasted_iota(jnp.int32, table.shape, 0)
    given = route_weights[...]
    shares = given / jnp.sum(given, axis=0, keepdims=True)
    chosen = routes[...]
    table[...] = sum(
        jnp.where(experts == chosen[k : k + 1], shares[k : k + 1], 0.0) for k in range(chosen.shape[0])
    )


class Gather:
    def __init__(self, g, s, groups, seqs, shard, whole, rows, by_lanes, deep, own_sem, send_sem, recv_sem):
        self.g, self.s, self.groups = g, s, groups
        self.shard, self.whole, self.by_lanes = shard, whole, by_lanes
        self.own_sem, self.send_sem, self.recv_sem = own_sem, send_sem, recv_sem
        self.first, self.rows = rows
        self.routed = groups == 4
        self.deep = deep and self.routed and seqs % 4 == 0
        core, plane = lax.rem(s, 2), lax.rem(s // 2, 2)
        self.other = s + 1 - 2 * core
        self.paired = s + 2 - 4 * plane
        if self.deep:
            self.size = self.rows // 4
            self.start = self.first + (plane * 2 + core) * self.size
            self.paired_start = self.first + ((1 - plane) * 2 + core) * self.size
        else:
            self.size = self.rows // 2
            self.start = self.first + core * self.size
        self.cut = (self.size // 2 + 15) // 16 * 16
        self.copies = {}

    def part(self, group, first, count):
        if self.by_lanes:
            columns = self.shard.shape[1]
            start = pl.multiple_of(group * columns, 128)
            return self.whole.at[pl.ds(pl.multiple_of(first, 16), count), pl.ds(start, columns)]
        return self.whole.at[pl.ds(pl.multiple_of(group * self.shard.shape[0] + first, 16), count)]

    def source(self, first, count):
        return self.shard.at[pl.ds(pl.multiple_of(first, 16), count)]

    def send(self, event, source, target, grp, seq):
        copy = pltpu.make_async_remote_copy(
            src_ref=source,
            dst_ref=target,
            send_sem=self.send_sem.at[event],
            recv_sem=self.recv_sem.at[event],
            device_id={"grp": grp, "seq": seq},
            device_id_type=MESH,
        )
        copy.start()
        self.copies[event] = copy

    def pass_on(self, event, part, grp, seq):
        self.send(event, part, part, grp, seq)

    def got(self, *events):
        for event in events:
            self.copies[event].wait_recv()

    def xor(self, k):
        if k == 1:
            return self.g + 1 - 2 * lax.rem(self.g, 2)
        if k == 2:
            return lax.rem(self.g + 2, 4)
        return 3 - self.g

    def begin(self):
        if self.routed:
            for event, k in ((0, 1), (1, 2)):
                self.send(
                    event,
                    self.source(self.start, self.size),
                    self.part(self.g, self.start, self.size),
                    self.xor(k),
                    self.s,
                )
        else:
            for k in range(1, self.groups):
                self.send(
                    k - 1,
                    self.source(self.first, self.rows),
                    self.part(self.g, self.first, self.rows),
                    lax.rem(self.g + k, self.groups),
                    self.s,
                )
        self.own = pltpu.make_async_copy(
            self.source(self.first, self.rows), self.part(self.g, self.first, self.rows), self.own_sem
        )
        self.own.start()

    def forward(self):
        if not self.routed:
            return
        x, y = self.xor(1), self.xor(2)
        self.got(0, 1)
        self.pass_on(2, self.part(y, self.start, self.cut), x, self.s)
        self.pass_on(3, self.part(x, self.start + self.cut, self.size - self.cut), y, self.s)
        for event, k in ((0, x), (1, y)):
            near = self.part(k, self.start, self.size)
            if self.deep:
                self.pass_on(7 + event, near, self.g, self.paired)
            self.pass_on(4 + event, near, self.g, self.other)

    def share(self):
        if not self.routed:
            return
        self.got(2, 3)
        far = self.part(self.xor(3), self.start, self.size)
        if self.deep:
            self.pass_on(9, far, self.g, self.paired)
        self.pass_on(6, far, self.g, self.other)

    def relay(self):
        if not self.deep:
            return
        for event, k in ((0, 1), (1, 2), (2, 3)):
            self.got(7 + event)
            self.pass_on(10 + event, self.part(self.xor(k), self.paired_start, self.size), self.g, self.other)

    def end(self):
        self.own.wait()
        if self.deep:
            self.got(4, 5, 6, 10, 11, 12)
        elif self.routed:
            self.got(4, 5, 6)
        else:
            self.got(*range(self.groups - 1))

    def drain(self):
        for copy in self.copies.values():
            copy.wait_send()


class PairShare:
    def __init__(self, g, s, shard, whole, first, rows, send_sem, recv_sem):
        self.g, self.s, self.shard, self.whole = g, s, shard, whole
        self.send_sem, self.recv_sem = send_sem, recv_sem
        core, plane = lax.rem(s, 2), lax.rem(s // 2, 2)
        self.other, self.paired = s + 1 - 2 * core, s + 2 - 4 * plane
        self.size = rows // 4
        self.here = self.span(first + (plane * 2 + core) * self.size)
        self.there = self.span(first + ((1 - plane) * 2 + core) * self.size)
        self.copies = {}

    def span(self, first):
        return pl.ds(pl.multiple_of(first, 16), self.size)

    def send(self, event, source, rows, grp, seq):
        copy = pltpu.make_async_remote_copy(
            src_ref=source.at[rows],
            dst_ref=self.whole.at[rows],
            send_sem=self.send_sem.at[event],
            recv_sem=self.recv_sem.at[event],
            device_id={"grp": grp, "seq": seq},
            device_id_type=MESH,
        )
        copy.start()
        self.copies[event] = copy

    def begin(self):
        self.send(0, self.shard, self.here, lax.rem(self.g + 2, 4), self.s)

    def forward(self):
        self.copies[0].wait_recv()
        self.send(1, self.whole, self.here, self.g, self.paired)
        self.send(2, self.whole, self.here, self.g, self.other)

    def share(self):
        pass

    def relay(self):
        self.copies[1].wait_recv()
        self.send(3, self.whole, self.there, self.g, self.other)

    def end(self):
        self.copies[2].wait_recv()
        self.copies[3].wait_recv()

    def drain(self):
        for copy in self.copies.values():
            copy.wait_send()


def encoder_kernel(
    groups,
    seqs,
    audio_block,
    ids,
    gain,
    moe_gain,
    routes,
    route_weights,
    qkv_shard,
    out_shard,
    adapter_shard,
    thinker,
    expert_in,
    tables,
    qkv_w,
    out_w,
    adapter_w,
    normed,
    query,
    pairs,
    ids_ext,
    table,
    attended,
    even,
    odd,
    own_sem,
    weight_send,
    weight_recv,
    edge_send,
    edge_recv,
    tab_send,
    tab_recv,
):
    g, s = lax.axis_index("grp"), lax.axis_index("seq")
    audio = audio_block.at[0]
    frames, width = audio.shape
    heads_pairs = width // 128
    blocks = frames // EDGE
    fill_table(routes, route_weights, table)
    for b in range(blocks):
        ids_ext[b + 1] = jnp.broadcast_to(ids[0:1, b * EDGE : (b + 1) * EDGE], (8, EDGE))
    greet(g, s, groups, seqs, True)

    def gather(i, shard, whole, rows, by_lanes, deep):
        return Gather(
            g, s, groups, seqs, shard, whole, rows, by_lanes, deep, own_sem.at[i], weight_send.at[i], weight_recv.at[i]
        )

    def split(rows, at):
        return (0, at), (at, rows - at)

    qkv_rows, ad_rows = qkv_shard.shape[0], adapter_shard.shape[0]
    qkv_deep, qkv_plain = split(qkv_rows, (qkv_rows // 2 + 63) // 64 * 64)
    ad_deep, ad_plain = split(ad_rows, ad_rows // 2)
    qkv_a = gather(0, qkv_shard, qkv_w, qkv_deep, False, True)
    qkv_b = gather(1, qkv_shard, qkv_w, qkv_plain, False, False)
    out = gather(2, out_shard, out_w, (0, out_shard.shape[0]), False, False)
    ad_a = gather(3, adapter_shard, adapter_w, ad_deep, True, True)
    ad_b = gather(4, adapter_shard, adapter_w, ad_plain, True, False)
    qkv_a.begin()
    qkv_b.begin()

    table_copies = []
    for k in range(1, seqs):
        copy = pltpu.make_async_remote_copy(
            src_ref=table,
            dst_ref=tables.at[s],
            send_sem=tab_send.at[k - 1],
            recv_sem=tab_recv.at[k - 1],
            device_id={"grp": g, "seq": lax.rem(s + k, seqs)},
            device_id_type=MESH,
        )
        copy.start()
        table_copies.append(copy)
    tables[s] = table[...]

    def edge(event, source, target, step):
        return pltpu.make_async_remote_copy(
            src_ref=source,
            dst_ref=target,
            send_sem=edge_send.at[event],
            recv_sem=edge_recv.at[event],
            device_id={"grp": g, "seq": lax.rem(s + step + seqs, seqs)},
            device_id_type=MESH,
        )

    ids_right = edge(0, ids_ext.at[blocks], ids_ext.at[0], 1)
    ids_left = edge(1, ids_ext.at[1], ids_ext.at[blocks + 1], -1)
    pairs_right = edge(2, pairs.at[pl.ds(frames, EDGE)], pairs.at[pl.ds(0, EDGE)], 1)
    pairs_left = edge(3, pairs.at[pl.ds(EDGE, EDGE)], pairs.at[pl.ds(frames + EDGE, EDGE)], -1)
    has_left, has_right = s > 0, s < seqs - 1

    @pl.when(has_right)
    def _():
        ids_right.start()

    @pl.when(has_left)
    def _():
        ids_left.start()

    @pl.when(s == 0)
    def _():
        ids_ext[0] = jnp.full(ids_ext.shape[1:], -1, jnp.int32)
        pairs[0:EDGE] = jnp.zeros((EDGE, pairs.shape[1]), BF16)

    @pl.when(s == seqs - 1)
    def _():
        ids_ext[blocks + 1] = jnp.full(ids_ext.shape[1:], -1, jnp.int32)
        pairs[frames + EDGE :] = jnp.zeros((EDGE, pairs.shape[1]), BF16)

    def norm_rows(i, _):
        rows = pl.ds(pl.multiple_of(i * 64, 64), 64)
        signal = audio[rows].astype(F32)
        centred = signal - jnp.mean(signal, axis=-1, keepdims=True)
        variance = jnp.mean(centred * centred, axis=-1, keepdims=True)
        normed[rows] = (centred * lax.rsqrt(variance + LN_EPSILON) * gain[...]).astype(BF16)
        return 0

    lax.fori_loop(0, frames // 64, norm_rows, 0)

    qkv_a.forward()
    qkv_b.forward()
    out.begin()
    ad_a.begin()
    qkv_a.share()
    qkv_b.share()
    qkv_a.relay()
    qkv_a.end()
    qkv_b.end()

    tile = 256

    def project_pairs(i, _):
        source = pl.ds(pl.multiple_of(width + i * tile, tile), tile)
        columns = pl.ds(pl.multiple_of(i * tile, tile), tile)
        pairs[EDGE : EDGE + frames, columns] = lax.dot_general(
            normed[...], qkv_w[source], NT, preferred_element_type=F32
        ).astype(BF16)
        return 0

    lax.fori_loop(0, 2 * width // tile, project_pairs, 0)

    @pl.when(has_right)
    def _():
        pairs_right.start()

    @pl.when(has_left)
    def _():
        pairs_left.start()

    out.forward()
    ad_b.begin()

    def project_query(i, _):
        columns = pl.ds(pl.multiple_of(i * tile, tile), tile)
        query[:, columns] = lax.dot_general(
            normed[...], qkv_w[columns], NT, preferred_element_type=F32
        ).astype(BF16)
        return 0

    lax.fori_loop(0, width // tile, project_query, 0)
    out.share()
    ad_a.forward()

    @pl.when(has_left)
    def _():
        ids_right.wait_recv()
        pairs_right.wait_recv()

    @pl.when(has_right)
    def _():
        ids_left.wait_recv()
        pairs_left.wait_recv()

    low = lax.broadcasted_iota(jnp.int32, (EDGE, 128), 1) < HEAD
    span = 3 * EDGE
    for b in range(blocks):
        rows = slice(b * EDGE, (b + 1) * EDGE)
        keys = slice(b * EDGE, b * EDGE + span)
        key_ids = jnp.concatenate([ids_ext[b + j][0:1] for j in range(3)], axis=1)
        frame_ids = jnp.broadcast_to(ids_ext[b + 1][0:1], (EDGE, EDGE)).T[:, 0:1]
        same = frame_ids == key_ids
        allowed = jnp.concatenate([same, same], axis=0)

        def attend(p, _, rows=rows, keys=keys, allowed=allowed):
            columns = pl.ds(pl.multiple_of(p * 128, 128), 128)
            both = query[rows, columns]
            nothing = jnp.zeros_like(both)
            stacked = jnp.concatenate(
                [jnp.where(low, both, nothing), jnp.where(low, nothing, both)], axis=0
            )
            scores = lax.dot_general(
                stacked, pairs[keys, columns], NT, preferred_element_type=F32
            ) * HEAD ** (-0.5)
            scores = jnp.where(allowed, scores, MASKED)
            highest = jnp.max(scores, axis=-1, keepdims=True)
            exponent = jnp.exp(scores - highest)
            total = jnp.sum(exponent, axis=-1, keepdims=True)
            value_columns = pl.ds(pl.multiple_of(width + p * 128, 128), 128)
            mixed = jnp.dot(
                (exponent / total).astype(BF16), pairs[keys, value_columns], preferred_element_type=F32
            )
            attended[rows, columns] = jnp.where(low, mixed[:EDGE], mixed[EDGE:]).astype(BF16)
            return 0

        lax.fori_loop(0, heads_pairs, attend, 0)

    out.end()
    tokens = frames // 2
    at_row = lax.broadcasted_iota(jnp.int32, (tokens, frames), 0)
    at_frame = lax.broadcasted_iota(jnp.int32, (tokens, frames), 1)
    first = jnp.where(at_frame == 2 * at_row, 1.0, 0.0).astype(BF16)
    second = jnp.where(at_frame == 2 * at_row + 1, 1.0, 0.0).astype(BF16)

    def encode(i, _):
        columns = pl.ds(pl.multiple_of(i * tile, tile), tile)
        projected = lax.dot_general(attended[...], out_w[columns], NT, preferred_element_type=F32)
        encoded = (audio[:, columns].astype(F32) + projected).astype(BF16)
        even[:, columns] = jnp.dot(first, encoded, preferred_element_type=F32).astype(BF16)
        odd[:, columns] = jnp.dot(second, encoded, preferred_element_type=F32).astype(BF16)
        return 0

    lax.fori_loop(0, width // tile, encode, 0)
    ad_b.forward()
    ad_a.share()
    ad_a.relay()
    ad_b.share()
    ad_a.end()
    ad_b.end()

    def adapt(i, _):
        columns = pl.ds(pl.multiple_of(i * tile, tile), tile)
        thinker[:, columns] = (
            jnp.dot(even[...], adapter_w[0:width, columns], preferred_element_type=F32)
            + jnp.dot(odd[...], adapter_w[width:, columns], preferred_element_type=F32)
        ).astype(BF16)
        return 0

    lax.fori_loop(0, thinker.shape[1] // tile, adapt, 0)

    def rms_rows(i, _):
        rows = pl.ds(pl.multiple_of(i * 32, 32), 32)
        widened = thinker[rows].astype(F32)
        squares = jnp.mean(widened * widened, axis=-1, keepdims=True)
        expert_in[rows] = (widened * lax.rsqrt(squares + RMS_EPSILON) * moe_gain[...]).astype(BF16)
        return 0

    lax.fori_loop(0, tokens // 32, rms_rows, 0)

    for copy in table_copies:
        copy.wait()
    for weight in (qkv_a, qkv_b, out, ad_a, ad_b):
        weight.drain()

    @pl.when(has_right)
    def _():
        ids_right.wait_send()
        pairs_right.wait_send()

    @pl.when(has_left)
    def _():
        ids_left.wait_send()
        pairs_left.wait_send()


def fused_kernel(
    groups,
    seqs,
    audio_block,
    ids,
    gain,
    moe_gain,
    routes,
    route_weights,
    qkv_shard,
    out_shard,
    adapter_shard,
    gate_hbm,
    up_hbm,
    down_hbm,
    result,
    thinker,
    expert_in,
    tables,
    *scratch,
):
    def prepare(start_loads):
        return encode_tokens(
            start_loads,
            groups,
            seqs,
            audio_block,
            ids,
            gain,
            moe_gain,
            routes,
            route_weights,
            qkv_shard,
            out_shard,
            adapter_shard,
            thinker,
            expert_in,
            tables,
            *scratch[:32],
        )

    expert_kernel(
        seqs, expert_in, thinker, tables, gate_hbm, up_hbm, down_hbm, result, *scratch[32:], prepare=prepare
    )


def encode_tokens(
    start_loads,
    groups,
    seqs,
    audio_hbm,
    ids_hbm,
    gain_hbm,
    moe_gain_hbm,
    routes_hbm,
    route_weights_hbm,
    qkv_shard,
    out_shard,
    adapter_shard,
    thinker,
    expert_in,
    tables,
    audio,
    ids,
    gain,
    moe_gain,
    routes,
    route_weights,
    input_sem,
    qkv_w,
    out_w,
    adapter_w,
    normed,
    query,
    pairs,
    halo,
    ids_ext,
    table,
    attended,
    pooled,
    partner,
    produced,
    adapter_sem,
    own_sem,
    weight_send,
    weight_recv,
    pair_send,
    pair_recv,
    swap_send,
    swap_recv,
    edge_send,
    edge_recv,
    tab_send,
    tab_recv,
):
    g, s = lax.axis_index("grp"), lax.axis_index("seq")
    frames, width = audio.shape
    blocks = frames // EDGE
    inputs = [
        pltpu.make_async_copy(source, target, input_sem.at[i])
        for i, (source, target) in enumerate(
            (
                (audio_hbm.at[0], audio),
                (ids_hbm, ids),
                (gain_hbm, gain),
                (moe_gain_hbm, moe_gain),
                (routes_hbm, routes),
                (route_weights_hbm, route_weights),
            )
        )
    ]
    for load in inputs:
        load.start()
    greet(g, s, groups, seqs, True)

    def gather(i, shard, whole, first, rows, deep, by_lanes=False):
        return Gather(
            g, s, groups, seqs, shard, whole, (first, rows), by_lanes, deep,
            own_sem.at[i], weight_send.at[i], weight_recv.at[i],
        )

    items, count = [], 0
    for shard, whole, by_lanes, plan in (
        (qkv_shard, qkv_w, False, QKV_PLAN),
        (out_shard, out_w, False, OUT_PLAN),
    ):
        units, first = sum(sum(pair) for pair in plan), 0
        for pair in plan:
            item = []
            for deep, share in ((True, pair[0]), (False, pair[1])):
                if share:
                    rows = shard.shape[0] * share // units
                    item.append(gather(count, shard, whole, first, rows, deep, by_lanes))
                    first, count = first + rows, count + 1
            items.append(item)
    stripe = adapter_shard.shape[0] // ADAPTER_PARTS
    for k in range(ADAPTER_PARTS):
        items.append(
            [PairShare(g, s, adapter_shard, adapter_w.at[1], k * stripe, stripe, pair_send.at[k], pair_recv.at[k])]
        )
    own_adapter = pltpu.make_async_copy(adapter_shard, adapter_w.at[0], adapter_sem)

    def steps(point):
        for what, k in STEPS[point]:
            for one in items[k]:
                getattr(one, what)()

    steps(0)

    def edge(event, source, target, step):
        return pltpu.make_async_remote_copy(
            src_ref=source,
            dst_ref=target,
            send_sem=edge_send.at[event],
            recv_sem=edge_recv.at[event],
            device_id={"grp": g, "seq": lax.rem(s + step + seqs, seqs)},
            device_id_type=MESH,
        )

    ids_right = edge(0, ids_ext.at[blocks], ids_ext.at[0], 1)
    ids_left = edge(1, ids_ext.at[1], ids_ext.at[blocks + 1], -1)
    halo_right = edge(2, audio_hbm.at[0, pl.ds(frames - HALO, HALO)], halo.at[0], 1)
    halo_left = edge(3, audio_hbm.at[0, pl.ds(0, HALO)], halo.at[1], -1)
    has_left, has_right = s > 0, s < seqs - 1

    @pl.when(has_right)
    def _():
        halo_right.start()

    @pl.when(has_left)
    def _():
        halo_left.start()

    steps(1)
    for load in inputs:
        load.wait()
    for b in range(blocks):
        ids_ext[b + 1] = jnp.broadcast_to(ids[0:1, b * EDGE : (b + 1) * EDGE], (8, EDGE))

    @pl.when(has_right)
    def _():
        ids_right.start()

    @pl.when(has_left)
    def _():
        ids_left.start()

    fill_table(routes, route_weights, table)
    table_copies = []
    for k in range(1, seqs):
        copy = pltpu.make_async_remote_copy(
            src_ref=table,
            dst_ref=tables.at[s],
            send_sem=tab_send.at[k - 1],
            recv_sem=tab_recv.at[k - 1],
            device_id={"grp": g, "seq": lax.rem(s + k, seqs)},
            device_id_type=MESH,
        )
        copy.start()
        table_copies.append(copy)
    tables[s] = table[...]
    own_adapter.start()
    start_loads()

    @pl.when(s == 0)
    def _():
        ids_ext[0] = jnp.full(ids_ext.shape[1:], -1, jnp.int32)
        halo[0] = jnp.zeros(halo.shape[1:], BF16)

    @pl.when(s == seqs - 1)
    def _():
        ids_ext[blocks + 1] = jnp.full(ids_ext.shape[1:], -1, jnp.int32)
        halo[1] = jnp.zeros(halo.shape[1:], BF16)

    def layer_norm(signal):
        signal = signal.astype(F32)
        centred = signal - jnp.mean(signal, axis=-1, keepdims=True)
        variance = jnp.mean(centred * centred, axis=-1, keepdims=True)
        return (centred * lax.rsqrt(variance + LN_EPSILON) * gain[...]).astype(BF16)

    def norm_rows(i, _):
        rows = pl.multiple_of(i * 64, 64)
        normed[pl.ds(EDGE + rows, 64)] = layer_norm(audio[pl.ds(rows, 64)])
        return 0

    lax.fori_loop(0, frames // 64, norm_rows, 0)
    spare = jnp.zeros((EDGE - HALO, width), BF16)
    normed[0 : EDGE - HALO] = spare
    normed[frames + EDGE + HALO :] = spare
    steps(2)

    @pl.when(has_left)
    def _():
        ids_right.wait_recv()
        halo_right.wait_recv()

    @pl.when(has_right)
    def _():
        ids_left.wait_recv()
        halo_left.wait_recv()

    def norm_halo(i, _):
        rows = pl.multiple_of(i * 16, 16)
        normed[pl.ds(EDGE - HALO + rows, 16)] = layer_norm(halo[0, pl.ds(rows, 16)])
        normed[pl.ds(EDGE + frames + rows, 16)] = layer_norm(halo[1, pl.ds(rows, 16)])
        return 0

    lax.fori_loop(0, HALO // 16, norm_halo, 0)
    steps(3)
    tile = 256

    def project_pairs(i, _):
        source = pl.ds(pl.multiple_of(width + i * tile, tile), tile)
        columns = pl.ds(pl.multiple_of(i * tile, tile), tile)
        pairs[:, columns] = lax.dot_general(
            normed[...], qkv_w[source], NT, preferred_element_type=F32
        ).astype(BF16)
        return 0

    half = width // tile
    lax.fori_loop(0, half, project_pairs, 0)
    steps(4)
    lax.fori_loop(half, 2 * half, project_pairs, 0)
    steps(5)

    def project_query(i, _):
        columns = pl.ds(pl.multiple_of(i * tile, tile), tile)
        query[:, columns] = lax.dot_general(
            normed[EDGE : EDGE + frames], qkv_w[columns], NT, preferred_element_type=F32
        ).astype(BF16) * BF16(HEAD ** (-0.5))
        return 0

    lax.fori_loop(0, half, project_query, 0)
    steps(6)
    low = lax.broadcasted_iota(jnp.int32, (EDGE, 128), 1) < HEAD
    span = 3 * EDGE
    for b in range(blocks):
        rows = slice(b * EDGE, (b + 1) * EDGE)
        keys = slice(b * EDGE, b * EDGE + span)
        key_ids = jnp.concatenate([ids_ext[b + j][0:1] for j in range(3)], axis=1)
        frame_ids = jnp.broadcast_to(ids_ext[b + 1][0:1], (EDGE, EDGE)).T[:, 0:1]
        same = frame_ids == key_ids
        allowed = jnp.concatenate([same, same], axis=0)

        def attend(p, _, rows=rows, keys=keys, allowed=allowed):
            columns = pl.ds(pl.multiple_of(p * 128, 128), 128)
            both = query[rows, columns]
            nothing = jnp.zeros_like(both)
            stacked = jnp.concatenate(
                [jnp.where(low, both, nothing), jnp.where(low, nothing, both)], axis=0
            )
            scores = lax.dot_general(stacked, pairs[keys, columns], NT, preferred_element_type=F32)
            scores = jnp.where(allowed, scores, MASKED)
            highest = jnp.max(scores, axis=-1, keepdims=True)
            exponent = jnp.exp(scores - highest)
            total = jnp.sum(exponent, axis=-1, keepdims=True)
            value_columns = pl.ds(pl.multiple_of(width + p * 128, 128), 128)
            mixed = jnp.dot(
                exponent.astype(BF16), pairs[keys, value_columns], preferred_element_type=F32
            ) / total
            attended[rows, columns] = jnp.where(low, mixed[:EDGE], mixed[EDGE:]).astype(BF16)
            return 0

        heads_pairs = width // 128
        cuts = [heads_pairs * k // 4 for k in range(5)]
        for k in range(4):
            lax.fori_loop(cuts[k], cuts[k + 1], attend, 0, unroll=True)
            steps(7 + 4 * b + k)

    for one in items[len(QKV_PLAN)]:
        one.end()
    steps(15)
    tokens = frames // 2
    part = tokens // 2
    x, y = g + 1 - 2 * lax.rem(g, 2), lax.rem(g + 2, 4)
    columns_here = adapter_shard.shape[1]
    at_row = lax.broadcasted_iota(jnp.int32, (part, EDGE), 0)
    at_frame = lax.broadcasted_iota(jnp.int32, (part, EDGE), 1)
    first = jnp.where(at_frame == 2 * at_row, 1.0, 0.0).astype(BF16)
    second = jnp.where(at_frame == 2 * at_row + 1, 1.0, 0.0).astype(BF16)

    def encode_block(b, low_tile, high_tile):
        rows, out_rows = slice(b * EDGE, (b + 1) * EDGE), slice(b * part, (b + 1) * part)

        def encode(i, _):
            columns = pl.ds(pl.multiple_of(i * tile, tile), tile)
            projected = lax.dot_general(attended[rows], out_w[columns], NT, preferred_element_type=F32)
            encoded = (audio[rows, columns].astype(F32) + projected).astype(BF16)
            pooled[out_rows, columns] = jnp.dot(first, encoded, preferred_element_type=F32).astype(BF16)
            pooled[out_rows, pl.ds(pl.multiple_of(width + i * tile, tile), tile)] = jnp.dot(
                second, encoded, preferred_element_type=F32
            ).astype(BF16)
            return 0

        lax.fori_loop(low_tile, high_tile, encode, 0)

    def to_partner(event, source, target):
        return pltpu.make_async_remote_copy(
            src_ref=source,
            dst_ref=target,
            send_sem=swap_send.at[event],
            recv_sem=swap_recv.at[event],
            device_id={"grp": x, "seq": s},
            device_id_type=MESH,
        )

    piece = part // PIECES
    batches = [(0, part)] + [(part + k * piece, piece) for k in range(PIECES)]
    early = (half + 1) // 2 * tile
    spans = ((0, early), (width, early), (early, width - early), (width + early, width - early))
    spreads = []
    for b, (start, rows) in enumerate(batches):
        parts = spans if b == 0 else ((0, 2 * width),)
        copies = []
        for first_column, count in parts:
            where = (pl.ds(start, rows), pl.ds(first_column, count))
            copies.append(to_partner(len(copies) if b == 0 else len(spans) + b - 1, pooled.at[where], partner.at[where]))
        spreads.append(copies)
    events = len(spans) + len(batches) - 1

    def shard_columns(k):
        return pl.ds(pl.multiple_of((g, y)[k] * columns_here, 128), columns_here)

    def give_back(b, k):
        rows = pl.ds(*batches[b])
        return to_partner(events + 2 * b + k, produced.at[k, rows], thinker.at[rows, shard_columns(k)])

    backs = [[give_back(b, k) for k in range(2)] for b in range(len(batches))]

    def project(b):
        count = batches[b][1]
        rows = slice(batches[b][0], batches[b][0] + count)
        for copy in spreads[b]:
            copy.wait_recv()
        for k in range(2):
            if b == 0 and k == 1:
                for share in sum(items[len(QKV_PLAN) + 1 :], []):
                    share.end()

            def one(i, _, k=k):
                columns = pl.ds(pl.multiple_of(i * tile, tile), tile)
                batch = jnp.concatenate([pooled[rows], partner[rows]], axis=0)
                found = jnp.dot(batch, adapter_w[k, :, columns], preferred_element_type=F32).astype(BF16)
                start = pl.multiple_of((g, y)[k] * columns_here + i * tile, tile)
                thinker[rows, pl.ds(start, tile)] = found[:count]
                produced[k, rows, columns] = found[count:]
                return 0

            lax.fori_loop(0, columns_here // tile, one, 0)
            backs[b][k].start()

    def normalise(b):
        for back in backs[b]:
            back.wait_recv()

        def rms_rows(i, _):
            rows = pl.ds(pl.multiple_of(batches[b][0] + i * 32, 32), 32)
            widened = thinker[rows].astype(F32)
            squares = jnp.mean(widened * widened, axis=-1, keepdims=True)
            expert_in[rows] = (widened * lax.rsqrt(squares + RMS_EPSILON) * moe_gain[...]).astype(BF16)
            return 0

        lax.fori_loop(0, batches[b][1] // 32, rms_rows, 0)

    encode_block(0, 0, early // tile)
    for copy in spreads[0][:2]:
        copy.start()
    encode_block(0, early // tile, half)
    for copy in spreads[0][2:]:
        copy.start()
    steps(16)
    encode_block(1, 0, half)
    spreads[1][0].start()
    steps(17)
    own_adapter.wait()
    steps(18)
    for copy in table_copies:
        copy.wait()
    project(0)
    project(1)
    spreads[2][0].start()
    normalise(0)


    def finish():
        for weight in sum(items, []):
            weight.drain()
        for copy in sum(spreads, []) + sum(backs, []):
            copy.wait_send()

        @pl.when(has_right)
        def _():
            ids_right.wait_send()
            halo_right.wait_send()

        @pl.when(has_left)
        def _():
            ids_left.wait_send()
            halo_left.wait_send()

    return finish, project, normalise


def expert_kernel(
    seqs,
    expert_in,
    thinker,
    tables,
    gate_hbm,
    up_hbm,
    down_hbm,
    result,
    gate_w,
    up_w,
    down_w,
    tokens_all,
    hidden,
    mine,
    theirs,
    to_other,
    incoming,
    outgoing,
    load_sem,
    tok_send,
    tok_recv,
    half_send,
    half_recv,
    sum_send,
    sum_recv,
    share_of,
    done,
    done_sem,
    prepare=None,
):
    g, s = lax.axis_index("grp"), lax.axis_index("seq")
    planes = seqs // 2
    z, c = s // 2, lax.rem(s, 2)
    other = 1 - c
    rows, width = expert_in.shape
    ff = gate_w.shape[1]
    loads = [
        pltpu.make_async_copy(source, target, load_sem.at[i])
        for i, (source, target) in enumerate(((gate_hbm, gate_w), (up_hbm, up_w), (down_hbm, down_w)))
    ]

    def start_loads():
        for load in loads:
            load.start()

    if prepare is None:
        start_loads()
        greet(g, s, 1, seqs, False)
    else:
        settle, project, normalise = prepare(start_loads)

    part = rows // 2

    piece = part // PIECES

    def span(h):
        return pl.ds(pl.multiple_of(h * part, part), part)

    def strip(h, k):
        return pl.ds(pl.multiple_of(h * part + k * piece, piece), piece)

    def move(source, target, send, recv, plane, core):
        return pltpu.make_async_remote_copy(
            src_ref=source,
            dst_ref=target,
            send_sem=send,
            recv_sem=recv,
            device_id={"grp": g, "seq": plane * 2 + core},
            device_id_type=MESH,
        )

    def token_copy(side, origin, h, k, plane, own=False):
        slot = tokens_all.at[origin, c, strip(h, k)]
        source = expert_in.at[strip(h, k)] if own else slot
        event = h * PIECES + k
        return move(source, slot, tok_send.at[side, origin, event], tok_recv.at[0, origin, event], plane, c)

    def other_copy(origin, h, k, own=False):
        slot = tokens_all.at[origin, c, strip(h, k)]
        source = expert_in.at[strip(h, k)] if own else slot
        event = h * PIECES + k
        return move(source, slot, tok_send.at[2, origin, event], tok_recv.at[1, origin, event], z, other)

    def own_tokens(side, h, *pieces):
        for k in pieces or range(PIECES):
            token_copy(side, z, h, k, z + 1 - 2 * side, True).start()

    def own_other(h, *pieces):
        for k in pieces or range(PIECES):
            other_copy(z, h, k, True).start()

    def second_half(k):
        if prepare is not None:
            normalise(1 + k)
        for side in range(2):

            @pl.when((z == planes - 1, z == 0)[1 - side])
            def _(side=side):
                own_tokens(side, 1, k)

        own_other(1, k)
        here = slice(part + k * piece, part + (k + 1) * piece)
        tokens_all[z, c, here] = expert_in[here]

    def half_copy(origin, h):
        return move(
            to_other.at[origin, span(h)],
            theirs.at[origin, span(h)],
            half_send.at[origin, h],
            half_recv.at[origin, h],
            z,
            other,
        )

    def sum_copy(side, target, h, k, plane):
        return move(
            outgoing.at[side, target, strip(h, k)],
            incoming.at[side, target, strip(h, k)],
            sum_send.at[side, target, h * PIECES + k],
            sum_recv.at[side, target, h * PIECES + k],
            plane,
            c,
        )

    has_above, has_below = z < planes - 1, z > 0

    @pl.when(has_above)
    def _():
        own_tokens(0, 0)

    @pl.when(has_below)
    def _():
        own_tokens(1, 0)

    own_other(0)
    tokens_all[z, c, 0:part] = expert_in[0:part]
    second_half(0)
    for load in loads:
        load.wait()
    for k in range(seqs):
        share_of[k] = jnp.broadcast_to(tables[k, pl.ds(s, 1)], (128, rows)).T
    rise_tile = 384 if ff % 384 == 0 else 128
    fall_tile = 512 if width % 512 == 0 else 128

    def experts(origin, h):
        for k in range(PIECES):
            other_copy(origin, h, k).wait_recv()

        def rise(i, _):
            columns = pl.ds(pl.multiple_of(i * rise_tile, rise_tile), rise_tile)
            batch = tokens_all[origin, :, span(h)].reshape(2 * part, width)
            gate = jnp.dot(batch, gate_w[:, columns], preferred_element_type=F32)
            up = jnp.dot(batch, up_w[:, columns], preferred_element_type=F32)
            hidden[:, columns] = (gate / (1.0 + jnp.exp(-gate)) * up).astype(BF16)
            return 0

        lax.fori_loop(0, ff // rise_tile, rise, 0)
        share = jnp.concatenate([share_of[origin * 2 + k, span(h), 0:1] for k in range(2)], axis=0)

        def fall(i, _):
            columns = pl.ds(pl.multiple_of(i * fall_tile, fall_tile), fall_tile)
            produced = jnp.dot(hidden[...], down_w[:, columns], preferred_element_type=F32)
            weighted = (produced.astype(BF16).astype(F32) * share).astype(BF16)
            mine[origin, span(h), columns] = jnp.where(c == 0, weighted[:part], weighted[part:])
            to_other[origin, span(h), columns] = jnp.where(c == 0, weighted[part:], weighted[:part])
            return 0

        lax.fori_loop(0, width // fall_tile, fall, 0)
        half_copy(origin, h).start()

    def take(side, origin, h):
        for k in range(PIECES):
            token_copy(side, origin, h, k, z).wait_recv()

            @pl.when(jnp.where(side == 0, has_above, has_below))
            def _(k=k):
                token_copy(side, origin, h, k, z + 1 - 2 * side).start()

            other_copy(origin, h, k).start()

    def send_sum(side, origin, h, starts):
        half_copy(origin, h).wait_recv()
        for k in range(PIECES):
            here = strip(h, k)
            total = mine[origin, here].astype(F32) + theirs[origin, here].astype(F32)

            @pl.when(starts)
            def _(here=here, total=total):
                outgoing[side, origin, here] = total.astype(BF16)

            @pl.when(jnp.logical_not(starts))
            def _(here=here, total=total, k=k):
                sum_copy(side, origin, h, k, z).wait_recv()
                came = incoming[side, origin, here].astype(F32)
                outgoing[side, origin, here] = (total + came).astype(BF16)

            sum_copy(side, origin, h, k, z + 2 * side - 1).start()

    def arrival(side, t):
        reach = jnp.where(side == 0, z, planes - 1 - z)
        first = t <= reach
        distance = jnp.where(first, t, 2 * reach + 1 - t)
        valid = (t >= 1) & (t <= 2 * reach)
        return z + (2 * side - 1) * distance, jnp.where(first, 0, 1), valid, t == 2 * reach

    ends = (z == planes - 1, z == 0)
    experts(z, 0)
    if prepare is not None:
        project(2)

    def slot(t, _):
        for side in range(2):
            origin, h, valid, last = arrival(side, t)

            @pl.when(valid)
            def _(side=side, origin=origin, h=h):
                take(side, origin, h)

            @pl.when(last & (has_above, has_below)[side])
            def _(side=side):
                own_tokens(side, 1)

        for side in range(2):
            passed = jnp.where(side == 0, planes - 1 - z, z)
            origin, h, valid, _ = arrival(side, t - 2 * passed - 1)

            @pl.when(valid)
            def _(side=side, origin=origin, h=h):
                send_sum(side, origin, h, ends[side])

        @pl.when(t == 1)
        def _():
            for k in range(1, PIECES):
                second_half(k)

        def compute(j, _):
            side = jnp.where(z >= planes // 2, j, 1 - j)
            origin, h, valid, _ = arrival(side, t)
            own = j == 2
            now = t == jnp.where(ends[0] | ends[1], 1, 2 * planes - 3)

            @pl.when(jnp.where(own, now, valid))
            def _():
                experts(jnp.where(own, z, origin), jnp.where(own, 1, h))

            return 0

        lax.fori_loop(0, 3, compute, 0)
        return 0

    lax.fori_loop(1, 2 * planes, slot, 0)

    @pl.when(z == 0)
    def _():
        incoming[1, z] = jnp.zeros((rows, width), BF16)

    @pl.when(z == planes - 1)
    def _():
        incoming[0, z] = jnp.zeros((rows, width), BF16)

    outs = [
        pltpu.make_async_copy(
            done.at[pl.ds(h * part, part)], result.at[pl.ds(h * part, part)], done_sem.at[h]
        )
        for h in range(2)
    ]
    for h in range(2):
        half_copy(z, h).wait_recv()

        @pl.when(has_below)
        def _(h=h):
            for k in range(PIECES):
                sum_copy(1, z, h, k, z).wait_recv()

        @pl.when(has_above)
        def _(h=h):
            for k in range(PIECES):
                sum_copy(0, z, h, k, z).wait_recv()

        def finish(i, _, h=h):
            here = pl.ds(pl.multiple_of(h * part + i * 32, 32), 32)
            total = thinker[here].astype(F32) + mine[z, here].astype(F32) + theirs[z, here].astype(F32)
            total = total + incoming[0, z, here].astype(F32) + incoming[1, z, here].astype(F32)
            done[here] = total.astype(BF16)
            return 0

        lax.fori_loop(0, part // 32, finish, 0)
        outs[h].start()

    def drain(origin, _):
        for h in range(2):
            half_copy(origin, h).wait_send()
            for k in range(PIECES):
                other_copy(origin, h, k).wait_send()

                @pl.when((origin <= z) & has_above)
                def _(h=h, k=k):
                    token_copy(0, origin, h, k, z).wait_send()

                @pl.when((origin >= z) & has_below)
                def _(h=h, k=k):
                    token_copy(1, origin, h, k, z).wait_send()

                @pl.when(origin > z)
                def _(h=h, k=k):
                    sum_copy(1, origin, h, k, z).wait_send()

                @pl.when(origin < z)
                def _(h=h, k=k):
                    sum_copy(0, origin, h, k, z).wait_send()

        return 0

    lax.fori_loop(0, planes, drain, 0)
    if prepare is not None:
        settle()
    for out in outs:
        out.wait()


def body(
    groups,
    seqs,
    audio,
    block_ids,
    norm_gain,
    qkv_weight,
    out_weight,
    adapter_weight,
    moe_gain,
    gate_weight,
    up_weight,
    down_weight,
    routes,
    route_weights,
):
    frames, width = audio.shape[1:]
    tokens, features = routes.shape[1], moe_gain.shape[0]
    blocks = frames // EDGE
    vmem = pl.BlockSpec(memory_space=pltpu.VMEM)
    anywhere = pl.BlockSpec(memory_space=pl.ANY)
    dma = pltpu.SemaphoreType.DMA
    events = max(13, groups - 1)
    planes = seqs // 2
    ff = gate_weight.shape[2]
    block = (planes, tokens, features)
    expert_scratch = [
        pltpu.VMEM((features, ff), BF16),
        pltpu.VMEM((features, ff), BF16),
        pltpu.VMEM((ff, features), BF16),
        pltpu.VMEM((planes, 2, tokens, features), BF16),
        pltpu.VMEM((tokens, ff), BF16),
        pltpu.VMEM(block, BF16),
        pltpu.VMEM(block, BF16),
        pltpu.VMEM(block, BF16),
        pltpu.VMEM((2,) + block, BF16),
        pltpu.VMEM((2,) + block, BF16),
        dma((3,)),
        dma((3, planes, 2 * PIECES)),
        dma((2, planes, 2 * PIECES)),
        dma((planes, 2)),
        dma((planes, 2)),
        dma((2, planes, 2 * PIECES)),
        dma((2, planes, 2 * PIECES)),
        pltpu.VMEM((seqs, tokens, 128), F32),
        pltpu.VMEM((tokens, features), BF16),
        dma((2,)),
    ]
    expert_weights = (gate_weight[0], up_weight[0], down_weight[0])
    if groups == 4 and seqs == 8:
        gathers = sum(sum(1 for share in pair if share) for plan in (QKV_PLAN, OUT_PLAN) for pair in plan)
        result = pl.pallas_call(
            functools.partial(fused_kernel, groups, seqs),
            out_shape=jax.ShapeDtypeStruct((tokens, features), BF16),
            in_specs=[anywhere] * 12,
            out_specs=anywhere,
            scratch_shapes=[
                pltpu.VMEM((tokens, features), BF16),
                pltpu.VMEM((tokens, features), BF16),
                pltpu.VMEM((seqs, seqs, tokens), F32),
                pltpu.VMEM((frames, width), BF16),
                pltpu.VMEM(block_ids.shape, jnp.int32),
                pltpu.VMEM(norm_gain.shape, F32),
                pltpu.VMEM(moe_gain.shape, F32),
                pltpu.VMEM(routes.shape[:0:-1], jnp.int32),
                pltpu.VMEM(routes.shape[:0:-1], F32),
                dma((6,)),
                pltpu.VMEM((3 * width, width), BF16),
                pltpu.VMEM((width, width), BF16),
                pltpu.VMEM((2,) + adapter_weight.shape, BF16),
                pltpu.VMEM((frames + 2 * EDGE, width), BF16),
                pltpu.VMEM((frames, width), BF16),
                pltpu.VMEM((frames + 2 * EDGE, 2 * width), BF16),
                pltpu.VMEM((2, HALO, width), BF16),
                pltpu.VMEM((blocks + 2, 8, EDGE), jnp.int32),
                pltpu.VMEM((seqs, tokens), F32),
                pltpu.VMEM((frames, width), BF16),
                pltpu.VMEM((tokens, 2 * width), BF16),
                pltpu.VMEM((tokens, 2 * width), BF16),
                pltpu.VMEM((2, tokens, adapter_weight.shape[1]), BF16),
                dma,
                dma((gathers,)),
                dma((gathers, events)),
                dma((gathers, events)),
                dma((ADAPTER_PARTS, 4)),
                dma((ADAPTER_PARTS, 4)),
                dma((3 * (2 + PIECES),)),
                dma((3 * (2 + PIECES),)),
                dma((4,)),
                dma((4,)),
                dma((seqs - 1,)),
                dma((seqs - 1,)),
            ]
            + expert_scratch,
            compiler_params=pltpu.CompilerParams(
                collective_id=2, has_side_effects=True, vmem_limit_bytes=VMEM_LIMIT
            ),
            name="fused",
        )(
            audio,
            block_ids,
            norm_gain,
            moe_gain,
            routes[0].T,
            route_weights[0].T,
            qkv_weight.T,
            out_weight.T,
            adapter_weight,
            *expert_weights,
        )
        return result[None]
    thinker, expert_in, tables = pl.pallas_call(
        functools.partial(encoder_kernel, groups, seqs),
        out_shape=(
            jax.ShapeDtypeStruct((tokens, features), BF16),
            jax.ShapeDtypeStruct((tokens, features), BF16),
            jax.ShapeDtypeStruct((seqs, seqs, tokens), F32),
        ),
        in_specs=[vmem] * 6 + [anywhere] * 3,
        out_specs=(vmem,) * 3,
        scratch_shapes=[
            pltpu.VMEM((3 * width, width), BF16),
            pltpu.VMEM((width, width), BF16),
            pltpu.VMEM((2 * width, features), BF16),
            pltpu.VMEM((frames, width), BF16),
            pltpu.VMEM((frames, width), BF16),
            pltpu.VMEM((frames + 2 * EDGE, 2 * width), BF16),
            pltpu.VMEM((blocks + 2, 8, EDGE), jnp.int32),
            pltpu.VMEM((seqs, tokens), F32),
            pltpu.VMEM((frames, width), BF16),
            pltpu.VMEM((frames // 2, width), BF16),
            pltpu.VMEM((frames // 2, width), BF16),
            dma((5,)),
            dma((5, events)),
            dma((5, events)),
            dma((4,)),
            dma((4,)),
            dma((seqs - 1,)),
            dma((seqs - 1,)),
        ],
        compiler_params=pltpu.CompilerParams(
            collective_id=0, has_side_effects=True, vmem_limit_bytes=VMEM_LIMIT
        ),
        name="encoder",
    )(
        audio,
        block_ids,
        norm_gain,
        moe_gain,
        routes[0].T,
        route_weights[0].T,
        qkv_weight.T,
        out_weight.T,
        adapter_weight,
    )
    result = pl.pallas_call(
        functools.partial(expert_kernel, seqs),
        out_shape=jax.ShapeDtypeStruct((tokens, features), BF16),
        in_specs=[vmem] * 3 + [anywhere] * 3,
        out_specs=anywhere,
        scratch_shapes=expert_scratch,
        compiler_params=pltpu.CompilerParams(
            collective_id=1, has_side_effects=True, vmem_limit_bytes=VMEM_LIMIT
        ),
        name="experts",
    )(expert_in, thinker, tables, *expert_weights)
    return result[None]


def solution(mesh):
    placed = (
        P("grp", "seq", None),
        P("grp", "seq"),
        P(),
        P(None, "grp"),
        P(None, "grp"),
        P(None, "grp"),
        P(),
        P("seq", None, None),
        P("seq", None, None),
        P("seq", None, None),
        P("grp", "seq", None),
        P("grp", "seq", None),
    )
    return jax.shard_map(
        functools.partial(body, mesh.shape["grp"], mesh.shape["seq"]),
        mesh=mesh,
        in_specs=placed,
        out_specs=P("grp", "seq", None),
        check_vma=False,
    )
```
